256 devices in a mesh: freq: 16 (over x, z_hi), tile: 16 (over z_lo, y, core).
Axes of the slice: x: 4, y: 4, z: 8 (z_hi: 4, z_lo: 2; z = z_hi * 2 + z_lo), core: 2. Of those that a mesh axis runs over, the one named last changes fastest.
Arguments:
- sky_cube: float32 [256, 256, 128], P(('freq', 'tile')), may hold values from -6 to 6
- kernel_one: bfloat16 [8, 1, 3, 3, 3], replicated, may hold values from -1.25 to 1.25
- bias_one: float32 [8], replicated, may hold values from -2 to 2
- kernel_two: bfloat16 [8, 8, 3, 3, 3], replicated, may hold values from -0.4375 to 0.4375
- bias_two: float32 [8], replicated, may hold values from -2 to 2
- kernel_three: bfloat16 [16, 8, 3, 3, 3], replicated, may hold values from -0.4375 to 0.4375
- bias_three: float32 [16], replicated, may hold values from -2 to 2
Outputs:
- features: bfloat16 [16, 128, 128, 64], P(None, 'freq', 'tile')
The draws below stay inside these ranges and needn't reach their ends.
All inputs are finite; a program needn't handle non-finite values.
Results may differ from the reference program's by a relative error of at most 0.0066.
Values may be sent and summed in bfloat16 or wider, within the bound.
A program may use at most 64 MiB of HBM per device.

```python
import jax
import jax.numpy as jnp
from jax import lax

NX = 128
C1 = 8
C2 = 8
C3 = 16
GROUP = 16
CH = 256
NY = 256
N_FREQ = 16


def level_of(own_key, dims, pieces, low, largest):
    level = 1.0
    for axis_at, shards_of in pieces:
        heights = jax.random.uniform(jax.random.fold_in(jax.random.fold_in(own_key, 6), axis_at), (shards_of,), jnp.float32, low / len(pieces), largest / len(pieces))
        level = level * jnp.repeat(jnp.exp(heights), dims[axis_at] // shards_of).reshape((-1,) + (1,) * (len(dims) - 1 - axis_at))
    return level


def centred(stream_key, extent, deviation, reach, shards=(), held_as=jnp.bfloat16):
    entries = deviation * jax.random.normal(stream_key, extent, jnp.float32)
    if shards:
        entries = entries * level_of(stream_key, extent, shards, -0.22, 0.18)
    return jnp.clip(entries, -reach, reach).astype(held_as)


def setup_inputs(seed: int = 0) -> dict:
    arg_keys = jax.random.split(jax.random.key(seed), 8)
    return {
        "sky_cube": centred(arg_keys[0], (CH, NY, NX), 1.0, 6.0, ((0, 256),), jnp.float32),
        "kernel_one": centred(arg_keys[1], (C1, 1, 3, 3, 3), 27 ** -0.5, 1.25),
        "bias_one": centred(arg_keys[2], (C1,), 0.4, 2.0, (), jnp.float32),
        "kernel_two": centred(arg_keys[3], (C2, C1, 3, 3, 3), (27 * C1) ** -0.5, 0.4375),
        "bias_two": centred(arg_keys[4], (C2,), 0.4, 2.0, (), jnp.float32),
        "kernel_three": centred(arg_keys[5], (C3, C2, 3, 3, 3), (27 * C2) ** -0.5, 0.4375),
        "bias_three": centred(arg_keys[6], (C3,), 0.4, 2.0, (), jnp.float32),
    }


def convolve(volume, kernel, strides, padding):
    result = lax.conv_general_dilated(volume[None], kernel, strides, padding, dimension_numbers=("NCDHW", "OIDHW", "NCDHW"), preferred_element_type=jnp.float32)
    return result[0]


def leaky_relu(values):
    return jnp.maximum(values, 0.1 * values)


def reference(sky_cube, kernel_one, bias_one, kernel_two, bias_two, kernel_three, bias_three):
    slab = sky_cube.astype(jnp.bfloat16)
    padded = jnp.pad(slab, ((3, 3), (0, 0), (0, 0)))
    same_rows = ((0, 0), (1, 1), (1, 1))

    def one_group(index):
        begin_at = (index * GROUP).astype(jnp.int32)
        section = lax.dynamic_slice_in_dim(padded, begin_at, GROUP + 6, 0)[None]
        planes = begin_at - 2 + jnp.arange(GROUP + 4, dtype=jnp.int32)
        inside = ((planes >= 0) & (planes < CH))[None, :, None, None]
        values = leaky_relu(convolve(section, kernel_one, (1, 1, 1), same_rows) + bias_one[:, None, None, None])
        layer_one = jnp.where(inside, values, 0.0).astype(jnp.bfloat16)
        planes = begin_at - 1 + jnp.arange(GROUP + 2, dtype=jnp.int32)
        inside = ((planes >= 0) & (planes < CH))[None, :, None, None]
        values = leaky_relu(convolve(layer_one, kernel_two, (1, 1, 1), same_rows) + bias_two[:, None, None, None])
        layer_two = jnp.where(inside, values, 0.0).astype(jnp.bfloat16)
        values = leaky_relu(convolve(layer_two[:, :GROUP + 1], kernel_three, (2, 2, 2), same_rows) + bias_three[:, None, None, None])
        return values.astype(jnp.bfloat16)

    stacked = lax.map(one_group, jnp.arange(N_FREQ).astype(jnp.int32))
    return jnp.transpose(stacked, (1, 0, 2, 3, 4)).reshape(C3, CH // 2, NY // 2, NX // 2)
```

```python
import functools

import jax
import jax.numpy as jnp
from jax import lax
from jax.experimental import pallas as pl
from jax.experimental.pallas import tpu as pltpu
from jax.sharding import PartitionSpec as P

MESH = pl.DeviceIdType.MESH
BF = jnp.bfloat16
F32 = jnp.float32

SPAN = 16
PLANES = SPAN + 5
ROWS = 24
F1, Y1 = SPAN + 3, SPAN + 3
F2, Y2 = SPAN + 1, SPAN + 1
K1 = 80
K2 = 464
K3 = 416


def iota(shape, dim):
    return lax.broadcasted_iota(jnp.int32, shape, dim)


def exchange_kernel(sky, out, raw, moved, slab, in_sem, send_sem, recv_sem):
    groups, strips = lax.axis_size("freq"), lax.axis_size("tile")
    g, t = lax.axis_index("freq"), lax.axis_index("tile")
    height = raw.shape[0]

    load = pltpu.make_async_copy(sky.at[0], raw, in_sem)
    load.start()

    barrier = pltpu.get_barrier_semaphore()

    def greet(group, strip):
        pl.semaphore_signal(barrier, inc=1, device_id=(group, strip), device_id_type=MESH)

    @pl.loop(1, strips)
    def _(k):
        greet(g, lax.rem(t + k, strips))

    @pl.when(g < groups - 1)
    def _():
        for strip in (0, 1):
            greet(g + 1, strip)

    @pl.when(g > 0)
    def _():
        for strip in (strips - 3, strips - 2, strips - 1):
            greet(g - 1, strip)

    lane = iota((128, 128), 1)
    column = jnp.where(lane < 64, 2 * lane, 2 * lane - 127)
    order = (iota((128, 128), 0) == column).astype(F32).astype(BF)
    load.wait()
    values = jnp.dot(raw[...].astype(BF), order, preferred_element_type=F32)
    moved[0:8, :] = jnp.zeros((8, 128), F32)
    moved[height : height + 16, :] = jnp.zeros((16, 128), F32)
    moved[4 : height + 4, :] = values
    slab[...] = moved[...].reshape(slab.shape).astype(BF)

    upper = t >= strips - 3
    low = t < 2
    beyond = jnp.logical_or(jnp.logical_and(low, g > 0), jnp.logical_and(upper, g < groups - 1))
    other = jnp.where(low, jnp.maximum(g - 1, 0), jnp.minimum(g + 1, groups - 1))
    plane = 3 + t
    far_plane = jnp.where(low, SPAN + 3 + t, jnp.maximum(t - (strips - 3), 0))

    @pl.when(beyond)
    def _():
        pl.semaphore_wait(barrier, 2 * strips - 1)

    @pl.when(jnp.logical_not(beyond))
    def _():
        pl.semaphore_wait(barrier, strips - 1)

    def near(k):
        strip = lax.rem(t + k, strips)
        return pltpu.make_async_remote_copy(
            src_ref=slab.at[pl.ds(2 * strip, 3)],
            dst_ref=out.at[plane],
            send_sem=send_sem.at[k],
            recv_sem=recv_sem.at[plane],
            device_id=(g, strip),
            device_id_type=MESH,
        )

    def far(k):
        strip = lax.rem(t + k, strips)
        return pltpu.make_async_remote_copy(
            src_ref=slab.at[pl.ds(2 * strip, 3)],
            dst_ref=out.at[far_plane],
            send_sem=send_sem.at[strips + k],
            recv_sem=recv_sem.at[far_plane],
            device_id=(other, strip),
            device_id_type=MESH,
        )

    @pl.when(beyond)
    def _():
        @pl.loop(0, strips)
        def _(k):
            far(k).start()

    @pl.loop(1, strips)
    def _(k):
        near(k).start()

    out[plane] = slab[pl.ds(2 * t, 3)]

    def arrived(p):
        pltpu.make_async_copy(out.at[p], out.at[p], recv_sem.at[p]).wait()

    @pl.loop(1, strips)
    def _(k):
        arrived(3 + lax.rem(t + k, strips))

    @pl.when(g > 0)
    def _():
        for p in range(3):
            arrived(p)

    @pl.when(g == 0)
    def _():
        out[0:3] = jnp.zeros((3, 3, 8, 128), BF)

    @pl.when(g < groups - 1)
    def _():
        for p in (SPAN + 3, SPAN + 4):
            arrived(p)

    @pl.when(g == groups - 1)
    def _():
        out[SPAN + 3 : SPAN + 5] = jnp.zeros((2, 3, 8, 128), BF)

    @pl.loop(1, strips)
    def _(k):
        near(k).wait_send()

    @pl.when(beyond)
    def _():
        @pl.loop(0, strips)
        def _(k):
            far(k).wait_send()


def exchange(sky_cube):
    height = sky_cube.shape[1]
    strips = height // SPAN
    return pl.pallas_call(
        exchange_kernel,
        out_shape=jax.ShapeDtypeStruct((PLANES, 3, 8, 128), BF),
        in_specs=[pl.BlockSpec(memory_space=pl.ANY)],
        out_specs=pl.BlockSpec(memory_space=pltpu.VMEM),
        scratch_shapes=[
            pltpu.VMEM((height, 128), F32),
            pltpu.VMEM((height + 16, 128), F32),
            pltpu.VMEM(((height + 16) // 8, 8, 128), BF),
            pltpu.SemaphoreType.DMA,
            pltpu.SemaphoreType.DMA((2 * strips,)),
            pltpu.SemaphoreType.DMA((PLANES,)),
        ],
        compiler_params=pltpu.CompilerParams(
            collective_id=0, has_side_effects=True, vmem_limit_bytes=8 << 20
        ),
        name="exchange",
    )(sky_cube)


def leaky(values):
    return jnp.maximum(values, 0.1 * values)


def parts_of(k):
    i = (k * 2428) >> 16
    k = k - 27 * i
    a = (k * 7282) >> 16
    k = k - 9 * a
    b = (k * 21846) >> 16
    return i, a, b, k - 3 * b


def placed(flat, columns, target):
    k = flat.shape[1]
    source = iota((k, columns), 0)
    hits = iota((k, columns), 1) == target(*parts_of(source))
    return jnp.dot(flat, hits.astype(F32).astype(BF), preferred_element_type=F32)


def beside(values):
    lane = iota(values.shape, 1)
    swapped = pltpu.roll(values, 64, 1)
    before = jnp.where(lane < 64, pltpu.roll(values, 65, 1), swapped)
    after = jnp.where(lane < 64, swapped, pltpu.roll(values, 63, 1))
    return (
        jnp.where(lane == 0, 0.0, before),
        values,
        jnp.where(lane == 127, 0.0, after),
    )


def column_of(bias, rows, count):
    row = iota((count, 128), 0)
    block = jnp.zeros((count, 128), F32)
    for o in range(count):
        block = jnp.where(row == o, bias[o], block)
    return jnp.concatenate([block] * (rows // count), axis=0)


def banded_weights(k1, k2, k3, w1, w2, w3):
    base = placed(k1[...], 256, lambda i, a, b, c: jnp.where(i == 0, a * K1 + c * ROWS + 1 + b, -1))
    for y in range(0, Y1, 2):
        both = [pltpu.roll(base, s, 1) if s else base for s in (y, y + 1)]
        w1[8 * y : 8 * y + 16, :] = jnp.concatenate(both, axis=0).astype(BF)

    base = placed(
        k2[...], 1408, lambda i, a, b, c: jnp.where(i < 8, a * K2 + c * (8 * Y1) + 8 * b + i, -1)
    )
    for y in range(0, Y2, 2):
        both = [pltpu.roll(base, 8 * s, 1) if s else base for s in (y, min(y + 1, Y2 - 1))]
        w2[8 * y : 8 * y + 16, :] = jnp.concatenate(both, axis=0).astype(BF)

    base = placed(
        k3[...], 1280, lambda i, a, b, c: jnp.where(i < 8, a * K3 + c * (8 * Y2) + 8 * b + i, -1)
    )
    rows = [pltpu.roll(base, 16 * y, 1) if y else base for y in range(SPAN // 2)]
    by_row = jnp.concatenate(rows, axis=0).astype(BF)
    r = iota((128, 128), 0)
    swap = iota((128, 128), 1) == (r & 7) * 16 + (r >> 3)
    w3[...] = jnp.dot(
        swap.astype(F32).astype(BF), by_row, preferred_element_type=F32
    ).astype(BF)


def conv_kernel(pos, cube, k1, k2, k3, b1, b2, b3, out, x1, x2, l2, x3, w1, w2, w3):
    if pos is None:
        groups, strips = lax.axis_size("freq"), lax.axis_size("tile")
        g, t = lax.axis_index("freq"), lax.axis_index("tile")
    else:
        groups, strips, g, t = pos
    banded_weights(k1, k2, k3, w1, w2, w3)

    def one_if(inside):
        return jnp.where(inside, 1.0, 0.0).astype(F32)

    for f in range(PLANES):
        pieces = beside(cube[f].astype(F32))
        block = jnp.concatenate([*pieces, jnp.zeros((K1 - 3 * ROWS, 128), F32)], axis=0)
        x1[f * K1 : (f + 1) * K1, :] = block.astype(BF)

    first_g, last_g = one_if(g > 0), one_if(g < groups - 1)
    first_t, last_t = one_if(t > 0), one_if(t < strips - 1)
    bias = column_of(b1, 8 * Y1, 8)
    row = iota((8 * Y1, 128), 0)
    keep = jnp.where(row < 16, first_t, jnp.where(row >= 8 * (Y1 - 1), last_t, 1.0))
    weights = w1[0 : 8 * Y1, 0 : 3 * K1]
    for f in range(0, F1, 2):
        fs = [f, f + 1] if f + 1 < F1 else [f]
        data = jnp.concatenate([x1[h * K1 : (h + 3) * K1, :] for h in fs], axis=1)
        sums = jnp.dot(weights, data, preferred_element_type=F32)
        for n, h in enumerate(fs):
            values = leaky(sums[:, 128 * n : 128 * (n + 1)] + bias) * keep
            if h < 2:
                values = values * first_g
            if h == F1 - 1:
                values = values * last_g
            block = jnp.concatenate(
                [*beside(values), jnp.zeros((K2 - 24 * Y1, 128), F32)], axis=0
            )
            x2[h * K2 : (h + 1) * K2, :] = block.astype(BF)

    bias = column_of(b2, 8 * Y2, 8)
    keep = jnp.where(iota((8 * Y2, 128), 0) < 8, first_t, 1.0)
    weights = w2[0 : 8 * Y2, 0 : 3 * K2]
    for f in range(0, F2, 2):
        fs = [f, f + 1] if f + 1 < F2 else [f]
        data = jnp.concatenate([x2[h * K2 : (h + 3) * K2, :] for h in fs], axis=1)
        sums = jnp.dot(weights, data, preferred_element_type=F32)
        for n, h in enumerate(fs):
            values = leaky(sums[:, 128 * n : 128 * (n + 1)] + bias) * keep
            if h == 0:
                values = values * first_g
            l2[h] = values

    half = SPAN // 2
    lane = iota((8 * Y2, 128), 1)
    for f in range(half + 1):
        lower, upper = l2[f], l2[f + half]
        before = jnp.where(lane < 64, pltpu.roll(lower, 65, 1), pltpu.roll(upper, 1, 1))
        block = jnp.concatenate(
            [
                jnp.where((lane & 63) == 0, 0.0, before),
                jnp.where(lane < 64, lower, pltpu.roll(upper, 64, 1)),
                jnp.where(lane < 64, pltpu.roll(lower, 64, 1), upper),
                jnp.zeros((K3 - 24 * Y2, 128), F32),
            ],
            axis=0,
        )
        x3[f * K3 : (f + 1) * K3, :] = block.astype(BF)
    bias = jnp.concatenate([jnp.full((8, 128), b3[o], F32) for o in range(16)], axis=0)
    weights = w3[:, 0 : 3 * K3]
    quarter = half // 2
    for f in range(0, quarter, 2):
        data = jnp.concatenate(
            [x3[2 * h * K3 : (2 * h + 3) * K3, :] for h in (f, f + 1)], axis=1
        )
        sums = jnp.dot(weights, data, preferred_element_type=F32)
        for n, h in enumerate((f, f + 1)):
            values = leaky(sums[:, 128 * n : 128 * (n + 1)] + bias)
            out[:, h, :, :] = values[:, 0:64].reshape(16, 8, 64).astype(BF)
            swapped = pltpu.roll(values, 64, 1)
            out[:, h + quarter, :, :] = swapped[:, 0:64].reshape(16, 8, 64).astype(BF)


def convolutions(cube, k1, k2, k3, b1, b2, b3, pos=None, interpret=False):
    vmem = pl.BlockSpec(memory_space=pltpu.VMEM)
    smem = pl.BlockSpec(memory_space=pltpu.SMEM)
    half = SPAN // 2
    return pl.pallas_call(
        functools.partial(conv_kernel, pos),
        out_shape=jax.ShapeDtypeStruct((16, half, half, 64), BF),
        in_specs=[vmem, vmem, vmem, vmem, smem, smem, smem],
        out_specs=vmem,
        scratch_shapes=[
            pltpu.VMEM((PLANES * K1, 128), BF),
            pltpu.VMEM((F1 * K2, 128), BF),
            pltpu.VMEM((F2, 8 * Y2, 128), F32),
            pltpu.VMEM(((half + 1) * K3, 128), BF),
            pltpu.VMEM((160, 256), BF),
            pltpu.VMEM((144, 1408), BF),
            pltpu.VMEM((128, 1280), BF),
        ],
        compiler_params=pltpu.CompilerParams(vmem_limit_bytes=24 << 20),
        interpret=interpret,
        name="convolutions",
    )(cube, k1, k2, k3, b1, b2, b3)


def flat(kernel):
    rows = kernel.shape[0]
    count = kernel.size // rows
    return jnp.pad(kernel.reshape(rows, count), ((0, 0), (0, -count % 128)))


def body(sky_cube, kernel_one, bias_one, kernel_two, bias_two, kernel_three, bias_three):
    cube = exchange(sky_cube).reshape(PLANES, ROWS, 128)
    return convolutions(
        cube,
        flat(kernel_one),
        flat(kernel_two),
        flat(kernel_three),
        bias_one,
        bias_two,
        bias_three,
    )


def solution(mesh):
    return jax.shard_map(
        body,
        mesh=mesh,
        in_specs=(P(("freq", "tile"), None, None), P(), P(), P(), P(), P(), P()),
        out_specs=P(None, "freq", "tile", None),
        check_vma=False,
    )
```

```python
import jax
import jax.numpy as jnp
from jax import lax
from jax.experimental import pallas as pl
from jax.experimental.pallas import tpu as pltpu
from jax.sharding import PartitionSpec as P

MESH = pl.DeviceIdType.MESH
BF = jnp.bfloat16
F32 = jnp.float32

SPAN = 16
PLANES = SPAN + 5
ROWS = 24
F1, Y1 = SPAN + 3, SPAN + 3
F2, Y2 = SPAN + 1, SPAN + 1
K1 = 80
K2 = 464
K3 = 416


def iota(shape, dim):
    return lax.broadcasted_iota(jnp.int32, shape, dim)


def leaky(values):
    return jnp.maximum(values, 0.1 * values)


def beside(values):
    lane = iota(values.shape, 1)
    swapped = pltpu.roll(values, 64, 1)
    before = jnp.where(lane < 64, pltpu.roll(values, 65, 1), swapped)
    after = jnp.where(lane < 64, swapped, pltpu.roll(values, 63, 1))
    return (
        jnp.where(lane == 0, 0.0, before),
        values,
        jnp.where(lane == 127, 0.0, after),
    )


def column_of(bias, rows, count):
    row = iota((count, 128), 0)
    block = jnp.zeros((count, 128), F32)
    for o in range(count):
        block = jnp.where(row == o, bias[o], block)
    return jnp.concatenate([block] * (rows // count), axis=0)


def taps():
    return [(a, b, c) for a in range(3) for b in range(3) for c in range(3)]


def one_if(inside):
    return jnp.where(inside, 1.0, 0.0).astype(F32)


def banded_weights(k1, k2, k3, stack1, base2, stack3, w1, w2, w3):
    stack1[...] = jnp.zeros(stack1.shape, F32)
    for a in range(3):
        for b in range(3):
            at = 8 * (3 * a + b)
            stack1[at : at + 3, 0:8] = k1[0, a, b].astype(F32)
    source = iota((128, 256), 0)
    tap, c = source >> 3, source & 7
    a = (tap * 21846) >> 16
    target = jnp.where((tap < 9) & (c < 3), a * K1 + c * ROWS + 1 + tap - 3 * a, -1)
    base = jnp.dot(
        stack1[...].T[0:8].astype(BF),
        (iota((128, 256), 1) == target).astype(F32).astype(BF),
        preferred_element_type=F32,
    )
    for y in range(0, Y1, 2):
        both = [pltpu.roll(base, s, 1) if s else base for s in (y, y + 1)]
        w1[8 * y : 8 * y + 16, :] = jnp.concatenate(both, axis=0).astype(BF)

    base2[...] = jnp.zeros(base2.shape, F32)
    for a, b, c in taps():
        at = a * K2 + c * (8 * Y1) + 8 * b
        base2[:, at : at + 8] = k2[a, b, c].astype(F32)
    base = base2[...]
    for y in range(0, Y2, 2):
        both = [pltpu.roll(base, 8 * s, 1) if s else base for s in (y, min(y + 1, Y2 - 1))]
        w2[8 * y : 8 * y + 16, :] = jnp.concatenate(both, axis=0).astype(BF)

    stack3[...] = jnp.zeros(stack3.shape, F32)
    for n, (a, b, c) in enumerate(taps()):
        stack3[8 * n : 8 * n + 8, 0:16] = k3[a, b, c].astype(F32)
    source = iota((256, 1280), 0)
    tap, i = source >> 3, source & 7
    a = (tap * 7282) >> 16
    rest = tap - 9 * a
    b = (rest * 21846) >> 16
    target = jnp.where(tap < 27, a * K3 + (rest - 3 * b) * (8 * Y2) + 8 * b + i, -1)
    base = jnp.dot(
        stack3[...].T[0:16].astype(BF),
        (iota((256, 1280), 1) == target).astype(F32).astype(BF),
        preferred_element_type=F32,
    )
    rows = [pltpu.roll(base, 16 * y, 1) if y else base for y in range(SPAN // 2)]
    by_row = jnp.concatenate(rows, axis=0).astype(BF)
    r = iota((128, 128), 0)
    swap = iota((128, 128), 1) == (r & 7) * 16 + (r >> 3)
    w3[...] = jnp.dot(
        swap.astype(F32).astype(BF), by_row, preferred_element_type=F32
    ).astype(BF)


def two_layers(place, cube, far_channels, b1, b2, x1, x2, l2, x3, w1, w2):
    groups, strips, g, t = place
    first_g, last_g = one_if(g > 0), one_if(g < groups - 1)
    first_t, last_t = one_if(t > 0), one_if(t < strips - 1)

    def operand(f):
        pieces = beside(cube[f].reshape(ROWS, 128).astype(F32))
        block = jnp.concatenate([*pieces, jnp.zeros((K1 - 3 * ROWS, 128), F32)], axis=0)
        x1[f * K1 : (f + 1) * K1, :] = block.astype(BF)

    bias1 = column_of(b1, 8 * Y1, 8)
    row = iota((8 * Y1, 128), 0)
    keep1 = jnp.where(row < 16, first_t, jnp.where(row >= 8 * (Y1 - 1), last_t, 1.0))

    def layer_one(*fs):
        data = jnp.concatenate([x1[h * K1 : (h + 3) * K1, :] for h in fs], axis=1)
        sums = jnp.dot(w1[0 : 8 * Y1, 0 : 3 * K1], data, preferred_element_type=F32)
        for n, h in enumerate(fs):
            values = leaky(sums[:, 128 * n : 128 * (n + 1)] + bias1) * keep1
            if h < 2:
                values = values * first_g
            if h == F1 - 1:
                values = values * last_g
            block = jnp.concatenate(
                [*beside(values), jnp.zeros((K2 - 24 * Y1, 128), F32)], axis=0
            )
            x2[h * K2 : (h + 1) * K2, :] = block.astype(BF)

    bias2 = column_of(b2, 8 * Y2, 8)
    keep2 = jnp.where(iota((8 * Y2, 128), 0) < 8, first_t, 1.0)

    def layer_two(*fs):
        data = jnp.concatenate([x2[h * K2 : (h + 3) * K2, :] for h in fs], axis=1)
        sums = jnp.dot(w2[0 : 8 * Y2, 0 : 3 * K2], data, preferred_element_type=F32)
        for n, h in enumerate(fs):
            values = leaky(sums[:, 128 * n : 128 * (n + 1)] + bias2) * keep2
            if h == 0:
                values = values * first_g
            l2[h] = values

    half = SPAN // 2
    lane = iota((8 * Y2, 128), 1)

    def joined(f):
        lower, upper = l2[f], l2[f + half]
        before = jnp.where(lane < 64, pltpu.roll(lower, 65, 1), pltpu.roll(upper, 1, 1))
        block = jnp.concatenate(
            [
                jnp.where((lane & 63) == 0, 0.0, before),
                jnp.where(lane < 64, lower, pltpu.roll(upper, 64, 1)),
                jnp.where(lane < 64, pltpu.roll(lower, 64, 1), upper),
                jnp.zeros((K3 - 24 * Y2, 128), F32),
            ],
            axis=0,
        )
        x3[f * K3 : (f + 1) * K3, :] = block.astype(BF)

    for f in range(3, SPAN + 3):
        operand(f)
    for f in range(3, SPAN + 1, 2):
        layer_one(f, f + 1)
    for f in range(3, SPAN - 1, 2):
        layer_two(f, f + 1)
    for f in range(3, 7):
        joined(f)
    far_channels()
    for f in (0, 1, 2, SPAN + 3, SPAN + 4):
        operand(f)
    layer_one(0, 1)
    layer_one(2, 17)
    layer_one(18)
    layer_two(0, 1)
    layer_two(2, 15)
    layer_two(16)
    for f in (0, 1, 2, 7, 8):
        joined(f)


def spread_kernel(
    sky, k1_in, k2_in, k3_in, b1_in, b2_in, b3_in,
    x3, w3, bias3,
    raw, moved, slab, cube, k1, k2, k3, b1, b2, b3, stack1, base2, stack3, w1, w2, x1, x2, l2,
    in_sem, send_sem, recv_sem,
):
    groups, strips = lax.axis_size("freq"), lax.axis_size("tile")
    g, t = lax.axis_index("freq"), lax.axis_index("tile")
    height = raw.shape[0]

    barrier = pltpu.get_barrier_semaphore()

    def greet(group, strip):
        pl.semaphore_signal(barrier, inc=1, device_id=(group, strip), device_id_type=MESH)

    @pl.when(g < groups - 1)
    def _():
        for strip in (0, 1):
            greet(g + 1, strip)

    @pl.when(g > 0)
    def _():
        for strip in (strips - 3, strips - 2, strips - 1):
            greet(g - 1, strip)

    @pl.loop(1, strips)
    def _(k):
        greet(g, lax.rem(t + k, strips))

    pairs = [(sky.at[0], raw), (k1_in, k1), (k2_in, k2), (k3_in, k3), (b1_in, b1), (b2_in, b2), (b3_in, b3)]
    loads = [pltpu.make_async_copy(a, b, in_sem.at[n]) for n, (a, b) in enumerate(pairs)]
    for load in loads:
        load.start()

    lane = iota((128, 128), 1)
    column = jnp.where(lane < 64, 2 * lane, 2 * lane - 127)
    order = (iota((128, 128), 0) == column).astype(F32).astype(BF)
    moved[0:8, :] = jnp.zeros((8, 128), F32)
    moved[height : height + 16, :] = jnp.zeros((16, 128), F32)
    loads[0].wait()
    values = jnp.dot(raw[...].astype(BF), order, preferred_element_type=F32)
    moved[4 : height + 4, :] = values
    slab[...] = moved[...].reshape(slab.shape).astype(BF)

    upper = t >= strips - 3
    low = t < 2
    beyond = jnp.logical_or(jnp.logical_and(low, g > 0), jnp.logical_and(upper, g < groups - 1))
    other = jnp.where(low, jnp.maximum(g - 1, 0), jnp.minimum(g + 1, groups - 1))
    plane = 3 + t
    far_plane = jnp.where(low, SPAN + 3 + t, jnp.maximum(t - (strips - 3), 0))

    @pl.when(beyond)
    def _():
        pl.semaphore_wait(barrier, 2 * strips - 1)

    @pl.when(jnp.logical_not(beyond))
    def _():
        pl.semaphore_wait(barrier, strips - 1)

    def near(k):
        strip = lax.rem(t + k, strips)
        return pltpu.make_async_remote_copy(
            src_ref=slab.at[pl.ds(2 * strip, 3)],
            dst_ref=cube.at[plane],
            send_sem=send_sem.at[k],
            recv_sem=recv_sem.at[plane],
            device_id=(g, strip),
            device_id_type=MESH,
        )

    def far(k):
        strip = lax.rem(t + k, strips)
        return pltpu.make_async_remote_copy(
            src_ref=slab.at[pl.ds(2 * strip, 3)],
            dst_ref=cube.at[far_plane],
            send_sem=send_sem.at[strips + k],
            recv_sem=recv_sem.at[far_plane],
            device_id=(other, strip),
            device_id_type=MESH,
        )

    @pl.when(beyond)
    def _():
        @pl.loop(0, strips)
        def _(k):
            far(k).start()

    @pl.loop(1, strips)
    def _(k):
        near(k).start()

    cube[plane] = slab[pl.ds(2 * t, 3)]

    for load in loads[1:]:
        load.wait()
    banded_weights(k1, k2, k3, stack1, base2, stack3, w1, w2, w3)
    for o in range(16):
        bias3[8 * o : 8 * o + 8, :] = jnp.full((8, 128), b3[o], F32)

    def arrived(p):
        pltpu.make_async_copy(cube.at[p], cube.at[p], recv_sem.at[p]).wait()

    @pl.loop(1, strips)
    def _(k):
        arrived(3 + lax.rem(t + k, strips))

    def far_channels():
        @pl.when(g > 0)
        def _():
            for p in range(3):
                arrived(p)

        @pl.when(g == 0)
        def _():
            cube[0:3] = jnp.zeros((3, 3, 8, 128), BF)

        @pl.when(g < groups - 1)
        def _():
            for p in (SPAN + 3, SPAN + 4):
                arrived(p)

        @pl.when(g == groups - 1)
        def _():
            cube[SPAN + 3 : SPAN + 5] = jnp.zeros((2, 3, 8, 128), BF)

    two_layers((groups, strips, g, t), cube, far_channels, b1, b2, x1, x2, l2, x3, w1, w2)

    @pl.loop(1, strips)
    def _(k):
        near(k).wait_send()

    @pl.when(beyond)
    def _():
        @pl.loop(0, strips)
        def _(k):
            far(k).wait_send()


X3_SHAPE = ((SPAN // 2 + 1) * K3, 128)
WEIGHT_SCRATCH = [
    pltpu.VMEM((128, 128), F32),
    pltpu.VMEM((8, 1408), F32),
    pltpu.VMEM((256, 128), F32),
    pltpu.VMEM((160, 256), BF),
    pltpu.VMEM((144, 1408), BF),
]
LAYER_SCRATCH = [
    pltpu.VMEM((PLANES * K1, 128), BF),
    pltpu.VMEM((F1 * K2, 128), BF),
    pltpu.VMEM((F2, 8 * Y2, 128), F32),
]


def first_layers(sky_cube, k1, k2, k3, b1, b2, b3):
    height = sky_cube.shape[1]
    strips = height // SPAN
    operands = [
        pltpu.with_memory_space_constraint(x, pltpu.HBM)
        for x in (sky_cube, k1, k2, k3, b1, b2, b3)
    ]
    vmem = pl.BlockSpec(memory_space=pltpu.VMEM)
    return pl.pallas_call(
        spread_kernel,
        out_shape=[
            jax.ShapeDtypeStruct(X3_SHAPE, BF),
            jax.ShapeDtypeStruct((128, 1280), BF),
            jax.ShapeDtypeStruct((128, 128), F32),
        ],
        in_specs=[pl.BlockSpec(memory_space=pltpu.HBM)] * len(operands),
        out_specs=[vmem] * 3,
        scratch_shapes=[
            pltpu.VMEM((height, 128), F32),
            pltpu.VMEM((height + 16, 128), F32),
            pltpu.VMEM(((height + 16) // 8, 8, 128), BF),
            pltpu.VMEM((PLANES, 3, 8, 128), BF),
            pltpu.VMEM(k1.shape, BF),
            pltpu.VMEM(k2.shape, BF),
            pltpu.VMEM(k3.shape, BF),
            pltpu.SMEM(b1.shape, F32),
            pltpu.SMEM(b2.shape, F32),
            pltpu.SMEM(b3.shape, F32),
            *WEIGHT_SCRATCH,
            *LAYER_SCRATCH,
            pltpu.SemaphoreType.DMA((len(operands),)),
            pltpu.SemaphoreType.DMA((2 * strips,)),
            pltpu.SemaphoreType.DMA((PLANES,)),
        ],
        compiler_params=pltpu.CompilerParams(
            collective_id=0, has_side_effects=True, vmem_limit_bytes=24 << 20
        ),
        name="first_layers",
    )(*operands)


def third_kernel(x3, w3, bias3, out):
    quarter = SPAN // 4
    for f in range(0, quarter, 2):
        data = jnp.concatenate(
            [x3[2 * h * K3 : (2 * h + 3) * K3, :] for h in (f, f + 1)], axis=1
        )
        sums = jnp.dot(w3[:, 0 : 3 * K3], data, preferred_element_type=F32)
        for n, h in enumerate((f, f + 1)):
            values = leaky(sums[:, 128 * n : 128 * (n + 1)] + bias3[...])
            out[:, h, :, :] = values[:, 0:64].reshape(16, 8, 64).astype(BF)
            swapped = pltpu.roll(values, 64, 1)
            out[:, h + quarter, :, :] = swapped[:, 0:64].reshape(16, 8, 64).astype(BF)


def third_layer(x3, w3, bias3):
    vmem = pl.BlockSpec(memory_space=pltpu.VMEM)
    half = SPAN // 2
    return pl.pallas_call(
        third_kernel,
        out_shape=jax.ShapeDtypeStruct((16, half, half, 64), BF),
        in_specs=[vmem] * 3,
        out_specs=vmem,
        compiler_params=pltpu.CompilerParams(vmem_limit_bytes=8 << 20),
        name="third_layer",
    )(x3, w3, bias3)


def body(sky_cube, kernel_one, bias_one, kernel_two, bias_two, kernel_three, bias_three):
    return third_layer(
        *first_layers(
            sky_cube,
            kernel_one.transpose(1, 2, 3, 4, 0),
            kernel_two.transpose(2, 3, 4, 0, 1),
            kernel_three.transpose(2, 3, 4, 1, 0),
            bias_one,
            bias_two,
            bias_three,
        )
    )


def solution(mesh):
    return jax.shard_map(
        body,
        mesh=mesh,
        in_specs=(P(("freq", "tile"), None, None), P(), P(), P(), P(), P(), P()),
        out_specs=P(None, "freq", "tile", None),
        check_vma=False,
    )
```

```python
import jax
import jax.numpy as jnp
from jax import lax
from jax.experimental import pallas as pl
from jax.experimental.pallas import tpu as pltpu
from jax.sharding import PartitionSpec as P

MESH = pl.DeviceIdType.MESH
BF = jnp.bfloat16
F32 = jnp.float32

SPAN = 16
PLANES = SPAN + 5
ROWS = 24
F1, Y1 = SPAN + 3, SPAN + 3
F2, Y2 = SPAN + 1, SPAN + 1
K1 = 80
K2 = 464
K3 = 416


def iota(shape, dim):
    return lax.broadcasted_iota(jnp.int32, shape, dim)


def leaky(values):
    return jnp.maximum(values, 0.1 * values)


def beside(values):
    lane = iota(values.shape, 1)
    swapped = pltpu.roll(values, 64, 1)
    before = jnp.where(lane < 64, pltpu.roll(values, 65, 1), swapped)
    after = jnp.where(lane < 64, swapped, pltpu.roll(values, 63, 1))
    return (
        jnp.where(lane == 0, 0.0, before),
        values,
        jnp.where(lane == 127, 0.0, after),
    )


def column_of(bias, rows, count):
    row = iota((count, 128), 0)
    block = jnp.zeros((count, 128), F32)
    for o in range(count):
        block = jnp.where(row == o, bias[o], block)
    return jnp.concatenate([block] * (rows // count), axis=0)


def taps():
    return [(a, b, c) for a in range(3) for b in range(3) for c in range(3)]


def one_if(inside):
    return jnp.where(inside, 1.0, 0.0).astype(F32)


def banded_weights(k1, k2, k3, stack1, base2, stack3, w1, w2, w3):
    stack1[...] = jnp.zeros(stack1.shape, F32)
    for a in range(3):
        for b in range(3):
            at = 8 * (3 * a + b)
            stack1[at : at + 3, 0:8] = k1[0, a, b].astype(F32)
    source = iota((128, 256), 0)
    tap, c = source >> 3, source & 7
    a = (tap * 21846) >> 16
    target = jnp.where((tap < 9) & (c < 3), a * K1 + c * ROWS + 1 + tap - 3 * a, -1)
    base = jnp.dot(
        stack1[...].T[0:8].astype(BF),
        (iota((128, 256), 1) == target).astype(F32).astype(BF),
        preferred_element_type=F32,
    )
    for y in range(0, Y1, 2):
        both = [pltpu.roll(base, s, 1) if s else base for s in (y, y + 1)]
        w1[8 * y : 8 * y + 16, :] = jnp.concatenate(both, axis=0).astype(BF)

    base2[...] = jnp.zeros(base2.shape, F32)
    for a, b, c in taps():
        at = a * K2 + c * (8 * Y1) + 8 * b
        base2[:, at : at + 8] = k2[a, b, c].astype(F32)
    base = base2[...]
    for y in range(0, Y2, 2):
        both = [pltpu.roll(base, 8 * s, 1) if s else base for s in (y, min(y + 1, Y2 - 1))]
        w2[8 * y : 8 * y + 16, :] = jnp.concatenate(both, axis=0).astype(BF)

    stack3[...] = jnp.zeros(stack3.shape, F32)
    for n, (a, b, c) in enumerate(taps()):
        stack3[8 * n : 8 * n + 8, 0:16] = k3[a, b, c].astype(F32)
    source = iota((256, 1280), 0)
    tap, i = source >> 3, source & 7
    a = (tap * 7282) >> 16
    rest = tap - 9 * a
    b = (rest * 21846) >> 16
    target = jnp.where(tap < 27, a * K3 + (rest - 3 * b) * (8 * Y2) + 8 * b + i, -1)
    base = jnp.dot(
        stack3[...].T[0:16].astype(BF),
        (iota((256, 1280), 1) == target).astype(F32).astype(BF),
        preferred_element_type=F32,
    )
    rows = [pltpu.roll(base, 16 * y, 1) if y else base for y in range(SPAN // 2)]
    by_row = jnp.concatenate(rows, axis=0).astype(BF)
    r = iota((128, 128), 0)
    swap = iota((128, 128), 1) == (r & 7) * 16 + (r >> 3)
    w3[...] = jnp.dot(
        swap.astype(F32).astype(BF), by_row, preferred_element_type=F32
    ).astype(BF)


def third_matmul(x3, first, w3, bias3, out):
    data = jnp.concatenate(
        [x3[h * K3 : (h + 3) * K3, :] for h in (first, first + 2)], axis=1
    )
    sums = jnp.dot(w3[:, 0 : 3 * K3], data, preferred_element_type=F32)
    for n in range(2):
        values = leaky(sums[:, 128 * n : 128 * (n + 1)] + bias3[...])
        out[:, n, :, :] = values[:, 0:64].reshape(16, 8, 64).astype(BF)
        swapped = pltpu.roll(values, 64, 1)
        out[:, n + 2, :, :] = swapped[:, 0:64].reshape(16, 8, 64).astype(BF)


def all_layers(place, cube, arrive, b1, b2, bias3, x1, x2, l2, x3_upper, x3, w1, w2, w3, upper):
    groups, strips, g, t = place
    first_g, last_g = one_if(g > 0), one_if(g < groups - 1)
    first_t, last_t = one_if(t > 0), one_if(t < strips - 1)

    def operand(f):
        pieces = beside(cube[f].reshape(ROWS, 128).astype(F32))
        block = jnp.concatenate([*pieces, jnp.zeros((K1 - 3 * ROWS, 128), F32)], axis=0)
        x1[f * K1 : (f + 1) * K1, :] = block.astype(BF)

    bias1 = column_of(b1, 8 * Y1, 8)
    row = iota((8 * Y1, 128), 0)
    keep1 = jnp.where(row < 16, first_t, jnp.where(row >= 8 * (Y1 - 1), last_t, 1.0))

    def layer_one(*fs):
        data = jnp.concatenate([x1[h * K1 : (h + 3) * K1, :] for h in fs], axis=1)
        sums = jnp.dot(w1[0 : 8 * Y1, 0 : 3 * K1], data, preferred_element_type=F32)
        for n, h in enumerate(fs):
            values = leaky(sums[:, 128 * n : 128 * (n + 1)] + bias1) * keep1
            if h < 2:
                values = values * first_g
            if h == F1 - 1:
                values = values * last_g
            block = jnp.concatenate(
                [*beside(values), jnp.zeros((K2 - 24 * Y1, 128), F32)], axis=0
            )
            x2[h * K2 : (h + 1) * K2, :] = block.astype(BF)

    bias2 = column_of(b2, 8 * Y2, 8)
    keep2 = jnp.where(iota((8 * Y2, 128), 0) < 8, first_t, 1.0)

    def layer_two(*fs):
        data = jnp.concatenate([x2[h * K2 : (h + 3) * K2, :] for h in fs], axis=1)
        sums = jnp.dot(w2[0 : 8 * Y2, 0 : 3 * K2], data, preferred_element_type=F32)
        for n, h in enumerate(fs):
            values = leaky(sums[:, 128 * n : 128 * (n + 1)] + bias2) * keep2
            if h == 0:
                values = values * first_g
            l2[h] = values

    lane = iota((8 * Y2, 128), 1)

    def joined(to, at, f):
        lower, upper = l2[f], l2[f + 4]
        before = jnp.where(lane < 64, pltpu.roll(lower, 65, 1), pltpu.roll(upper, 1, 1))
        block = jnp.concatenate(
            [
                jnp.where((lane & 63) == 0, 0.0, before),
                jnp.where(lane < 64, lower, pltpu.roll(upper, 64, 1)),
                jnp.where(lane < 64, pltpu.roll(lower, 64, 1), upper),
                jnp.zeros((K3 - 24 * Y2, 128), F32),
            ],
            axis=0,
        )
        to[at * K3 : (at + 1) * K3, :] = block.astype(BF)

    arrive("inner")
    for f in range(5, SPAN):
        operand(f)
    for f in (5, 7, 9, 11):
        layer_one(f, f + 1)
    for f in (5, 7, 9):
        layer_two(f, f + 1)
    arrive("upper")
    for f in range(SPAN, PLANES):
        operand(f)
    for f in (13, 15, 17):
        layer_one(f, f + 1)
    for f in (11, 13, 15):
        layer_two(f, f + 1)
    for n in range(5):
        joined(x3_upper, n, 8 + n)
    third_matmul(x3_upper, 0, w3, bias3, upper)
    arrive("lower")
    for f in range(5):
        operand(f)
    layer_one(0, 1)
    layer_one(2, 3)
    layer_one(4)
    layer_two(0, 1)
    layer_two(2, 3)
    layer_two(4)
    for n in range(5):
        joined(x3, n, n)


def spread_kernel(
    sky, k1_in, k2_in, k3_in, b1_in, b2_in, b3_in,
    x3, w3, bias3, upper,
    raw, moved, slab, cube, k1, k2, k3, b1, b2, b3, stack1, base2, stack3, w1, w2, x1, x2, l2, x3_upper,
    in_sem, send_sem, recv_sem,
):
    groups, strips = lax.axis_size("freq"), lax.axis_size("tile")
    g, t = lax.axis_index("freq"), lax.axis_index("tile")
    height = raw.shape[0]

    barrier = pltpu.get_barrier_semaphore()

    def greet(group, strip):
        pl.semaphore_signal(barrier, inc=1, device_id=(group, strip), device_id_type=MESH)

    @pl.when(g < groups - 1)
    def _():
        for strip in (0, 1):
            greet(g + 1, strip)

    @pl.when(g > 0)
    def _():
        for strip in (strips - 3, strips - 2, strips - 1):
            greet(g - 1, strip)

    @pl.loop(1, strips)
    def _(k):
        greet(g, lax.rem(t + k, strips))

    pairs = [(sky.at[0], raw), (k1_in, k1), (k2_in, k2), (k3_in, k3), (b1_in, b1), (b2_in, b2), (b3_in, b3)]
    loads = [pltpu.make_async_copy(a, b, in_sem.at[n]) for n, (a, b) in enumerate(pairs)]
    for load in loads:
        load.start()

    lane = iota((128, 128), 1)
    column = jnp.where(lane < 64, 2 * lane, 2 * lane - 127)
    order = (iota((128, 128), 0) == column).astype(F32).astype(BF)
    moved[0:8, :] = jnp.zeros((8, 128), F32)
    moved[height : height + 16, :] = jnp.zeros((16, 128), F32)
    loads[0].wait()
    values = jnp.dot(raw[...].astype(BF), order, preferred_element_type=F32)
    moved[4 : height + 4, :] = values
    slab[...] = moved[...].reshape(slab.shape).astype(BF)

    high = t >= strips - 3
    low = t < 2
    beyond = jnp.logical_or(jnp.logical_and(low, g > 0), jnp.logical_and(high, g < groups - 1))
    other = jnp.where(low, jnp.maximum(g - 1, 0), jnp.minimum(g + 1, groups - 1))
    plane = 3 + t
    far_plane = jnp.where(low, SPAN + 3 + t, jnp.maximum(t - (strips - 3), 0))

    @pl.when(beyond)
    def _():
        pl.semaphore_wait(barrier, 2 * strips - 1)

    @pl.when(jnp.logical_not(beyond))
    def _():
        pl.semaphore_wait(barrier, strips - 1)

    def near(k):
        strip = lax.rem(t + k, strips)
        return pltpu.make_async_remote_copy(
            src_ref=slab.at[pl.ds(2 * strip, 3)],
            dst_ref=cube.at[plane],
            send_sem=send_sem.at[k],
            recv_sem=recv_sem.at[plane],
            device_id=(g, strip),
            device_id_type=MESH,
        )

    def far(k):
        strip = lax.rem(t + k, strips)
        return pltpu.make_async_remote_copy(
            src_ref=slab.at[pl.ds(2 * strip, 3)],
            dst_ref=cube.at[far_plane],
            send_sem=send_sem.at[strips + k],
            recv_sem=recv_sem.at[far_plane],
            device_id=(other, strip),
            device_id_type=MESH,
        )

    @pl.when(beyond)
    def _():
        @pl.loop(0, strips)
        def _(k):
            far(k).start()

    @pl.loop(1, strips)
    def _(k):
        near(k).start()

    pltpu.make_async_copy(slab.at[pl.ds(2 * t, 3)], cube.at[plane], recv_sem.at[plane]).start()

    for load in loads[1:]:
        load.wait()
    banded_weights(k1, k2, k3, stack1, base2, stack3, w1, w2, w3)
    for o in range(16):
        bias3[8 * o : 8 * o + 8, :] = jnp.full((8, 128), b3[o], F32)

    def arrived(p):
        pltpu.make_async_copy(cube.at[p], cube.at[p], recv_sem.at[p]).wait()

    def arrive(side):
        if side == "inner":
            @pl.loop(5, SPAN)
            def _(p):
                arrived(p)
        elif side == "upper":
            for p in (SPAN, SPAN + 1, SPAN + 2):
                arrived(p)

            @pl.when(g < groups - 1)
            def _():
                for p in (SPAN + 3, SPAN + 4):
                    arrived(p)

            @pl.when(g == groups - 1)
            def _():
                cube[SPAN + 3 : SPAN + 5] = jnp.zeros((2, 3, 8, 128), BF)
        else:
            for p in (3, 4):
                arrived(p)

            @pl.when(g > 0)
            def _():
                for p in range(3):
                    arrived(p)

            @pl.when(g == 0)
            def _():
                cube[0:3] = jnp.zeros((3, 3, 8, 128), BF)

    all_layers(
        (groups, strips, g, t), cube, arrive, b1, b2, bias3, x1, x2, l2, x3_upper, x3, w1, w2, w3, upper
    )

    @pl.loop(1, strips)
    def _(k):
        near(k).wait_send()

    @pl.when(beyond)
    def _():
        @pl.loop(0, strips)
        def _(k):
            far(k).wait_send()


X3_SHAPE = (5 * K3, 128)
HALF_SHAPE = (16, SPAN // 4, SPAN // 2, 64)
WEIGHT_SCRATCH = [
    pltpu.VMEM((128, 128), F32),
    pltpu.VMEM((8, 1408), F32),
    pltpu.VMEM((256, 128), F32),
    pltpu.VMEM((160, 256), BF),
    pltpu.VMEM((144, 1408), BF),
]
LAYER_SCRATCH = [
    pltpu.VMEM((PLANES * K1, 128), BF),
    pltpu.VMEM((F1 * K2, 128), BF),
    pltpu.VMEM((F2, 8 * Y2, 128), F32),
    pltpu.VMEM(X3_SHAPE, BF),
]


def first_layers(sky_cube, k1, k2, k3, b1, b2, b3):
    height = sky_cube.shape[1]
    strips = height // SPAN
    operands = [
        pltpu.with_memory_space_constraint(x, pltpu.HBM)
        for x in (sky_cube, k1, k2, k3, b1, b2, b3)
    ]
    vmem = pl.BlockSpec(memory_space=pltpu.VMEM)
    return pl.pallas_call(
        spread_kernel,
        out_shape=[
            jax.ShapeDtypeStruct(X3_SHAPE, BF),
            jax.ShapeDtypeStruct((128, 1280), BF),
            jax.ShapeDtypeStruct((128, 128), F32),
            jax.ShapeDtypeStruct(HALF_SHAPE, BF),
        ],
        in_specs=[pl.BlockSpec(memory_space=pltpu.HBM)] * len(operands),
        out_specs=[vmem] * 4,
        scratch_shapes=[
            pltpu.VMEM((height, 128), F32),
            pltpu.VMEM((height + 16, 128), F32),
            pltpu.VMEM(((height + 16) // 8, 8, 128), BF),
            pltpu.VMEM((PLANES, 3, 8, 128), BF),
            pltpu.VMEM(k1.shape, BF),
            pltpu.VMEM(k2.shape, BF),
            pltpu.VMEM(k3.shape, BF),
            pltpu.SMEM(b1.shape, F32),
            pltpu.SMEM(b2.shape, F32),
            pltpu.SMEM(b3.shape, F32),
            *WEIGHT_SCRATCH,
            *LAYER_SCRATCH,
            pltpu.SemaphoreType.DMA((len(operands),)),
            pltpu.SemaphoreType.DMA((2 * strips,)),
            pltpu.SemaphoreType.DMA((PLANES,)),
        ],
        compiler_params=pltpu.CompilerParams(
            collective_id=0, has_side_effects=True, vmem_limit_bytes=24 << 20
        ),
        name="first_layers",
    )(*operands)


def third_kernel(x3, w3, bias3, upper, out, lower, sem):
    quarter = SPAN // 4
    done = pltpu.make_async_copy(upper, out.at[:, quarter : 2 * quarter], sem.at[0])
    done.start()
    third_matmul(x3, 0, w3, bias3, lower)
    rest = pltpu.make_async_copy(lower, out.at[:, 0:quarter], sem.at[1])
    rest.start()
    done.wait()
    rest.wait()


def third_layer(x3, w3, bias3, upper):
    vmem = pl.BlockSpec(memory_space=pltpu.VMEM)
    half = SPAN // 2
    return pl.pallas_call(
        third_kernel,
        out_shape=jax.ShapeDtypeStruct((16, half, half, 64), BF),
        in_specs=[vmem] * 4,
        out_specs=pl.BlockSpec(memory_space=pl.ANY),
        scratch_shapes=[pltpu.VMEM(HALF_SHAPE, BF), pltpu.SemaphoreType.DMA((2,))],
        compiler_params=pltpu.CompilerParams(vmem_limit_bytes=8 << 20),
        name="third_layer",
    )(x3, w3, bias3, upper)


def body(sky_cube, kernel_one, bias_one, kernel_two, bias_two, kernel_three, bias_three):
    return third_layer(
        *first_layers(
            sky_cube,
            kernel_one.transpose(1, 2, 3, 4, 0),
            kernel_two.transpose(2, 3, 4, 0, 1),
            kernel_three.transpose(2, 3, 4, 1, 0),
            bias_one,
            bias_two,
            bias_three,
        )
    )


def solution(mesh):
    return jax.shard_map(
        body,
        mesh=mesh,
        in_specs=(P(("freq", "tile"), None, None), P(), P(), P(), P(), P(), P()),
        out_specs=P(None, "freq", "tile", None),
        check_vma=False,
    )
```

```python
import jax
import jax.numpy as jnp
from jax import lax
from jax.experimental import pallas as pl
from jax.experimental.pallas import tpu as pltpu
from jax.sharding import PartitionSpec as P

MESH = pl.DeviceIdType.MESH
BF = jnp.bfloat16
F32 = jnp.float32

SPAN = 16
PLANES = SPAN + 5
ROWS = 24
F1, Y1 = SPAN + 3, SPAN + 3
F2, Y2 = SPAN + 1, SPAN + 1
K1 = 80
K2 = 464
K3 = 416


def iota(shape, dim):
    return lax.broadcasted_iota(jnp.int32, shape, dim)


def leaky(values):
    return jnp.maximum(values, 0.1 * values)


def beside(values):
    lane = iota(values.shape, 1)
    swapped = pltpu.roll(values, 64, 1)
    before = jnp.where(lane < 64, pltpu.roll(values, 65, 1), swapped)
    after = jnp.where(lane < 64, swapped, pltpu.roll(values, 63, 1))
    return (
        jnp.where(lane == 0, 0.0, before),
        values,
        jnp.where(lane == 127, 0.0, after),
    )


def column_of(bias, rows, count):
    row = iota((count, 128), 0)
    block = jnp.zeros((count, 128), F32)
    for o in range(count):
        block = jnp.where(row == o, bias[o], block)
    return jnp.concatenate([block] * (rows // count), axis=0)


def taps():
    return [(a, b, c) for a in range(3) for b in range(3) for c in range(3)]


def one_if(inside):
    return jnp.where(inside, 1.0, 0.0).astype(F32)


def banded_weights(k1, k2, k3, stack1, base2, stack3, w1, w2, w3):
    stack1[...] = jnp.zeros(stack1.shape, F32)
    for a in range(3):
        for b in range(3):
            at = 8 * (3 * a + b)
            stack1[at : at + 3, 0:8] = k1[0, a, b].astype(F32)
    source = iota((128, 256), 0)
    tap, c = source >> 3, source & 7
    a = (tap * 21846) >> 16
    target = jnp.where((tap < 9) & (c < 3), a * K1 + c * ROWS + 1 + tap - 3 * a, -1)
    base = jnp.dot(
        stack1[...].T[0:8].astype(BF),
        (iota((128, 256), 1) == target).astype(F32).astype(BF),
        preferred_element_type=F32,
    )
    for y in range(0, Y1, 2):
        both = [pltpu.roll(base, s, 1) if s else base for s in (y, y + 1)]
        w1[8 * y : 8 * y + 16, :] = jnp.concatenate(both, axis=0).astype(BF)

    base2[...] = jnp.zeros(base2.shape, F32)
    for a, b, c in taps():
        at = a * K2 + c * (8 * Y1) + 8 * b
        base2[:, at : at + 8] = k2[a, b, c].astype(F32)
    base = base2[...]
    for y in range(0, Y2, 2):
        both = [pltpu.roll(base, 8 * s, 1) if s else base for s in (y, min(y + 1, Y2 - 1))]
        w2[8 * y : 8 * y + 16, :] = jnp.concatenate(both, axis=0).astype(BF)

    stack3[...] = jnp.zeros(stack3.shape, F32)
    for n, (a, b, c) in enumerate(taps()):
        stack3[8 * n : 8 * n + 8, 0:16] = k3[a, b, c].astype(F32)
    source = iota((256, 1280), 0)
    tap, i = source >> 3, source & 7
    a = (tap * 7282) >> 16
    rest = tap - 9 * a
    b = (rest * 21846) >> 16
    target = jnp.where(tap < 27, a * K3 + (rest - 3 * b) * (8 * Y2) + 8 * b + i, -1)
    base = jnp.dot(
        stack3[...].T[0:16].astype(BF),
        (iota((256, 1280), 1) == target).astype(F32).astype(BF),
        preferred_element_type=F32,
    )
    rows = [pltpu.roll(base, 16 * y, 1) if y else base for y in range(SPAN // 2)]
    by_row = jnp.concatenate(rows, axis=0).astype(BF)
    r = iota((128, 128), 0)
    swap = iota((128, 128), 1) == (r & 7) * 16 + (r >> 3)
    w3[...] = jnp.dot(
        swap.astype(F32).astype(BF), by_row, preferred_element_type=F32
    ).astype(BF)


def third_matmul(x3, first, w3, bias3, out):
    data = jnp.concatenate(
        [x3[h * K3 : (h + 3) * K3, :] for h in (first, first + 2)], axis=1
    )
    sums = jnp.dot(w3[:, 0 : 3 * K3], data, preferred_element_type=F32)
    for n in range(2):
        values = leaky(sums[:, 128 * n : 128 * (n + 1)] + bias3[...])
        out[:, n, :, :] = values[:, 0:64].reshape(16, 8, 64).astype(BF)
        swapped = pltpu.roll(values, 64, 1)
        out[:, n + 2, :, :] = swapped[:, 0:64].reshape(16, 8, 64).astype(BF)


def lower_last(g):
    return lax.rem(g, 4) == 0


def all_layers(place, cube, arrive, b1, b2, bias3, x1, x2, l2, x3_early, x3, w1, w2, w3, early):
    groups, strips, g, t = place
    first_g, last_g = one_if(g > 0), one_if(g < groups - 1)
    first_t, last_t = one_if(t > 0), one_if(t < strips - 1)

    def operand(f):
        pieces = beside(cube[f].reshape(ROWS, 128).astype(F32))
        block = jnp.concatenate([*pieces, jnp.zeros((K1 - 3 * ROWS, 128), F32)], axis=0)
        x1[f * K1 : (f + 1) * K1, :] = block.astype(BF)

    bias1 = column_of(b1, 8 * Y1, 8)
    row = iota((8 * Y1, 128), 0)
    keep1 = jnp.where(row < 16, first_t, jnp.where(row >= 8 * (Y1 - 1), last_t, 1.0))

    def layer_one(*fs):
        data = jnp.concatenate([x1[h * K1 : (h + 3) * K1, :] for h in fs], axis=1)
        sums = jnp.dot(w1[0 : 8 * Y1, 0 : 3 * K1], data, preferred_element_type=F32)
        for n, h in enumerate(fs):
            values = leaky(sums[:, 128 * n : 128 * (n + 1)] + bias1) * keep1
            if h < 2:
                values = values * first_g
            if h == F1 - 1:
                values = values * last_g
            block = jnp.concatenate(
                [*beside(values), jnp.zeros((K2 - 24 * Y1, 128), F32)], axis=0
            )
            x2[h * K2 : (h + 1) * K2, :] = block.astype(BF)

    bias2 = column_of(b2, 8 * Y2, 8)
    keep2 = jnp.where(iota((8 * Y2, 128), 0) < 8, first_t, 1.0)

    def layer_two(*fs):
        data = jnp.concatenate([x2[h * K2 : (h + 3) * K2, :] for h in fs], axis=1)
        sums = jnp.dot(w2[0 : 8 * Y2, 0 : 3 * K2], data, preferred_element_type=F32)
        for n, h in enumerate(fs):
            values = leaky(sums[:, 128 * n : 128 * (n + 1)] + bias2) * keep2
            if h == 0:
                values = values * first_g
            l2[h] = values

    lane = iota((8 * Y2, 128), 1)

    def joined(to, at, f):
        lower, upper = l2[f], l2[f + 4]
        before = jnp.where(lane < 64, pltpu.roll(lower, 65, 1), pltpu.roll(upper, 1, 1))
        block = jnp.concatenate(
            [
                jnp.where((lane & 63) == 0, 0.0, before),
                jnp.where(lane < 64, lower, pltpu.roll(upper, 64, 1)),
                jnp.where(lane < 64, pltpu.roll(lower, 64, 1), upper),
                jnp.zeros((K3 - 24 * Y2, 128), F32),
            ],
            axis=0,
        )
        to[at * K3 : (at + 1) * K3, :] = block.astype(BF)

    def lower_side(to):
        arrive("lower near")
        operand(3)
        operand(4)
        layer_one(3, 4)
        layer_two(3, 4)
        joined(to, 3, 3)
        joined(to, 4, 4)
        arrive("lower far")
        for f in range(3):
            operand(f)
        layer_one(1, 2)
        layer_one(0)
        layer_two(1, 2)
        layer_two(0)
        for n in range(3):
            joined(to, n, n)

    def upper_side(to):
        arrive("upper near")
        for f in (SPAN, SPAN + 1, SPAN + 2):
            operand(f)
        layer_one(13, 14)
        layer_one(15, 16)
        layer_two(11, 12)
        layer_two(13, 14)
        for n in range(3):
            joined(to, n, 8 + n)
        arrive("upper far")
        operand(SPAN + 3)
        operand(SPAN + 4)
        layer_one(17, 18)
        layer_two(15, 16)
        joined(to, 3, 11)
        joined(to, 4, 12)

    arrive("inner")
    for f in range(5, SPAN):
        operand(f)
    for f in (5, 7, 9, 11):
        layer_one(f, f + 1)
    for f in (5, 7, 9):
        layer_two(f, f + 1)

    @pl.when(lower_last(g))
    def _():
        upper_side(x3_early)
        third_matmul(x3_early, 0, w3, bias3, early)
        lower_side(x3)

    @pl.when(jnp.logical_not(lower_last(g)))
    def _():
        lower_side(x3_early)
        third_matmul(x3_early, 0, w3, bias3, early)
        upper_side(x3)


def spread_kernel(
    sky, k1_in, k2_in, k3_in, b1_in, b2_in, b3_in,
    x3, w3, bias3, early,
    raw, moved, slab, cube, k1, k2, k3, b1, b2, b3, stack1, base2, stack3, w1, w2, x1, x2, l2, x3_early,
    in_sem, send_sem, recv_sem,
):
    groups, strips = lax.axis_size("freq"), lax.axis_size("tile")
    g, t = lax.axis_index("freq"), lax.axis_index("tile")
    height = raw.shape[0]

    pairs = [(sky.at[0], raw), (k1_in, k1), (k2_in, k2), (k3_in, k3), (b1_in, b1), (b2_in, b2), (b3_in, b3)]
    loads = [pltpu.make_async_copy(a, b, in_sem.at[n]) for n, (a, b) in enumerate(pairs)]
    loads[0].start()
    barrier = pltpu.get_barrier_semaphore()

    def greet(group, strip):
        pl.semaphore_signal(barrier, inc=1, device_id=(group, strip), device_id_type=MESH)

    @pl.when(g < groups - 1)
    def _():
        for strip in (0, 1):
            greet(g + 1, strip)

    @pl.when(g > 0)
    def _():
        for strip in (strips - 3, strips - 2, strips - 1):
            greet(g - 1, strip)

    @pl.loop(1, strips)
    def _(k):
        greet(g, lax.rem(t + k, strips))

    for load in loads[1:]:
        load.start()

    lane = iota((128, 128), 1)
    column = jnp.where(lane < 64, 2 * lane, 2 * lane - 127)
    order = (iota((128, 128), 0) == column).astype(F32).astype(BF)
    moved[0:8, :] = jnp.zeros((8, 128), F32)
    moved[height : height + 16, :] = jnp.zeros((16, 128), F32)
    loads[0].wait()
    values = jnp.dot(raw[...].astype(BF), order, preferred_element_type=F32)
    moved[4 : height + 4, :] = values
    slab[...] = moved[...].reshape(slab.shape).astype(BF)

    high = t >= strips - 3
    low = t < 2
    beyond = jnp.logical_or(jnp.logical_and(low, g > 0), jnp.logical_and(high, g < groups - 1))
    other = jnp.where(low, jnp.maximum(g - 1, 0), jnp.minimum(g + 1, groups - 1))
    plane = 3 + t
    far_plane = jnp.where(low, SPAN + 3 + t, jnp.maximum(t - (strips - 3), 0))

    @pl.when(beyond)
    def _():
        pl.semaphore_wait(barrier, 2 * strips - 1)

    @pl.when(jnp.logical_not(beyond))
    def _():
        pl.semaphore_wait(barrier, strips - 1)

    def near(k):
        strip = lax.rem(t + k, strips)
        return pltpu.make_async_remote_copy(
            src_ref=slab.at[pl.ds(2 * strip, 3)],
            dst_ref=cube.at[plane],
            send_sem=send_sem.at[k],
            recv_sem=recv_sem.at[plane],
            device_id=(g, strip),
            device_id_type=MESH,
        )

    def far(k):
        pair = k // 2
        strip = lax.rem(pair, 2) * (strips // 2) + pair // 2 * 2 + lax.rem(k, 2)
        return pltpu.make_async_remote_copy(
            src_ref=slab.at[pl.ds(2 * strip, 3)],
            dst_ref=cube.at[far_plane],
            send_sem=send_sem.at[strips + k],
            recv_sem=recv_sem.at[far_plane],
            device_id=(other, strip),
            device_id_type=MESH,
        )

    @pl.when(beyond)
    def _():
        @pl.loop(0, strips)
        def _(k):
            far(k).start()

    @pl.loop(1, strips)
    def _(k):
        near(k).start()

    pltpu.make_async_copy(slab.at[pl.ds(2 * t, 3)], cube.at[plane], recv_sem.at[plane]).start()

    for load in loads[1:]:
        load.wait()
    banded_weights(k1, k2, k3, stack1, base2, stack3, w1, w2, w3)
    for o in range(16):
        bias3[8 * o : 8 * o + 8, :] = jnp.full((8, 128), b3[o], F32)

    def arrived(p):
        pltpu.make_async_copy(cube.at[p], cube.at[p], recv_sem.at[p]).wait()

    def arrive(side):
        if side == "inner":
            @pl.loop(5, SPAN)
            def _(p):
                arrived(p)
        elif side == "upper near":
            for p in (SPAN, SPAN + 1, SPAN + 2):
                arrived(p)
        elif side == "lower near":
            for p in (3, 4):
                arrived(p)
        elif side == "upper far":
            @pl.when(g < groups - 1)
            def _():
                for p in (SPAN + 3, SPAN + 4):
                    arrived(p)

            @pl.when(g == groups - 1)
            def _():
                cube[SPAN + 3 : SPAN + 5] = jnp.zeros((2, 3, 8, 128), BF)
        else:
            @pl.when(g > 0)
            def _():
                for p in range(3):
                    arrived(p)

            @pl.when(g == 0)
            def _():
                cube[0:3] = jnp.zeros((3, 3, 8, 128), BF)

    all_layers(
        (groups, strips, g, t), cube, arrive, b1, b2, bias3, x1, x2, l2, x3_early, x3, w1, w2, w3, early
    )

    @pl.loop(1, strips)
    def _(k):
        near(k).wait_send()

    @pl.when(beyond)
    def _():
        @pl.loop(0, strips)
        def _(k):
            far(k).wait_send()


X3_SHAPE = (5 * K3, 128)
HALF_SHAPE = (16, SPAN // 4, SPAN // 2, 64)
WEIGHT_SCRATCH = [
    pltpu.VMEM((128, 128), F32),
    pltpu.VMEM((8, 1408), F32),
    pltpu.VMEM((256, 128), F32),
    pltpu.VMEM((160, 256), BF),
    pltpu.VMEM((144, 1408), BF),
]
LAYER_SCRATCH = [
    pltpu.VMEM((PLANES * K1, 128), BF),
    pltpu.VMEM((F1 * K2, 128), BF),
    pltpu.VMEM((F2, 8 * Y2, 128), F32),
    pltpu.VMEM(X3_SHAPE, BF),
]


def first_layers(sky_cube, k1, k2, k3, b1, b2, b3):
    height = sky_cube.shape[1]
    strips = height // SPAN
    operands = [
        pltpu.with_memory_space_constraint(x, pltpu.HBM)
        for x in (sky_cube, k1, k2, k3, b1, b2, b3)
    ]
    vmem = pl.BlockSpec(memory_space=pltpu.VMEM)
    return pl.pallas_call(
        spread_kernel,
        out_shape=[
            jax.ShapeDtypeStruct(X3_SHAPE, BF),
            jax.ShapeDtypeStruct((128, 1280), BF),
            jax.ShapeDtypeStruct((128, 128), F32),
            jax.ShapeDtypeStruct(HALF_SHAPE, BF),
        ],
        in_specs=[pl.BlockSpec(memory_space=pltpu.HBM)] * len(operands),
        out_specs=[vmem] * 4,
        scratch_shapes=[
            pltpu.VMEM((height, 128), F32),
            pltpu.VMEM((height + 16, 128), F32),
            pltpu.VMEM(((height + 16) // 8, 8, 128), BF),
            pltpu.VMEM((PLANES, 3, 8, 128), BF),
            pltpu.VMEM(k1.shape, BF),
            pltpu.VMEM(k2.shape, BF),
            pltpu.VMEM(k3.shape, BF),
            pltpu.SMEM(b1.shape, F32),
            pltpu.SMEM(b2.shape, F32),
            pltpu.SMEM(b3.shape, F32),
            *WEIGHT_SCRATCH,
            *LAYER_SCRATCH,
            pltpu.SemaphoreType.DMA((len(operands),)),
            pltpu.SemaphoreType.DMA((2 * strips,)),
            pltpu.SemaphoreType.DMA((PLANES,)),
        ],
        compiler_params=pltpu.CompilerParams(
            collective_id=0, has_side_effects=True, vmem_limit_bytes=24 << 20
        ),
        name="first_layers",
    )(*operands)


def third_kernel(x3, w3, bias3, early, out, late, sem):
    quarter = SPAN // 4
    lower_is_late = lower_last(lax.axis_index("freq"))
    early_at = jnp.where(lower_is_late, quarter, 0)
    done = pltpu.make_async_copy(early, out.at[:, pl.ds(early_at, quarter)], sem.at[0])
    done.start()
    third_matmul(x3, 0, w3, bias3, late)
    rest = pltpu.make_async_copy(late, out.at[:, pl.ds(quarter - early_at, quarter)], sem.at[1])
    rest.start()
    done.wait()
    rest.wait()


def third_layer(x3, w3, bias3, early):
    vmem = pl.BlockSpec(memory_space=pltpu.VMEM)
    half = SPAN // 2
    return pl.pallas_call(
        third_kernel,
        out_shape=jax.ShapeDtypeStruct((16, half, half, 64), BF),
        in_specs=[vmem] * 4,
        out_specs=pl.BlockSpec(memory_space=pl.ANY),
        scratch_shapes=[pltpu.VMEM(HALF_SHAPE, BF), pltpu.SemaphoreType.DMA((2,))],
        compiler_params=pltpu.CompilerParams(vmem_limit_bytes=8 << 20),
        name="third_layer",
    )(x3, w3, bias3, early)


def body(sky_cube, kernel_one, bias_one, kernel_two, bias_two, kernel_three, bias_three):
    return third_layer(
        *first_layers(
            sky_cube,
            kernel_one.transpose(1, 2, 3, 4, 0),
            kernel_two.transpose(2, 3, 4, 0, 1),
            kernel_three.transpose(2, 3, 4, 1, 0),
            bias_one,
            bias_two,
            bias_three,
        )
    )


def solution(mesh):
    return jax.shard_map(
        body,
        mesh=mesh,
        in_specs=(P(("freq", "tile"), None, None), P(), P(), P(), P(), P(), P()),
        out_specs=P(None, "freq", "tile", None),
        check_vma=False,
    )
```

```python
import jax
import jax.numpy as jnp
from jax import lax
from jax.experimental import pallas as pl
from jax.experimental.pallas import tpu as pltpu
from jax.sharding import PartitionSpec as P

MESH = pl.DeviceIdType.MESH
BF = jnp.bfloat16
F32 = jnp.float32

SPAN = 16
PLANES = SPAN + 5
ROWS = 24
F1, Y1 = SPAN + 3, SPAN + 3
F2, Y2 = SPAN + 1, SPAN + 1
K1 = 80
K2 = 464
K3 = 416


def iota(shape, dim):
    return lax.broadcasted_iota(jnp.int32, shape, dim)


def leaky(values):
    return jnp.maximum(values, 0.1 * values)


def beside(values):
    lane = iota(values.shape, 1)
    swapped = pltpu.roll(values, 64, 1)
    before = jnp.where(lane < 64, pltpu.roll(values, 65, 1), swapped)
    after = jnp.where(lane < 64, swapped, pltpu.roll(values, 63, 1))
    return (
        jnp.where(lane == 0, 0.0, before),
        values,
        jnp.where(lane == 127, 0.0, after),
    )


def column_of(bias, rows, count):
    row = iota((count, 128), 0)
    block = jnp.zeros((count, 128), F32)
    for o in range(count):
        block = jnp.where(row == o, bias[o], block)
    return jnp.concatenate([block] * (rows // count), axis=0)


def taps():
    return [(a, b, c) for a in range(3) for b in range(3) for c in range(3)]


def one_if(inside):
    return jnp.where(inside, 1.0, 0.0).astype(F32)


def banded_weights(k1, k2, k3, stack1, base2, stack3, w1, w2, w3):
    stack1[...] = jnp.zeros(stack1.shape, F32)
    for a in range(3):
        for b in range(3):
            at = 8 * (3 * a + b)
            stack1[at : at + 3, 0:8] = k1[0, a, b].astype(F32)
    source = iota((128, 256), 0)
    tap, c = source >> 3, source & 7
    a = (tap * 21846) >> 16
    target = jnp.where((tap < 9) & (c < 3), a * K1 + c * ROWS + 1 + tap - 3 * a, -1)
    base = jnp.dot(
        stack1[...].T[0:8].astype(BF),
        (iota((128, 256), 1) == target).astype(F32).astype(BF),
        preferred_element_type=F32,
    )
    for y in range(0, Y1, 2):
        both = [pltpu.roll(base, s, 1) if s else base for s in (y, y + 1)]
        w1[8 * y : 8 * y + 16, :] = jnp.concatenate(both, axis=0).astype(BF)

    base2[...] = jnp.zeros(base2.shape, F32)
    for a, b, c in taps():
        at = a * K2 + c * (8 * Y1) + 8 * b
        base2[:, at : at + 8] = k2[a, b, c].astype(F32)
    base = base2[...]
    for y in range(0, Y2, 2):
        both = [pltpu.roll(base, 8 * s, 1) if s else base for s in (y, min(y + 1, Y2 - 1))]
        w2[8 * y : 8 * y + 16, :] = jnp.concatenate(both, axis=0).astype(BF)

    stack3[...] = jnp.zeros(stack3.shape, F32)
    for n, (a, b, c) in enumerate(taps()):
        stack3[8 * n : 8 * n + 8, 0:16] = k3[a, b, c].astype(F32)
    source = iota((256, 1280), 0)
    tap, i = source >> 3, source & 7
    a = (tap * 7282) >> 16
    rest = tap - 9 * a
    b = (rest * 21846) >> 16
    target = jnp.where(tap < 27, a * K3 + (rest - 3 * b) * (8 * Y2) + 8 * b + i, -1)
    base = jnp.dot(
        stack3[...].T[0:16].astype(BF),
        (iota((256, 1280), 1) == target).astype(F32).astype(BF),
        preferred_element_type=F32,
    )
    rows = [pltpu.roll(base, 16 * y, 1) if y else base for y in range(SPAN // 2)]
    by_row = jnp.concatenate(rows, axis=0).astype(BF)
    r = iota((128, 128), 0)
    swap = iota((128, 128), 1) == (r & 7) * 16 + (r >> 3)
    w3[...] = jnp.dot(
        swap.astype(F32).astype(BF), by_row, preferred_element_type=F32
    ).astype(BF)


def third_matmul(x3, start, w3, bias3, out):
    data = jnp.concatenate(
        [x3[start + h * K3 : start + (h + 3) * K3, :] for h in (0, 2)], axis=1
    )
    sums = jnp.dot(w3[:, 0 : 3 * K3], data, preferred_element_type=F32)
    for n in range(2):
        values = leaky(sums[:, 128 * n : 128 * (n + 1)] + bias3[...])
        out[:, n, :, :] = values[:, 0:64].reshape(16, 8, 64).astype(BF)
        swapped = pltpu.roll(values, 64, 1)
        out[:, n + 2, :, :] = swapped[:, 0:64].reshape(16, 8, 64).astype(BF)


def lower_last(g):
    return lax.rem(g, 4) == 0


def rows_at(index, block, count):
    return pl.ds(pl.multiple_of(index * block, 16), count)


def all_layers(place, cube, ready, b1, b2, bias3, x1, x2, l2, x3, w1, w2, w3, early):
    groups, strips, g, t = place
    first_g, last_g = one_if(g > 0), one_if(g < groups - 1)
    first_t, last_t = one_if(t > 0), one_if(t < strips - 1)
    low_last = lower_last(g)

    def operand(f):
        pieces = beside(cube[f].reshape(ROWS, 128).astype(F32))
        block = jnp.concatenate([*pieces, jnp.zeros((K1 - 3 * ROWS, 128), F32)], axis=0)
        x1[rows_at(f, K1, K1), :] = block.astype(BF)

    bias1 = column_of(b1, 8 * Y1, 8)
    row = iota((8 * Y1, 128), 0)
    keep1 = jnp.where(row < 16, first_t, jnp.where(row >= 8 * (Y1 - 1), last_t, 1.0))
    bias2 = column_of(b2, 8 * Y2, 8)
    keep2 = jnp.where(iota((8 * Y2, 128), 0) < 8, first_t, 1.0)

    def layer_one(f):
        data = jnp.concatenate([x1[rows_at(h, K1, 3 * K1), :] for h in (f, f + 1)], axis=1)
        sums = jnp.dot(w1[0 : 8 * Y1, 0 : 3 * K1], data, preferred_element_type=F32)
        for n in range(2):
            h = f + n
            inside = jnp.where(h < 2, first_g, jnp.where(h == F1 - 1, last_g, 1.0))
            values = leaky(sums[:, 128 * n : 128 * (n + 1)] + bias1) * (keep1 * inside)
            block = jnp.concatenate(
                [*beside(values), jnp.zeros((K2 - 24 * Y1, 128), F32)], axis=0
            )
            x2[rows_at(h, K2, K2), :] = block.astype(BF)

    def layer_two(f):
        data = jnp.concatenate([x2[rows_at(h, K2, 3 * K2), :] for h in (f, f + 1)], axis=1)
        sums = jnp.dot(w2[0 : 8 * Y2, 0 : 3 * K2], data, preferred_element_type=F32)
        for n in range(2):
            inside = jnp.where(f + n == 0, first_g, 1.0)
            values = leaky(sums[:, 128 * n : 128 * (n + 1)] + bias2) * (keep2 * inside)
            l2[f + n] = values

    lane = iota((8 * Y2, 128), 1)

    def joined(at, f):
        lower, upper = l2[f], l2[f + 4]
        before = jnp.where(lane < 64, pltpu.roll(lower, 65, 1), pltpu.roll(upper, 1, 1))
        block = jnp.concatenate(
            [
                jnp.where((lane & 63) == 0, 0.0, before),
                jnp.where(lane < 64, lower, pltpu.roll(upper, 64, 1)),
                jnp.where(lane < 64, pltpu.roll(lower, 64, 1), upper),
                jnp.zeros((K3 - 24 * Y2, 128), F32),
            ],
            axis=0,
        )
        x3[rows_at(at, K3, K3), :] = block.astype(BF)

    for p in (5, 6):
        ready(p)
        operand(p)

    lower_from = jnp.where(low_last, 7, 4)

    @pl.loop(0, 2)
    def _(half):
        @pl.loop(7 * half, 7 + 3 * half)
        def _(step):
            low = jnp.logical_and(step >= lower_from, step < lower_from + 3)
            f_low = jnp.maximum(3 - 2 * (step - lower_from), 0)
            f_up = 5 + 2 * jnp.where(step < lower_from, step, step - 3)
            f = jnp.where(low, f_low, f_up)
            new = jnp.where(low, f_low, f_up + 2)
            ready(new)

            @pl.when(new > 0)
            def _():
                ready(new + 1)

            operand(new)
            operand(new + 1)
            layer_one(f)

            @pl.when(step > 0)
            def _():
                layer_two(jnp.where(low, f_low, f_up - 2))

        base = jnp.where(low_last, 8 - 8 * half, 8 * half)

        @pl.loop(0, 5)
        def _(n):
            joined(5 * half + n, base + n)

        @pl.when(half == 0)
        def _():
            third_matmul(x3, 0, w3, bias3, early)


def spread_kernel(
    sky, k1_in, k2_in, k3_in, b1_in, b2_in, b3_in,
    x3, w3, bias3, early,
    raw, moved, slab, cube, k1, k2, k3, b1, b2, b3, stack1, base2, stack3, w1, w2, x1, x2, l2,
    in_sem, send_sem, recv_sem,
):
    groups, strips = lax.axis_size("freq"), lax.axis_size("tile")
    g, t = lax.axis_index("freq"), lax.axis_index("tile")
    height = raw.shape[0]

    pairs = [(sky.at[0], raw), (k1_in, k1), (k2_in, k2), (k3_in, k3), (b1_in, b1), (b2_in, b2), (b3_in, b3)]
    loads = [pltpu.make_async_copy(a, b, in_sem.at[n]) for n, (a, b) in enumerate(pairs)]
    loads[0].start()
    barrier = pltpu.get_barrier_semaphore()

    def greet(group, strip):
        pl.semaphore_signal(barrier, inc=1, device_id=(group, strip), device_id_type=MESH)

    @pl.when(g < groups - 1)
    def _():
        for strip in (0, 1):
            greet(g + 1, strip)

    @pl.when(g > 0)
    def _():
        for strip in (strips - 3, strips - 2, strips - 1):
            greet(g - 1, strip)

    @pl.loop(1, strips)
    def _(k):
        greet(g, lax.rem(t + k, strips))

    for load in loads[1:]:
        load.start()

    lane = iota((128, 128), 1)
    column = jnp.where(lane < 64, 2 * lane, 2 * lane - 127)
    order = (iota((128, 128), 0) == column).astype(F32).astype(BF)
    moved[0:8, :] = jnp.zeros((8, 128), F32)
    moved[height : height + 16, :] = jnp.zeros((16, 128), F32)
    loads[0].wait()
    values = jnp.dot(raw[...].astype(BF), order, preferred_element_type=F32)
    moved[4 : height + 4, :] = values
    slab[...] = moved[...].reshape(slab.shape).astype(BF)

    high = t >= strips - 3
    low = t < 2
    beyond = jnp.logical_or(jnp.logical_and(low, g > 0), jnp.logical_and(high, g < groups - 1))
    other = jnp.where(low, jnp.maximum(g - 1, 0), jnp.minimum(g + 1, groups - 1))
    plane = 3 + t
    far_plane = jnp.where(low, SPAN + 3 + t, jnp.maximum(t - (strips - 3), 0))

    @pl.when(beyond)
    def _():
        pl.semaphore_wait(barrier, 2 * strips - 1)

    @pl.when(jnp.logical_not(beyond))
    def _():
        pl.semaphore_wait(barrier, strips - 1)

    def near(k):
        strip = lax.rem(t + k, strips)
        return pltpu.make_async_remote_copy(
            src_ref=slab.at[pl.ds(2 * strip, 3)],
            dst_ref=cube.at[plane],
            send_sem=send_sem.at[k],
            recv_sem=recv_sem.at[plane],
            device_id=(g, strip),
            device_id_type=MESH,
        )

    def far(k):
        pair = k // 2
        strip = lax.rem(pair, 2) * (strips // 2) + pair // 2 * 2 + lax.rem(k, 2)
        return pltpu.make_async_remote_copy(
            src_ref=slab.at[pl.ds(2 * strip, 3)],
            dst_ref=cube.at[far_plane],
            send_sem=send_sem.at[strips + k],
            recv_sem=recv_sem.at[far_plane],
            device_id=(other, strip),
            device_id_type=MESH,
        )

    @pl.when(beyond)
    def _():
        @pl.loop(0, strips)
        def _(k):
            far(k).start()

    @pl.loop(1, strips)
    def _(k):
        near(k).start()

    pltpu.make_async_copy(slab.at[pl.ds(2 * t, 3)], cube.at[plane], recv_sem.at[plane]).start()

    for load in loads[1:]:
        load.wait()
    banded_weights(k1, k2, k3, stack1, base2, stack3, w1, w2, w3)
    for o in range(16):
        bias3[8 * o : 8 * o + 8, :] = jnp.full((8, 128), b3[o], F32)

    def arrived(p):
        pltpu.make_async_copy(cube.at[p], cube.at[p], recv_sem.at[p]).wait()

    def ready(p):
        missing = jnp.logical_or(
            jnp.logical_and(p < 3, g == 0),
            jnp.logical_and(p >= SPAN + 3, g == groups - 1),
        )

        @pl.when(missing)
        def _():
            cube[p] = jnp.zeros((3, 8, 128), BF)

        @pl.when(jnp.logical_not(missing))
        def _():
            arrived(p)

    all_layers(
        (groups, strips, g, t), cube, ready, b1, b2, bias3, x1, x2, l2, x3, w1, w2, w3, early
    )

    @pl.loop(1, strips)
    def _(k):
        near(k).wait_send()

    @pl.when(beyond)
    def _():
        @pl.loop(0, strips)
        def _(k):
            far(k).wait_send()


X3_SHAPE = (10 * K3, 128)
HALF_SHAPE = (16, SPAN // 4, SPAN // 2, 64)
WEIGHT_SCRATCH = [
    pltpu.VMEM((128, 128), F32),
    pltpu.VMEM((8, 1408), F32),
    pltpu.VMEM((256, 128), F32),
    pltpu.VMEM((160, 256), BF),
    pltpu.VMEM((144, 1408), BF),
]
LAYER_SCRATCH = [
    pltpu.VMEM((PLANES * K1, 128), BF),
    pltpu.VMEM((F1 * K2, 128), BF),
    pltpu.VMEM((F2, 8 * Y2, 128), F32),
]


def first_layers(sky_cube, k1, k2, k3, b1, b2, b3):
    height = sky_cube.shape[1]
    strips = height // SPAN
    operands = [
        pltpu.with_memory_space_constraint(x, pltpu.HBM)
        for x in (sky_cube, k1, k2, k3, b1, b2, b3)
    ]
    vmem = pl.BlockSpec(memory_space=pltpu.VMEM)
    return pl.pallas_call(
        spread_kernel,
        out_shape=[
            jax.ShapeDtypeStruct(X3_SHAPE, BF),
            jax.ShapeDtypeStruct((128, 1280), BF),
            jax.ShapeDtypeStruct((128, 128), F32),
            jax.ShapeDtypeStruct(HALF_SHAPE, BF),
        ],
        in_specs=[pl.BlockSpec(memory_space=pltpu.HBM)] * len(operands),
        out_specs=[vmem] * 4,
        scratch_shapes=[
            pltpu.VMEM((height, 128), F32),
            pltpu.VMEM((height + 16, 128), F32),
            pltpu.VMEM(((height + 16) // 8, 8, 128), BF),
            pltpu.VMEM((PLANES, 3, 8, 128), BF),
            pltpu.VMEM(k1.shape, BF),
            pltpu.VMEM(k2.shape, BF),
            pltpu.VMEM(k3.shape, BF),
            pltpu.SMEM(b1.shape, F32),
            pltpu.SMEM(b2.shape, F32),
            pltpu.SMEM(b3.shape, F32),
            *WEIGHT_SCRATCH,
            *LAYER_SCRATCH,
            pltpu.SemaphoreType.DMA((len(operands),)),
            pltpu.SemaphoreType.DMA((2 * strips,)),
            pltpu.SemaphoreType.DMA((PLANES,)),
        ],
        compiler_params=pltpu.CompilerParams(
            collective_id=0, has_side_effects=True, vmem_limit_bytes=24 << 20
        ),
        name="first_layers",
    )(*operands)


def third_kernel(x3, w3, bias3, early, out, late, sem):
    quarter = SPAN // 4
    lower_is_late = lower_last(lax.axis_index("freq"))
    early_at = jnp.where(lower_is_late, quarter, 0)
    done = pltpu.make_async_copy(early, out.at[:, pl.ds(early_at, quarter)], sem.at[0])
    done.start()
    third_matmul(x3, 5 * K3, w3, bias3, late)
    rest = pltpu.make_async_copy(late, out.at[:, pl.ds(quarter - early_at, quarter)], sem.at[1])
    rest.start()
    done.wait()
    rest.wait()


def third_layer(x3, w3, bias3, early):
    vmem = pl.BlockSpec(memory_space=pltpu.VMEM)
    half = SPAN // 2
    return pl.pallas_call(
        third_kernel,
        out_shape=jax.ShapeDtypeStruct((16, half, half, 64), BF),
        in_specs=[vmem] * 4,
        out_specs=pl.BlockSpec(memory_space=pl.ANY),
        scratch_shapes=[pltpu.VMEM(HALF_SHAPE, BF), pltpu.SemaphoreType.DMA((2,))],
        compiler_params=pltpu.CompilerParams(vmem_limit_bytes=8 << 20),
        name="third_layer",
    )(x3, w3, bias3, early)


def body(sky_cube, kernel_one, bias_one, kernel_two, bias_two, kernel_three, bias_three):
    return third_layer(
        *first_layers(
            sky_cube,
            kernel_one.transpose(1, 2, 3, 4, 0),
            kernel_two.transpose(2, 3, 4, 0, 1),
            kernel_three.transpose(2, 3, 4, 1, 0),
            bias_one,
            bias_two,
            bias_three,
        )
    )


def solution(mesh):
    return jax.shard_map(
        body,
        mesh=mesh,
        in_specs=(P(("freq", "tile"), None, None), P(), P(), P(), P(), P(), P()),
        out_specs=P(None, "freq", "tile", None),
        check_vma=False,
    )
```

```python
import jax
import jax.numpy as jnp
from jax import lax
from jax.experimental import pallas as pl
from jax.experimental.pallas import tpu as pltpu
from jax.sharding import PartitionSpec as P

MESH = pl.DeviceIdType.MESH
BF = jnp.bfloat16
F32 = jnp.float32

SPAN = 16
PLANES = SPAN + 5
ROWS = 24
F1, Y1 = SPAN + 3, SPAN + 3
F2, Y2 = SPAN + 1, SPAN + 1
K1 = 80
K2 = 464
K3 = 416


def iota(shape, dim):
    return lax.broadcasted_iota(jnp.int32, shape, dim)


def leaky(values):
    return jnp.maximum(values, 0.1 * values)


def beside(values):
    lane = iota(values.shape, 1)
    swapped = pltpu.roll(values, 64, 1)
    before = jnp.where(lane < 64, pltpu.roll(values, 65, 1), swapped)
    after = jnp.where(lane < 64, swapped, pltpu.roll(values, 63, 1))
    return (
        jnp.where(lane == 0, 0.0, before),
        values,
        jnp.where(lane == 127, 0.0, after),
    )


def column_of(bias, rows, count):
    row = iota((count, 128), 0)
    block = jnp.zeros((count, 128), F32)
    for o in range(count):
        block = jnp.where(row == o, bias[o], block)
    return jnp.concatenate([block] * (rows // count), axis=0)


def taps():
    return [(a, b, c) for a in range(3) for b in range(3) for c in range(3)]


def one_if(inside):
    return jnp.where(inside, 1.0, 0.0).astype(F32)


def banded_weights(k1, k2, k3, stack1, base2, stack3, w1, w2, w3):
    stack1[...] = jnp.zeros(stack1.shape, F32)
    for a in range(3):
        for b in range(3):
            at = 8 * (3 * a + b)
            stack1[at : at + 3, 0:8] = k1[0, a, b].astype(F32)
    source = iota((128, 256), 0)
    tap, c = source >> 3, source & 7
    a = (tap * 21846) >> 16
    target = jnp.where((tap < 9) & (c < 3), a * K1 + c * ROWS + 1 + tap - 3 * a, -1)
    base = jnp.dot(
        stack1[...].T[0:8].astype(BF),
        (iota((128, 256), 1) == target).astype(F32).astype(BF),
        preferred_element_type=F32,
    )
    for y in range(0, Y1, 2):
        both = [pltpu.roll(base, s, 1) if s else base for s in (y, y + 1)]
        w1[8 * y : 8 * y + 16, :] = jnp.concatenate(both, axis=0).astype(BF)

    base2[...] = jnp.zeros(base2.shape, F32)
    for a, b, c in taps():
        at = a * K2 + c * (8 * Y1) + 8 * b
        base2[:, at : at + 8] = k2[a, b, c].astype(F32)
    base = base2[...]
    for y in range(0, Y2, 2):
        both = [pltpu.roll(base, 8 * s, 1) if s else base for s in (y, min(y + 1, Y2 - 1))]
        w2[8 * y : 8 * y + 16, :] = jnp.concatenate(both, axis=0).astype(BF)

    stack3[...] = jnp.zeros(stack3.shape, F32)
    for n, (a, b, c) in enumerate(taps()):
        stack3[8 * n : 8 * n + 8, 0:16] = k3[a, b, c].astype(F32)
    source = iota((256, 1280), 0)
    tap, i = source >> 3, source & 7
    a = (tap * 7282) >> 16
    rest = tap - 9 * a
    b = (rest * 21846) >> 16
    target = jnp.where(tap < 27, a * K3 + (rest - 3 * b) * (8 * Y2) + 8 * b + i, -1)
    base = jnp.dot(
        stack3[...].T[0:16].astype(BF),
        (iota((256, 1280), 1) == target).astype(F32).astype(BF),
        preferred_element_type=F32,
    )
    rows = [pltpu.roll(base, 16 * y, 1) if y else base for y in range(SPAN // 2)]
    by_row = jnp.concatenate(rows, axis=0).astype(BF)
    r = iota((128, 128), 0)
    swap = iota((128, 128), 1) == (r & 7) * 16 + (r >> 3)
    w3[...] = jnp.dot(
        swap.astype(F32).astype(BF), by_row, preferred_element_type=F32
    ).astype(BF)


def third_matmul(x3, first, w3, bias3, out):
    data = jnp.concatenate(
        [x3[h * K3 : (h + 3) * K3, :] for h in (first, first + 2)], axis=1
    )
    sums = jnp.dot(w3[:, 0 : 3 * K3], data, preferred_element_type=F32)
    for n in range(2):
        values = leaky(sums[:, 128 * n : 128 * (n + 1)] + bias3[...])
        out[:, n, :, :] = values[:, 0:64].reshape(16, 8, 64).astype(BF)
        swapped = pltpu.roll(values, 64, 1)
        out[:, n + 2, :, :] = swapped[:, 0:64].reshape(16, 8, 64).astype(BF)


def layer_steps(place, cube, arrive, b1, b2, bias3, x1, x2, l2, x3_upper, x3, w1, w2, w3, upper):
    groups, strips, g, t = place
    first_g, last_g = one_if(g > 0), one_if(g < groups - 1)
    first_t, last_t = one_if(t > 0), one_if(t < strips - 1)

    def operand(f):
        pieces = beside(cube[f].reshape(ROWS, 128).astype(F32))
        block = jnp.concatenate([*pieces, jnp.zeros((K1 - 3 * ROWS, 128), F32)], axis=0)
        x1[f * K1 : (f + 1) * K1, :] = block.astype(BF)

    bias1 = column_of(b1, 8 * Y1, 8)
    row = iota((8 * Y1, 128), 0)
    keep1 = jnp.where(row < 16, first_t, jnp.where(row >= 8 * (Y1 - 1), last_t, 1.0))

    def layer_one(*fs):
        data = jnp.concatenate([x1[h * K1 : (h + 3) * K1, :] for h in fs], axis=1)
        sums = jnp.dot(w1[0 : 8 * Y1, 0 : 3 * K1], data, preferred_element_type=F32)
        for n, h in enumerate(fs):
            values = leaky(sums[:, 128 * n : 128 * (n + 1)] + bias1) * keep1
            if h < 2:
                values = values * first_g
            if h == F1 - 1:
                values = values * last_g
            block = jnp.concatenate(
                [*beside(values), jnp.zeros((K2 - 24 * Y1, 128), F32)], axis=0
            )
            x2[h * K2 : (h + 1) * K2, :] = block.astype(BF)

    bias2 = column_of(b2, 8 * Y2, 8)
    keep2 = jnp.where(iota((8 * Y2, 128), 0) < 8, first_t, 1.0)

    def layer_two(*fs):
        data = jnp.concatenate([x2[h * K2 : (h + 3) * K2, :] for h in fs], axis=1)
        sums = jnp.dot(w2[0 : 8 * Y2, 0 : 3 * K2], data, preferred_element_type=F32)
        for n, h in enumerate(fs):
            values = leaky(sums[:, 128 * n : 128 * (n + 1)] + bias2) * keep2
            if h == 0:
                values = values * first_g
            l2[h] = values

    lane = iota((8 * Y2, 128), 1)

    def joined(to, at, f):
        lower, upper = l2[f], l2[f + 4]
        before = jnp.where(lane < 64, pltpu.roll(lower, 65, 1), pltpu.roll(upper, 1, 1))
        block = jnp.concatenate(
            [
                jnp.where((lane & 63) == 0, 0.0, before),
                jnp.where(lane < 64, lower, pltpu.roll(upper, 64, 1)),
                jnp.where(lane < 64, pltpu.roll(lower, 64, 1), upper),
                jnp.zeros((K3 - 24 * Y2, 128), F32),
            ],
            axis=0,
        )
        to[at * K3 : (at + 1) * K3, :] = block.astype(BF)

    def inner():
        arrive("inner")
        for f in range(5, SPAN):
            operand(f)
        for f in (5, 7, 9, 11):
            layer_one(f, f + 1)
        for f in (5, 7, 9):
            layer_two(f, f + 1)

    def rest():
        arrive("upper near")
        for f in (SPAN, SPAN + 1, SPAN + 2):
            operand(f)
        layer_one(13, 14)
        layer_one(15, 16)
        layer_two(11, 12)
        layer_two(13, 14)
        for n in range(3):
            joined(x3_upper, n, 8 + n)
        arrive("lower near")
        operand(3)
        operand(4)
        layer_one(3, 4)
        layer_two(3, 4)
        joined(x3, 3, 3)
        joined(x3, 4, 4)
        arrive("upper far")
        operand(SPAN + 3)
        operand(SPAN + 4)
        layer_one(17, 18)
        layer_two(15, 16)
        joined(x3_upper, 3, 11)
        joined(x3_upper, 4, 12)
        third_matmul(x3_upper, 0, w3, bias3, upper)
        arrive("lower far")
        for f in range(3):
            operand(f)
        layer_one(1, 2)
        layer_one(0)
        layer_two(1, 2)
        layer_two(0)
        for n in range(3):
            joined(x3, n, n)

    return inner, rest


def spread_kernel(
    sky, k1_in, k2_in, k3_in, b1_in, b2_in, b3_in,
    x3, w3, bias3, upper,
    raw, moved, slab, cube, k1, k2, k3, b1, b2, b3, stack1, base2, stack3, w1, w2, x1, x2, l2, x3_upper,
    in_sem, send_sem, recv_sem,
):
    groups, strips = lax.axis_size("freq"), lax.axis_size("tile")
    g, t = lax.axis_index("freq"), lax.axis_index("tile")
    height = raw.shape[0]

    pairs = [(sky.at[0], raw), (k1_in, k1), (k2_in, k2), (k3_in, k3), (b1_in, b1), (b2_in, b2), (b3_in, b3)]
    loads = [pltpu.make_async_copy(a, b, in_sem.at[n]) for n, (a, b) in enumerate(pairs)]
    for load in loads:
        load.start()

    barrier = pltpu.get_barrier_semaphore()

    def greet(group, strip):
        pl.semaphore_signal(barrier, inc=1, device_id=(group, strip), device_id_type=MESH)

    @pl.when(g < groups - 1)
    def _():
        for strip in (0, 1):
            greet(g + 1, strip)

    @pl.when(g > 0)
    def _():
        for strip in (strips - 3, strips - 2, strips - 1):
            greet(g - 1, strip)

    @pl.loop(1, strips)
    def _(k):
        greet(g, lax.rem(t + k, strips))

    lane = iota((128, 128), 1)
    column = jnp.where(lane < 64, 2 * lane, 2 * lane - 127)
    order = (iota((128, 128), 0) == column).astype(F32).astype(BF)
    moved[0:8, :] = jnp.zeros((8, 128), F32)
    moved[height : height + 16, :] = jnp.zeros((16, 128), F32)
    loads[0].wait()
    values = jnp.dot(raw[...].astype(BF), order, preferred_element_type=F32)
    moved[4 : height + 4, :] = values
    slab[...] = moved[...].reshape(slab.shape).astype(BF)

    high = t >= strips - 3
    low = t < 2
    beyond = jnp.logical_or(jnp.logical_and(low, g > 0), jnp.logical_and(high, g < groups - 1))
    other = jnp.where(low, jnp.maximum(g - 1, 0), jnp.minimum(g + 1, groups - 1))
    plane = 3 + t
    far_plane = jnp.where(low, SPAN + 3 + t, jnp.maximum(t - (strips - 3), 0))

    def near(k):
        strip = lax.rem(t + k, strips)
        return pltpu.make_async_remote_copy(
            src_ref=slab.at[pl.ds(2 * strip, 3)],
            dst_ref=cube.at[plane],
            send_sem=send_sem.at[k],
            recv_sem=recv_sem.at[plane],
            device_id=(g, strip),
            device_id_type=MESH,
        )

    def far(k):
        strip = lax.rem(t + k, strips)
        return pltpu.make_async_remote_copy(
            src_ref=slab.at[pl.ds(2 * strip, 3)],
            dst_ref=cube.at[far_plane],
            send_sem=send_sem.at[strips + k],
            recv_sem=recv_sem.at[far_plane],
            device_id=(other, strip),
            device_id_type=MESH,
        )

    own = pltpu.make_async_copy(slab.at[pl.ds(2 * t, 3)], cube.at[plane], recv_sem.at[plane])
    own.start()

    def send():
        @pl.when(beyond)
        def _():
            pl.semaphore_wait(barrier, 2 * strips - 1)

            @pl.loop(0, strips)
            def _(k):
                far(k).start()

        @pl.when(jnp.logical_not(beyond))
        def _():
            pl.semaphore_wait(barrier, strips - 1)

        @pl.loop(1, strips)
        def _(k):
            near(k).start()

    def arrived(p):
        pltpu.make_async_copy(cube.at[p], cube.at[p], recv_sem.at[p]).wait()

    def arrive(side):
        if side == "inner":
            @pl.loop(5, SPAN)
            def _(p):
                arrived(p)
        elif side == "upper near":
            for p in (SPAN, SPAN + 1, SPAN + 2):
                arrived(p)
        elif side == "lower near":
            for p in (3, 4):
                arrived(p)
        elif side == "upper far":
            @pl.when(g < groups - 1)
            def _():
                for p in (SPAN + 3, SPAN + 4):
                    arrived(p)

            @pl.when(g == groups - 1)
            def _():
                cube[SPAN + 3 : SPAN + 5] = jnp.zeros((2, 3, 8, 128), BF)
        else:
            @pl.when(g > 0)
            def _():
                for p in range(3):
                    arrived(p)

            @pl.when(g == 0)
            def _():
                cube[0:3] = jnp.zeros((3, 3, 8, 128), BF)

    for load in loads[1:]:
        load.wait()
    inner, rest = layer_steps(
        (groups, strips, g, t), cube, arrive, b1, b2, bias3, x1, x2, l2, x3_upper, x3, w1, w2, w3, upper
    )

    compute_first = jnp.logical_and(jnp.logical_and(low, g > 0), lax.rem(g, 4) == 0)
    compute_at = jnp.where(compute_first, 0, 1)

    @pl.loop(0, 2)
    def _(turn):
        @pl.when(turn == compute_at)
        def _():
            banded_weights(k1, k2, k3, stack1, base2, stack3, w1, w2, w3)
            for o in range(16):
                bias3[8 * o : 8 * o + 8, :] = jnp.full((8, 128), b3[o], F32)
            inner()

        @pl.when(turn == 0)
        def _():
            send()

    rest()

    @pl.loop(1, strips)
    def _(k):
        near(k).wait_send()

    @pl.when(beyond)
    def _():
        @pl.loop(0, strips)
        def _(k):
            far(k).wait_send()


X3_SHAPE = (5 * K3, 128)
HALF_SHAPE = (16, SPAN // 4, SPAN // 2, 64)
WEIGHT_SCRATCH = [
    pltpu.VMEM((128, 128), F32),
    pltpu.VMEM((8, 1408), F32),
    pltpu.VMEM((256, 128), F32),
    pltpu.VMEM((160, 256), BF),
    pltpu.VMEM((144, 1408), BF),
]
LAYER_SCRATCH = [
    pltpu.VMEM((PLANES * K1, 128), BF),
    pltpu.VMEM((F1 * K2, 128), BF),
    pltpu.VMEM((F2, 8 * Y2, 128), F32),
    pltpu.VMEM(X3_SHAPE, BF),
]


def first_layers(sky_cube, k1, k2, k3, b1, b2, b3):
    height = sky_cube.shape[1]
    strips = height // SPAN
    operands = [
        pltpu.with_memory_space_constraint(x, pltpu.HBM)
        for x in (sky_cube, k1, k2, k3, b1, b2, b3)
    ]
    vmem = pl.BlockSpec(memory_space=pltpu.VMEM)
    return pl.pallas_call(
        spread_kernel,
        out_shape=[
            jax.ShapeDtypeStruct(X3_SHAPE, BF),
            jax.ShapeDtypeStruct((128, 1280), BF),
            jax.ShapeDtypeStruct((128, 128), F32),
            jax.ShapeDtypeStruct(HALF_SHAPE, BF),
        ],
        in_specs=[pl.BlockSpec(memory_space=pltpu.HBM)] * len(operands),
        out_specs=[vmem] * 4,
        scratch_shapes=[
            pltpu.VMEM((height, 128), F32),
            pltpu.VMEM((height + 16, 128), F32),
            pltpu.VMEM(((height + 16) // 8, 8, 128), BF),
            pltpu.VMEM((PLANES, 3, 8, 128), BF),
            pltpu.VMEM(k1.shape, BF),
            pltpu.VMEM(k2.shape, BF),
            pltpu.VMEM(k3.shape, BF),
            pltpu.SMEM(b1.shape, F32),
            pltpu.SMEM(b2.shape, F32),
            pltpu.SMEM(b3.shape, F32),
            *WEIGHT_SCRATCH,
            *LAYER_SCRATCH,
            pltpu.SemaphoreType.DMA((len(operands),)),
            pltpu.SemaphoreType.DMA((2 * strips,)),
            pltpu.SemaphoreType.DMA((PLANES,)),
        ],
        compiler_params=pltpu.CompilerParams(
            collective_id=0, has_side_effects=True, vmem_limit_bytes=24 << 20
        ),
        name="first_layers",
    )(*operands)


def third_kernel(x3, w3, bias3, upper, out, lower, sem):
    quarter = SPAN // 4
    done = pltpu.make_async_copy(upper, out.at[:, quarter : 2 * quarter], sem.at[0])
    done.start()
    third_matmul(x3, 0, w3, bias3, lower)
    rest = pltpu.make_async_copy(lower, out.at[:, 0:quarter], sem.at[1])
    rest.start()
    done.wait()
    rest.wait()


def third_layer(x3, w3, bias3, upper):
    vmem = pl.BlockSpec(memory_space=pltpu.VMEM)
    half = SPAN // 2
    return pl.pallas_call(
        third_kernel,
        out_shape=jax.ShapeDtypeStruct((16, half, half, 64), BF),
        in_specs=[vmem] * 4,
        out_specs=pl.BlockSpec(memory_space=pl.ANY),
        scratch_shapes=[pltpu.VMEM(HALF_SHAPE, BF), pltpu.SemaphoreType.DMA((2,))],
        compiler_params=pltpu.CompilerParams(vmem_limit_bytes=8 << 20),
        name="third_layer",
    )(x3, w3, bias3, upper)


def body(sky_cube, kernel_one, bias_one, kernel_two, bias_two, kernel_three, bias_three):
    return third_layer(
        *first_layers(
            sky_cube,
            kernel_one.transpose(1, 2, 3, 4, 0),
            kernel_two.transpose(2, 3, 4, 0, 1),
            kernel_three.transpose(2, 3, 4, 1, 0),
            bias_one,
            bias_two,
            bias_three,
        )
    )


def solution(mesh):
    return jax.shard_map(
        body,
        mesh=mesh,
        in_specs=(P(("freq", "tile"), None, None), P(), P(), P(), P(), P(), P()),
        out_specs=P(None, "freq", "tile", None),
        check_vma=False,
    )
```

```python
import jax
import jax.numpy as jnp
from jax import lax
from jax.experimental import pallas as pl
from jax.experimental.pallas import tpu as pltpu
from jax.sharding import PartitionSpec as P

MESH = pl.DeviceIdType.MESH
BF = jnp.bfloat16
F32 = jnp.float32

SPAN = 16
PLANES = SPAN + 5
ROWS = 24
F1, Y1 = SPAN + 3, SPAN + 3
F2, Y2 = SPAN + 1, SPAN + 1
K1 = 80
K2 = 464
K3 = 416


def iota(shape, dim):
    return lax.broadcasted_iota(jnp.int32, shape, dim)


def leaky(values):
    return jnp.maximum(values, 0.1 * values)


def beside(values):
    lane = iota(values.shape, 1)
    swapped = pltpu.roll(values, 64, 1)
    before = jnp.where(lane < 64, pltpu.roll(values, 65, 1), swapped)
    after = jnp.where(lane < 64, swapped, pltpu.roll(values, 63, 1))
    return (
        jnp.where(lane == 0, 0.0, before),
        values,
        jnp.where(lane == 127, 0.0, after),
    )


def column_of(bias, rows, count):
    row = iota((count, 128), 0)
    block = jnp.zeros((count, 128), F32)
    for o in range(count):
        block = jnp.where(row == o, bias[o], block)
    return jnp.concatenate([block] * (rows // count), axis=0)


def taps():
    return [(a, b, c) for a in range(3) for b in range(3) for c in range(3)]


def one_if(inside):
    return jnp.where(inside, 1.0, 0.0).astype(F32)


def banded_weights(k1, k2, k3, stack1, base2, stack3, w1, w2, w3):
    stack1[...] = jnp.zeros(stack1.shape, F32)
    for a in range(3):
        for b in range(3):
            at = 8 * (3 * a + b)
            stack1[at : at + 3, 0:8] = k1[0, a, b].astype(F32)
    source = iota((128, 256), 0)
    tap, c = source >> 3, source & 7
    a = (tap * 21846) >> 16
    target = jnp.where((tap < 9) & (c < 3), a * K1 + c * ROWS + 1 + tap - 3 * a, -1)
    base = jnp.dot(
        stack1[...].T[0:8].astype(BF),
        (iota((128, 256), 1) == target).astype(F32).astype(BF),
        preferred_element_type=F32,
    )
    for y in range(0, Y1, 2):
        both = [pltpu.roll(base, s, 1) if s else base for s in (y, y + 1)]
        w1[8 * y : 8 * y + 16, :] = jnp.concatenate(both, axis=0).astype(BF)

    base2[...] = jnp.zeros(base2.shape, F32)
    for a, b, c in taps():
        at = a * K2 + c * (8 * Y1) + 8 * b
        base2[:, at : at + 8] = k2[a, b, c].astype(F32)
    base = base2[...]
    for y in range(0, Y2, 2):
        both = [pltpu.roll(base, 8 * s, 1) if s else base for s in (y, min(y + 1, Y2 - 1))]
        w2[8 * y : 8 * y + 16, :] = jnp.concatenate(both, axis=0).astype(BF)

    stack3[...] = jnp.zeros(stack3.shape, F32)
    for n, (a, b, c) in enumerate(taps()):
        stack3[8 * n : 8 * n + 8, 0:16] = k3[a, b, c].astype(F32)
    source = iota((256, 1280), 0)
    tap, i = source >> 3, source & 7
    a = (tap * 7282) >> 16
    rest = tap - 9 * a
    b = (rest * 21846) >> 16
    target = jnp.where(tap < 27, a * K3 + (rest - 3 * b) * (8 * Y2) + 8 * b + i, -1)
    base = jnp.dot(
        stack3[...].T[0:16].astype(BF),
        (iota((256, 1280), 1) == target).astype(F32).astype(BF),
        preferred_element_type=F32,
    )
    rows = [pltpu.roll(base, 16 * y, 1) if y else base for y in range(SPAN // 2)]
    by_row = jnp.concatenate(rows, axis=0).astype(BF)
    r = iota((128, 128), 0)
    swap = iota((128, 128), 1) == (r & 7) * 16 + (r >> 3)
    w3[...] = jnp.dot(
        swap.astype(F32).astype(BF), by_row, preferred_element_type=F32
    ).astype(BF)


def third_matmul(x3, first, w3, bias3, out):
    data = jnp.concatenate(
        [x3[h * K3 : (h + 3) * K3, :] for h in (first, first + 2)], axis=1
    )
    sums = jnp.dot(w3[:, 0 : 3 * K3], data, preferred_element_type=F32)
    for n in range(2):
        values = leaky(sums[:, 128 * n : 128 * (n + 1)] + bias3[...])
        out[:, n, :, :] = values[:, 0:64].reshape(16, 8, 64).astype(BF)
        swapped = pltpu.roll(values, 64, 1)
        out[:, n + 2, :, :] = swapped[:, 0:64].reshape(16, 8, 64).astype(BF)


def layer_steps(place, cube, arrive, b1, b2, bias3, x1, x2, l2, x3_upper, x3, w1, w2, w3, upper):
    groups, strips, g, t = place
    first_g, last_g = one_if(g > 0), one_if(g < groups - 1)
    first_t, last_t = one_if(t > 0), one_if(t < strips - 1)

    def operand(f):
        pieces = beside(cube[f].reshape(ROWS, 128).astype(F32))
        block = jnp.concatenate([*pieces, jnp.zeros((K1 - 3 * ROWS, 128), F32)], axis=0)
        x1[f * K1 : (f + 1) * K1, :] = block.astype(BF)

    bias1 = column_of(b1, 8 * Y1, 8)
    row = iota((8 * Y1, 128), 0)
    keep1 = jnp.where(row < 16, first_t, jnp.where(row >= 8 * (Y1 - 1), last_t, 1.0))

    def layer_one(*fs):
        data = jnp.concatenate([x1[h * K1 : (h + 3) * K1, :] for h in fs], axis=1)
        sums = jnp.dot(w1[0 : 8 * Y1, 0 : 3 * K1], data, preferred_element_type=F32)
        for n, h in enumerate(fs):
            values = leaky(sums[:, 128 * n : 128 * (n + 1)] + bias1) * keep1
            if h < 2:
                values = values * first_g
            if h == F1 - 1:
                values = values * last_g
            block = jnp.concatenate(
                [*beside(values), jnp.zeros((K2 - 24 * Y1, 128), F32)], axis=0
            )
            x2[h * K2 : (h + 1) * K2, :] = block.astype(BF)

    bias2 = column_of(b2, 8 * Y2, 8)
    keep2 = jnp.where(iota((8 * Y2, 128), 0) < 8, first_t, 1.0)

    def layer_two(*fs):
        data = jnp.concatenate([x2[h * K2 : (h + 3) * K2, :] for h in fs], axis=1)
        sums = jnp.dot(w2[0 : 8 * Y2, 0 : 3 * K2], data, preferred_element_type=F32)
        for n, h in enumerate(fs):
            values = leaky(sums[:, 128 * n : 128 * (n + 1)] + bias2) * keep2
            if h == 0:
                values = values * first_g
            l2[h] = values

    lane = iota((8 * Y2, 128), 1)

    def joined(to, at, f):
        lower, upper = l2[f], l2[f + 4]
        before = jnp.where(lane < 64, pltpu.roll(lower, 65, 1), pltpu.roll(upper, 1, 1))
        block = jnp.concatenate(
            [
                jnp.where((lane & 63) == 0, 0.0, before),
                jnp.where(lane < 64, lower, pltpu.roll(upper, 64, 1)),
                jnp.where(lane < 64, pltpu.roll(lower, 64, 1), upper),
                jnp.zeros((K3 - 24 * Y2, 128), F32),
            ],
            axis=0,
        )
        to[at * K3 : (at + 1) * K3, :] = block.astype(BF)

    def inner():
        arrive("inner")
        for f in range(5, SPAN):
            operand(f)
        for f in (5, 7, 9, 11):
            layer_one(f, f + 1)
        for f in (5, 7, 9):
            layer_two(f, f + 1)

    def rest():
        arrive("upper near")
        for f in (SPAN, SPAN + 1, SPAN + 2):
            operand(f)
        layer_one(13, 14)
        layer_one(15, 16)
        layer_two(11, 12)
        layer_two(13, 14)
        for n in range(3):
            joined(x3_upper, n, 8 + n)
        arrive("lower near")
        operand(3)
        operand(4)
        layer_one(3, 4)
        layer_two(3, 4)
        joined(x3, 3, 3)
        joined(x3, 4, 4)
        arrive("upper far")
        operand(SPAN + 3)
        operand(SPAN + 4)
        layer_one(17, 18)
        layer_two(15, 16)
        joined(x3_upper, 3, 11)
        joined(x3_upper, 4, 12)
        third_matmul(x3_upper, 0, w3, bias3, upper)
        arrive("lower far")
        for f in range(3):
            operand(f)
        layer_one(1, 2)
        layer_one(0)
        layer_two(1, 2)
        layer_two(0)
        for n in range(3):
            joined(x3, n, n)

    return inner, rest


def spread_kernel(
    sky, k1_in, k2_in, k3_in, b1_in, b2_in, b3_in,
    x3, w3, bias3, upper,
    raw, moved, slab, cube, k1, k2, k3, b1, b2, b3, stack1, base2, stack3, w1, w2, x1, x2, l2, x3_upper,
    in_sem, send_sem, recv_sem,
):
    groups, strips = lax.axis_size("freq"), lax.axis_size("tile")
    g, t = lax.axis_index("freq"), lax.axis_index("tile")
    height = raw.shape[0]

    barrier = pltpu.get_barrier_semaphore()

    def greet(group, strip):
        pl.semaphore_signal(barrier, inc=1, device_id=(group, strip), device_id_type=MESH)

    @pl.when(g < groups - 1)
    def _():
        for strip in (0, 1):
            greet(g + 1, strip)

    @pl.when(g > 0)
    def _():
        for strip in (strips - 3, strips - 2, strips - 1):
            greet(g - 1, strip)

    @pl.loop(1, strips)
    def _(k):
        greet(g, lax.rem(t + k, strips))

    pairs = [(sky.at[0], raw), (k1_in, k1), (k2_in, k2), (k3_in, k3), (b1_in, b1), (b2_in, b2), (b3_in, b3)]
    loads = [pltpu.make_async_copy(a, b, in_sem.at[n]) for n, (a, b) in enumerate(pairs)]
    for load in loads:
        load.start()

    lane = iota((128, 128), 1)
    column = jnp.where(lane < 64, 2 * lane, 2 * lane - 127)
    order = (iota((128, 128), 0) == column).astype(F32).astype(BF)
    moved[0:8, :] = jnp.zeros((8, 128), F32)
    moved[height : height + 16, :] = jnp.zeros((16, 128), F32)
    loads[0].wait()
    values = jnp.dot(raw[...].astype(BF), order, preferred_element_type=F32)
    moved[4 : height + 4, :] = values
    slab[...] = moved[...].reshape(slab.shape).astype(BF)

    high = t >= strips - 3
    low = t < 2
    beyond = jnp.logical_or(jnp.logical_and(low, g > 0), jnp.logical_and(high, g < groups - 1))
    other = jnp.where(low, jnp.maximum(g - 1, 0), jnp.minimum(g + 1, groups - 1))
    plane = 3 + t
    far_plane = jnp.where(low, SPAN + 3 + t, jnp.maximum(t - (strips - 3), 0))

    def near(k):
        strip = lax.rem(t + k, strips)
        return pltpu.make_async_remote_copy(
            src_ref=slab.at[pl.ds(2 * strip, 3)],
            dst_ref=cube.at[plane],
            send_sem=send_sem.at[k],
            recv_sem=recv_sem.at[plane],
            device_id=(g, strip),
            device_id_type=MESH,
        )

    def far(k):
        strip = lax.rem(t + k, strips)
        return pltpu.make_async_remote_copy(
            src_ref=slab.at[pl.ds(2 * strip, 3)],
            dst_ref=cube.at[far_plane],
            send_sem=send_sem.at[strips + k],
            recv_sem=recv_sem.at[far_plane],
            device_id=(other, strip),
            device_id_type=MESH,
        )

    own = pltpu.make_async_copy(slab.at[pl.ds(2 * t, 3)], cube.at[plane], recv_sem.at[plane])
    own.start()

    def send():
        @pl.when(beyond)
        def _():
            pl.semaphore_wait(barrier, 2 * strips - 1)

            @pl.loop(0, strips)
            def _(k):
                far(k).start()

        @pl.when(jnp.logical_not(beyond))
        def _():
            pl.semaphore_wait(barrier, strips - 1)

        @pl.loop(1, strips)
        def _(k):
            near(k).start()

    def arrived(p):
        pltpu.make_async_copy(cube.at[p], cube.at[p], recv_sem.at[p]).wait()

    def arrive(side):
        if side == "inner":
            @pl.loop(5, SPAN)
            def _(p):
                arrived(p)
        elif side == "upper near":
            for p in (SPAN, SPAN + 1, SPAN + 2):
                arrived(p)
        elif side == "lower near":
            for p in (3, 4):
                arrived(p)
        elif side == "upper far":
            @pl.when(g < groups - 1)
            def _():
                for p in (SPAN + 3, SPAN + 4):
                    arrived(p)

            @pl.when(g == groups - 1)
            def _():
                cube[SPAN + 3 : SPAN + 5] = jnp.zeros((2, 3, 8, 128), BF)
        else:
            @pl.when(g > 0)
            def _():
                for p in range(3):
                    arrived(p)

            @pl.when(g == 0)
            def _():
                cube[0:3] = jnp.zeros((3, 3, 8, 128), BF)

    for load in loads[1:]:
        load.wait()
    inner, rest = layer_steps(
        (groups, strips, g, t), cube, arrive, b1, b2, bias3, x1, x2, l2, x3_upper, x3, w1, w2, w3, upper
    )

    compute_first = jnp.logical_and(jnp.logical_and(low, g > 0), lax.rem(g, 4) == 0)
    compute_at = jnp.where(compute_first, 0, 1)

    @pl.loop(0, 2)
    def _(turn):
        @pl.when(turn == compute_at)
        def _():
            banded_weights(k1, k2, k3, stack1, base2, stack3, w1, w2, w3)
            for o in range(16):
                bias3[8 * o : 8 * o + 8, :] = jnp.full((8, 128), b3[o], F32)
            inner()

        @pl.when(turn == 0)
        def _():
            send()

    rest()

    @pl.loop(1, strips)
    def _(k):
        near(k).wait_send()

    @pl.when(beyond)
    def _():
        @pl.loop(0, strips)
        def _(k):
            far(k).wait_send()


X3_SHAPE = (5 * K3, 128)
HALF_SHAPE = (16, SPAN // 4, SPAN // 2, 64)
WEIGHT_SCRATCH = [
    pltpu.VMEM((128, 128), F32),
    pltpu.VMEM((8, 1408), F32),
    pltpu.VMEM((256, 128), F32),
    pltpu.VMEM((160, 256), BF),
    pltpu.VMEM((144, 1408), BF),
]
LAYER_SCRATCH = [
    pltpu.VMEM((PLANES * K1, 128), BF),
    pltpu.VMEM((F1 * K2, 128), BF),
    pltpu.VMEM((F2, 8 * Y2, 128), F32),
    pltpu.VMEM(X3_SHAPE, BF),
]


def first_layers(sky_cube, k1, k2, k3, b1, b2, b3):
    height = sky_cube.shape[1]
    strips = height // SPAN
    operands = [
        pltpu.with_memory_space_constraint(x, pltpu.HBM)
        for x in (sky_cube, k1, k2, k3, b1, b2, b3)
    ]
    vmem = pl.BlockSpec(memory_space=pltpu.VMEM)
    return pl.pallas_call(
        spread_kernel,
        out_shape=[
            jax.ShapeDtypeStruct(X3_SHAPE, BF),
            jax.ShapeDtypeStruct((128, 1280), BF),
            jax.ShapeDtypeStruct((128, 128), F32),
            jax.ShapeDtypeStruct(HALF_SHAPE, BF),
        ],
        in_specs=[pl.BlockSpec(memory_space=pltpu.HBM)] * len(operands),
        out_specs=[vmem] * 4,
        scratch_shapes=[
            pltpu.VMEM((height, 128), F32),
            pltpu.VMEM((height + 16, 128), F32),
            pltpu.VMEM(((height + 16) // 8, 8, 128), BF),
            pltpu.VMEM((PLANES, 3, 8, 128), BF),
            pltpu.VMEM(k1.shape, BF),
            pltpu.VMEM(k2.shape, BF),
            pltpu.VMEM(k3.shape, BF),
            pltpu.SMEM(b1.shape, F32),
            pltpu.SMEM(b2.shape, F32),
            pltpu.SMEM(b3.shape, F32),
            *WEIGHT_SCRATCH,
            *LAYER_SCRATCH,
            pltpu.SemaphoreType.DMA((len(operands),)),
            pltpu.SemaphoreType.DMA((2 * strips,)),
            pltpu.SemaphoreType.DMA((PLANES,)),
        ],
        compiler_params=pltpu.CompilerParams(
            collective_id=0, has_side_effects=True, vmem_limit_bytes=24 << 20
        ),
        name="first_layers",
    )(*operands)


def third_kernel(x3, w3, bias3, upper, out, lower, sem):
    quarter = SPAN // 4
    done = pltpu.make_async_copy(upper, out.at[:, quarter : 2 * quarter], sem.at[0])
    done.start()
    third_matmul(x3, 0, w3, bias3, lower)
    rest = pltpu.make_async_copy(lower, out.at[:, 0:quarter], sem.at[1])
    rest.start()
    done.wait()
    rest.wait()


def third_layer(x3, w3, bias3, upper):
    vmem = pl.BlockSpec(memory_space=pltpu.VMEM)
    half = SPAN // 2
    return pl.pallas_call(
        third_kernel,
        out_shape=jax.ShapeDtypeStruct((16, half, half, 64), BF),
        in_specs=[vmem] * 4,
        out_specs=pl.BlockSpec(memory_space=pl.ANY),
        scratch_shapes=[pltpu.VMEM(HALF_SHAPE, BF), pltpu.SemaphoreType.DMA((2,))],
        compiler_params=pltpu.CompilerParams(vmem_limit_bytes=8 << 20),
        name="third_layer",
    )(x3, w3, bias3, upper)


def body(sky_cube, kernel_one, bias_one, kernel_two, bias_two, kernel_three, bias_three):
    return third_layer(
        *first_layers(
            sky_cube,
            kernel_one.transpose(1, 2, 3, 4, 0),
            kernel_two.transpose(2, 3, 4, 0, 1),
            kernel_three.transpose(2, 3, 4, 1, 0),
            bias_one,
            bias_two,
            bias_three,
        )
    )


def solution(mesh):
    return jax.shard_map(
        body,
        mesh=mesh,
        in_specs=(P(("freq", "tile"), None, None), P(), P(), P(), P(), P(), P()),
        out_specs=P(None, "freq", "tile", None),
        check_vma=False,
    )
```

```python
import jax
import jax.numpy as jnp
from jax import lax
from jax.experimental import pallas as pl
from jax.experimental.pallas import tpu as pltpu
from jax.sharding import PartitionSpec as P

MESH = pl.DeviceIdType.MESH
BF = jnp.bfloat16
F32 = jnp.float32

SPAN = 16
PLANES = SPAN + 5
ROWS = 24
F1, Y1 = SPAN + 3, SPAN + 3
F2, Y2 = SPAN + 1, SPAN + 1
K1 = 80
K2 = 464
K3 = 416


def iota(shape, dim):
    return lax.broadcasted_iota(jnp.int32, shape, dim)


def leaky(values):
    return jnp.maximum(values, 0.1 * values)


def beside(values):
    lane = iota(values.shape, 1)
    swapped = pltpu.roll(values, 64, 1)
    before = jnp.where(lane < 64, pltpu.roll(values, 65, 1), swapped)
    after = jnp.where(lane < 64, swapped, pltpu.roll(values, 63, 1))
    return (
        jnp.where(lane == 0, 0.0, before),
        values,
        jnp.where(lane == 127, 0.0, after),
    )


def column_of(bias, rows, count):
    row = iota((count, 128), 0)
    block = jnp.zeros((count, 128), F32)
    for o in range(count):
        block = jnp.where(row == o, bias[o], block)
    return jnp.concatenate([block] * (rows // count), axis=0)


def taps():
    return [(a, b, c) for a in range(3) for b in range(3) for c in range(3)]


def one_if(inside):
    return jnp.where(inside, 1.0, 0.0).astype(F32)


def first_weights(k1, k2, stack1, base2, w1, w2):
    stack1[...] = jnp.zeros(stack1.shape, F32)
    for a in range(3):
        for b in range(3):
            at = 8 * (3 * a + b)
            stack1[at : at + 3, 0:8] = k1[0, a, b].astype(F32)
    source = iota((128, 256), 0)
    tap, c = source >> 3, source & 7
    a = (tap * 21846) >> 16
    target = jnp.where((tap < 9) & (c < 3), a * K1 + c * ROWS + 1 + tap - 3 * a, -1)
    base = jnp.dot(
        stack1[...].T[0:8].astype(BF),
        (iota((128, 256), 1) == target).astype(F32).astype(BF),
        preferred_element_type=F32,
    )
    for y in range(0, Y1, 2):
        both = [pltpu.roll(base, s, 1) if s else base for s in (y, y + 1)]
        w1[8 * y : 8 * y + 16, :] = jnp.concatenate(both, axis=0).astype(BF)

    base2[...] = jnp.zeros(base2.shape, F32)
    for a, b, c in taps():
        at = a * K2 + c * (8 * Y1) + 8 * b
        base2[:, at : at + 8] = k2[a, b, c].astype(F32)
    base = base2[...]
    for y in range(0, Y2, 2):
        both = [pltpu.roll(base, 8 * s, 1) if s else base for s in (y, min(y + 1, Y2 - 1))]
        w2[8 * y : 8 * y + 16, :] = jnp.concatenate(both, axis=0).astype(BF)


def third_weights(k3, stack3, w3):
    stack3[...] = jnp.zeros(stack3.shape, F32)
    for n, (a, b, c) in enumerate(taps()):
        stack3[8 * n : 8 * n + 8, 0:16] = k3[a, b, c].astype(F32)
    source = iota((256, 1280), 0)
    tap, i = source >> 3, source & 7
    a = (tap * 7282) >> 16
    rest = tap - 9 * a
    b = (rest * 21846) >> 16
    target = jnp.where(tap < 27, a * K3 + (rest - 3 * b) * (8 * Y2) + 8 * b + i, -1)
    base = jnp.dot(
        stack3[...].T[0:16].astype(BF),
        (iota((256, 1280), 1) == target).astype(F32).astype(BF),
        preferred_element_type=F32,
    )
    rows = [pltpu.roll(base, 16 * y, 1) if y else base for y in range(SPAN // 2)]
    by_row = jnp.concatenate(rows, axis=0).astype(BF)
    r = iota((128, 128), 0)
    swap = iota((128, 128), 1) == (r & 7) * 16 + (r >> 3)
    w3[...] = jnp.dot(
        swap.astype(F32).astype(BF), by_row, preferred_element_type=F32
    ).astype(BF)


def third_matmul(x3, first, w3, bias3, out):
    data = jnp.concatenate(
        [x3[h * K3 : (h + 3) * K3, :] for h in (first, first + 2)], axis=1
    )
    sums = jnp.dot(w3[:, 0 : 3 * K3], data, preferred_element_type=F32)
    for n in range(2):
        values = leaky(sums[:, 128 * n : 128 * (n + 1)] + bias3[...])
        out[:, n, :, :] = values[:, 0:64].reshape(16, 8, 64).astype(BF)
        swapped = pltpu.roll(values, 64, 1)
        out[:, n + 2, :, :] = swapped[:, 0:64].reshape(16, 8, 64).astype(BF)


def all_layers(place, cube, arrive, b1, b2, bias3, x1, x2, l2, x3_upper, x3, w1, w2, w3, upper):
    groups, strips, g, t = place
    first_g, last_g = one_if(g > 0), one_if(g < groups - 1)
    first_t, last_t = one_if(t > 0), one_if(t < strips - 1)

    def operand(f):
        pieces = beside(cube[f].reshape(ROWS, 128).astype(F32))
        block = jnp.concatenate([*pieces, jnp.zeros((K1 - 3 * ROWS, 128), F32)], axis=0)
        x1[f * K1 : (f + 1) * K1, :] = block.astype(BF)

    bias1 = column_of(b1, 8 * Y1, 8)
    row = iota((8 * Y1, 128), 0)
    keep1 = jnp.where(row < 16, first_t, jnp.where(row >= 8 * (Y1 - 1), last_t, 1.0))

    def layer_one(*fs):
        data = jnp.concatenate([x1[h * K1 : (h + 3) * K1, :] for h in fs], axis=1)
        sums = jnp.dot(w1[0 : 8 * Y1, 0 : 3 * K1], data, preferred_element_type=F32)
        for n, h in enumerate(fs):
            values = leaky(sums[:, 128 * n : 128 * (n + 1)] + bias1) * keep1
            if h < 2:
                values = values * first_g
            if h == F1 - 1:
                values = values * last_g
            block = jnp.concatenate(
                [*beside(values), jnp.zeros((K2 - 24 * Y1, 128), F32)], axis=0
            )
            x2[h * K2 : (h + 1) * K2, :] = block.astype(BF)

    bias2 = column_of(b2, 8 * Y2, 8)
    keep2 = jnp.where(iota((8 * Y2, 128), 0) < 8, first_t, 1.0)

    def layer_two(*fs):
        data = jnp.concatenate([x2[h * K2 : (h + 3) * K2, :] for h in fs], axis=1)
        sums = jnp.dot(w2[0 : 8 * Y2, 0 : 3 * K2], data, preferred_element_type=F32)
        for n, h in enumerate(fs):
            values = leaky(sums[:, 128 * n : 128 * (n + 1)] + bias2) * keep2
            if h == 0:
                values = values * first_g
            l2[h] = values

    lane = iota((8 * Y2, 128), 1)

    def joined(to, at, f):
        lower, upper = l2[f], l2[f + 4]
        before = jnp.where(lane < 64, pltpu.roll(lower, 65, 1), pltpu.roll(upper, 1, 1))
        block = jnp.concatenate(
            [
                jnp.where((lane & 63) == 0, 0.0, before),
                jnp.where(lane < 64, lower, pltpu.roll(upper, 64, 1)),
                jnp.where(lane < 64, pltpu.roll(lower, 64, 1), upper),
                jnp.zeros((K3 - 24 * Y2, 128), F32),
            ],
            axis=0,
        )
        to[at * K3 : (at + 1) * K3, :] = block.astype(BF)

    arrive("inner")
    for f in range(5, SPAN):
        operand(f)
    for f in (5, 7, 9, 11):
        layer_one(f, f + 1)
    for f in (5, 7, 9):
        layer_two(f, f + 1)
    arrive("upper")
    for f in range(SPAN, PLANES):
        operand(f)
    for f in (13, 15, 17):
        layer_one(f, f + 1)
    for f in (11, 13, 15):
        layer_two(f, f + 1)
    for n in range(5):
        joined(x3_upper, n, 8 + n)
    third_matmul(x3_upper, 0, w3, bias3, upper)
    arrive("lower near")
    operand(3)
    operand(4)
    layer_one(3, 4)
    layer_two(3, 4)
    joined(x3, 3, 3)
    joined(x3, 4, 4)
    arrive("lower far")
    for f in range(3):
        operand(f)
    layer_one(1, 2)
    layer_one(0)
    layer_two(1, 2)
    layer_two(0)
    for n in range(3):
        joined(x3, n, n)


def spread_kernel(
    sky, k1_in, k2_in, k3_in, b1_in, b2_in, b3_in,
    x3, w3, bias3, upper,
    raw, moved, slab, cube, k1, k2, k3, b1, b2, b3, stack1, base2, stack3, w1, w2, x1, x2, l2, x3_upper,
    in_sem, send_sem, recv_sem,
):
    groups, strips = lax.axis_size("freq"), lax.axis_size("tile")
    g, t = lax.axis_index("freq"), lax.axis_index("tile")
    height = raw.shape[0]

    barrier = pltpu.get_barrier_semaphore()

    def greet(group, strip):
        pl.semaphore_signal(barrier, inc=1, device_id=(group, strip), device_id_type=MESH)

    @pl.when(g < groups - 1)
    def _():
        for strip in (0, 1):
            greet(g + 1, strip)

    @pl.when(g > 0)
    def _():
        for strip in (strips - 3, strips - 2, strips - 1):
            greet(g - 1, strip)

    @pl.loop(1, strips)
    def _(k):
        greet(g, lax.rem(t + k, strips))

    pairs = [(k1_in, k1), (k2_in, k2), (sky.at[0], raw), (k3_in, k3), (b1_in, b1), (b2_in, b2), (b3_in, b3)]
    loads = [pltpu.make_async_copy(a, b, in_sem.at[n]) for n, (a, b) in enumerate(pairs)]
    for load in loads:
        load.start()

    lane = iota((128, 128), 1)
    column = jnp.where(lane < 64, 2 * lane, 2 * lane - 127)
    order = (iota((128, 128), 0) == column).astype(F32).astype(BF)
    moved[0:8, :] = jnp.zeros((8, 128), F32)
    moved[height : height + 16, :] = jnp.zeros((16, 128), F32)
    loads[0].wait()
    loads[1].wait()
    first_weights(k1, k2, stack1, base2, w1, w2)
    loads[2].wait()
    values = jnp.dot(raw[...].astype(BF), order, preferred_element_type=F32)
    moved[4 : height + 4, :] = values
    slab[...] = moved[...].reshape(slab.shape).astype(BF)

    high = t >= strips - 3
    low = t < 2
    beyond = jnp.logical_or(jnp.logical_and(low, g > 0), jnp.logical_and(high, g < groups - 1))
    other = jnp.where(low, jnp.maximum(g - 1, 0), jnp.minimum(g + 1, groups - 1))
    plane = 3 + t
    far_plane = jnp.where(low, SPAN + 3 + t, jnp.maximum(t - (strips - 3), 0))

    @pl.when(beyond)
    def _():
        pl.semaphore_wait(barrier, 2 * strips - 1)

    @pl.when(jnp.logical_not(beyond))
    def _():
        pl.semaphore_wait(barrier, strips - 1)

    def near(k):
        strip = lax.rem(t + k, strips)
        return pltpu.make_async_remote_copy(
            src_ref=slab.at[pl.ds(2 * strip, 3)],
            dst_ref=cube.at[plane],
            send_sem=send_sem.at[k],
            recv_sem=recv_sem.at[plane],
            device_id=(g, strip),
            device_id_type=MESH,
        )

    def far(k):
        strip = lax.rem(t + k, strips)
        return pltpu.make_async_remote_copy(
            src_ref=slab.at[pl.ds(2 * strip, 3)],
            dst_ref=cube.at[far_plane],
            send_sem=send_sem.at[strips + k],
            recv_sem=recv_sem.at[far_plane],
            device_id=(other, strip),
            device_id_type=MESH,
        )

    @pl.when(beyond)
    def _():
        @pl.loop(0, strips)
        def _(k):
            far(k).start()

    @pl.loop(1, strips)
    def _(k):
        near(k).start()

    pltpu.make_async_copy(slab.at[pl.ds(2 * t, 3)], cube.at[plane], recv_sem.at[plane]).start()

    for load in loads[3:]:
        load.wait()
    third_weights(k3, stack3, w3)
    for o in range(16):
        bias3[8 * o : 8 * o + 8, :] = jnp.full((8, 128), b3[o], F32)

    def arrived(p):
        pltpu.make_async_copy(cube.at[p], cube.at[p], recv_sem.at[p]).wait()

    def arrive(side):
        if side == "inner":
            @pl.loop(5, SPAN)
            def _(p):
                arrived(p)
        elif side == "upper":
            for p in (SPAN, SPAN + 1, SPAN + 2):
                arrived(p)

            @pl.when(g < groups - 1)
            def _():
                for p in (SPAN + 3, SPAN + 4):
                    arrived(p)

            @pl.when(g == groups - 1)
            def _():
                cube[SPAN + 3 : SPAN + 5] = jnp.zeros((2, 3, 8, 128), BF)
        elif side == "lower near":
            for p in (3, 4):
                arrived(p)
        else:
            @pl.when(g > 0)
            def _():
                for p in range(3):
                    arrived(p)

            @pl.when(g == 0)
            def _():
                cube[0:3] = jnp.zeros((3, 3, 8, 128), BF)

    all_layers(
        (groups, strips, g, t), cube, arrive, b1, b2, bias3, x1, x2, l2, x3_upper, x3, w1, w2, w3, upper
    )

    @pl.loop(1, strips)
    def _(k):
        near(k).wait_send()

    @pl.when(beyond)
    def _():
        @pl.loop(0, strips)
        def _(k):
            far(k).wait_send()


X3_SHAPE = (5 * K3, 128)
HALF_SHAPE = (16, SPAN // 4, SPAN // 2, 64)
WEIGHT_SCRATCH = [
    pltpu.VMEM((128, 128), F32),
    pltpu.VMEM((8, 1408), F32),
    pltpu.VMEM((256, 128), F32),
    pltpu.VMEM((160, 256), BF),
    pltpu.VMEM((144, 1408), BF),
]
LAYER_SCRATCH = [
    pltpu.VMEM((PLANES * K1, 128), BF),
    pltpu.VMEM((F1 * K2, 128), BF),
    pltpu.VMEM((F2, 8 * Y2, 128), F32),
    pltpu.VMEM(X3_SHAPE, BF),
]


def first_layers(sky_cube, k1, k2, k3, b1, b2, b3):
    height = sky_cube.shape[1]
    strips = height // SPAN
    operands = [
        pltpu.with_memory_space_constraint(x, pltpu.HBM)
        for x in (sky_cube, k1, k2, k3, b1, b2, b3)
    ]
    vmem = pl.BlockSpec(memory_space=pltpu.VMEM)
    return pl.pallas_call(
        spread_kernel,
        out_shape=[
            jax.ShapeDtypeStruct(X3_SHAPE, BF),
            jax.ShapeDtypeStruct((128, 1280), BF),
            jax.ShapeDtypeStruct((128, 128), F32),
            jax.ShapeDtypeStruct(HALF_SHAPE, BF),
        ],
        in_specs=[pl.BlockSpec(memory_space=pltpu.HBM)] * len(operands),
        out_specs=[vmem] * 4,
        scratch_shapes=[
            pltpu.VMEM((height, 128), F32),
            pltpu.VMEM((height + 16, 128), F32),
            pltpu.VMEM(((height + 16) // 8, 8, 128), BF),
            pltpu.VMEM((PLANES, 3, 8, 128), BF),
            pltpu.VMEM(k1.shape, BF),
            pltpu.VMEM(k2.shape, BF),
            pltpu.VMEM(k3.shape, BF),
            pltpu.SMEM(b1.shape, F32),
            pltpu.SMEM(b2.shape, F32),
            pltpu.SMEM(b3.shape, F32),
            *WEIGHT_SCRATCH,
            *LAYER_SCRATCH,
            pltpu.SemaphoreType.DMA((len(operands),)),
            pltpu.SemaphoreType.DMA((2 * strips,)),
            pltpu.SemaphoreType.DMA((PLANES,)),
        ],
        compiler_params=pltpu.CompilerParams(
            collective_id=0, has_side_effects=True, vmem_limit_bytes=24 << 20
        ),
        name="first_layers",
    )(*operands)


def third_kernel(x3, w3, bias3, upper, out, lower, sem):
    quarter = SPAN // 4
    done = pltpu.make_async_copy(upper, out.at[:, quarter : 2 * quarter], sem.at[0])
    done.start()
    third_matmul(x3, 0, w3, bias3, lower)
    rest = pltpu.make_async_copy(lower, out.at[:, 0:quarter], sem.at[1])
    rest.start()
    done.wait()
    rest.wait()


def third_layer(x3, w3, bias3, upper):
    vmem = pl.BlockSpec(memory_space=pltpu.VMEM)
    half = SPAN // 2
    return pl.pallas_call(
        third_kernel,
        out_shape=jax.ShapeDtypeStruct((16, half, half, 64), BF),
        in_specs=[vmem] * 4,
        out_specs=pl.BlockSpec(memory_space=pl.ANY),
        scratch_shapes=[pltpu.VMEM(HALF_SHAPE, BF), pltpu.SemaphoreType.DMA((2,))],
        compiler_params=pltpu.CompilerParams(vmem_limit_bytes=8 << 20),
        name="third_layer",
    )(x3, w3, bias3, upper)


def body(sky_cube, kernel_one, bias_one, kernel_two, bias_two, kernel_three, bias_three):
    return third_layer(
        *first_layers(
            sky_cube,
            kernel_one.transpose(1, 2, 3, 4, 0),
            kernel_two.transpose(2, 3, 4, 0, 1),
            kernel_three.transpose(2, 3, 4, 1, 0),
            bias_one,
            bias_two,
            bias_three,
        )
    )


def solution(mesh):
    return jax.shard_map(
        body,
        mesh=mesh,
        in_specs=(P(("freq", "tile"), None, None), P(), P(), P(), P(), P(), P()),
        out_specs=P(None, "freq", "tile", None),
        check_vma=False,
    )
```

```python
import jax
import jax.numpy as jnp
from jax import lax
from jax.experimental import pallas as pl
from jax.experimental.pallas import tpu as pltpu
from jax.sharding import PartitionSpec as P

MESH = pl.DeviceIdType.MESH
BF = jnp.bfloat16
F32 = jnp.float32

SPAN = 16
PLANES = SPAN + 5
ROWS = 24
F1, Y1 = SPAN + 3, SPAN + 3
F2, Y2 = SPAN + 1, SPAN + 1
K1 = 80
K2 = 464
K3 = 416


def iota(shape, dim):
    return lax.broadcasted_iota(jnp.int32, shape, dim)


def leaky(values):
    return jnp.maximum(values, 0.1 * values)


def beside(values):
    lane = iota(values.shape, 1)
    swapped = pltpu.roll(values, 64, 1)
    before = jnp.where(lane < 64, pltpu.roll(values, 65, 1), swapped)
    after = jnp.where(lane < 64, swapped, pltpu.roll(values, 63, 1))
    return (
        jnp.where(lane == 0, 0.0, before),
        values,
        jnp.where(lane == 127, 0.0, after),
    )


def column_of(bias, rows, count):
    row = iota((count, 128), 0)
    block = jnp.zeros((count, 128), F32)
    for o in range(count):
        block = jnp.where(row == o, bias[o], block)
    return jnp.concatenate([block] * (rows // count), axis=0)


def taps():
    return [(a, b, c) for a in range(3) for b in range(3) for c in range(3)]


def one_if(inside):
    return jnp.where(inside, 1.0, 0.0).astype(F32)


def banded_weights(k1, k2, k3, stack1, base2, stack3, w1, w2, w3):
    stack1[...] = jnp.zeros(stack1.shape, F32)
    for a in range(3):
        for b in range(3):
            at = 8 * (3 * a + b)
            stack1[at : at + 3, 0:8] = k1[0, a, b].astype(F32)
    source = iota((128, 256), 0)
    tap, c = source >> 3, source & 7
    a = (tap * 21846) >> 16
    target = jnp.where((tap < 9) & (c < 3), a * K1 + c * ROWS + 1 + tap - 3 * a, -1)
    base = jnp.dot(
        stack1[...].T[0:8].astype(BF),
        (iota((128, 256), 1) == target).astype(F32).astype(BF),
        preferred_element_type=F32,
    )
    for y in range(0, Y1, 2):
        both = [pltpu.roll(base, s, 1) if s else base for s in (y, y + 1)]
        w1[8 * y : 8 * y + 16, :] = jnp.concatenate(both, axis=0).astype(BF)

    base2[...] = jnp.zeros(base2.shape, F32)
    for a, b, c in taps():
        at = a * K2 + c * (8 * Y1) + 8 * b
        base2[:, at : at + 8] = k2[a, b, c].astype(F32)
    base = base2[...]
    for y in range(0, Y2, 2):
        both = [pltpu.roll(base, 8 * s, 1) if s else base for s in (y, min(y + 1, Y2 - 1))]
        w2[8 * y : 8 * y + 16, :] = jnp.concatenate(both, axis=0).astype(BF)

    stack3[...] = jnp.zeros(stack3.shape, F32)
    for n, (a, b, c) in enumerate(taps()):
        stack3[8 * n : 8 * n + 8, 0:16] = k3[a, b, c].astype(F32)
    source = iota((256, 1280), 0)
    tap, i = source >> 3, source & 7
    a = (tap * 7282) >> 16
    rest = tap - 9 * a
    b = (rest * 21846) >> 16
    target = jnp.where(tap < 27, a * K3 + (rest - 3 * b) * (8 * Y2) + 8 * b + i, -1)
    base = jnp.dot(
        stack3[...].T[0:16].astype(BF),
        (iota((256, 1280), 1) == target).astype(F32).astype(BF),
        preferred_element_type=F32,
    )
    rows = [pltpu.roll(base, 16 * y, 1) if y else base for y in range(SPAN // 2)]
    by_row = jnp.concatenate(rows, axis=0).astype(BF)
    r = iota((128, 128), 0)
    swap = iota((128, 128), 1) == (r & 7) * 16 + (r >> 3)
    w3[...] = jnp.dot(
        swap.astype(F32).astype(BF), by_row, preferred_element_type=F32
    ).astype(BF)


def third_matmul(x3, first, w3, bias3, out):
    data = jnp.concatenate(
        [x3[h * K3 : (h + 3) * K3, :] for h in (first, first + 2)], axis=1
    )
    sums = jnp.dot(w3[:, 0 : 3 * K3], data, preferred_element_type=F32)
    for n in range(2):
        values = leaky(sums[:, 128 * n : 128 * (n + 1)] + bias3[...])
        out[:, n, :, :] = values[:, 0:64].reshape(16, 8, 64).astype(BF)
        swapped = pltpu.roll(values, 64, 1)
        out[:, n + 2, :, :] = swapped[:, 0:64].reshape(16, 8, 64).astype(BF)


def all_layers(place, cube, arrive, b1, b2, bias3, x1, x2, l2, x3_upper, x3, w1, w2, w3, upper):
    groups, strips, g, t = place
    first_g, last_g = one_if(g > 0), one_if(g < groups - 1)
    first_t, last_t = one_if(t > 0), one_if(t < strips - 1)

    def operand(f):
        pieces = beside(cube[f].reshape(ROWS, 128).astype(F32))
        block = jnp.concatenate([*pieces, jnp.zeros((K1 - 3 * ROWS, 128), F32)], axis=0)
        x1[f * K1 : (f + 1) * K1, :] = block.astype(BF)

    bias1 = column_of(b1, 8 * Y1, 8)
    row = iota((8 * Y1, 128), 0)
    keep1 = jnp.where(row < 16, first_t, jnp.where(row >= 8 * (Y1 - 1), last_t, 1.0))

    def layer_one(*fs):
        data = jnp.concatenate([x1[h * K1 : (h + 3) * K1, :] for h in fs], axis=1)
        sums = jnp.dot(w1[0 : 8 * Y1, 0 : 3 * K1], data, preferred_element_type=F32)
        for n, h in enumerate(fs):
            values = leaky(sums[:, 128 * n : 128 * (n + 1)] + bias1) * keep1
            if h < 2:
                values = values * first_g
            if h == F1 - 1:
                values = values * last_g
            block = jnp.concatenate(
                [*beside(values), jnp.zeros((K2 - 24 * Y1, 128), F32)], axis=0
            )
            x2[h * K2 : (h + 1) * K2, :] = block.astype(BF)

    bias2 = column_of(b2, 8 * Y2, 8)
    keep2 = jnp.where(iota((8 * Y2, 128), 0) < 8, first_t, 1.0)

    def layer_two(*fs):
        data = jnp.concatenate([x2[h * K2 : (h + 3) * K2, :] for h in fs], axis=1)
        sums = jnp.dot(w2[0 : 8 * Y2, 0 : 3 * K2], data, preferred_element_type=F32)
        for n, h in enumerate(fs):
            values = leaky(sums[:, 128 * n : 128 * (n + 1)] + bias2) * keep2
            if h == 0:
                values = values * first_g
            l2[h] = values

    lane = iota((8 * Y2, 128), 1)

    def joined(to, at, f):
        lower, upper = l2[f], l2[f + 4]
        before = jnp.where(lane < 64, pltpu.roll(lower, 65, 1), pltpu.roll(upper, 1, 1))
        block = jnp.concatenate(
            [
                jnp.where((lane & 63) == 0, 0.0, before),
                jnp.where(lane < 64, lower, pltpu.roll(upper, 64, 1)),
                jnp.where(lane < 64, pltpu.roll(lower, 64, 1), upper),
                jnp.zeros((K3 - 24 * Y2, 128), F32),
            ],
            axis=0,
        )
        to[at * K3 : (at + 1) * K3, :] = block.astype(BF)

    arrive("inner")
    for f in range(5, SPAN):
        operand(f)
    for f in (5, 7, 9, 11):
        layer_one(f, f + 1)
    for f in (5, 7, 9):
        layer_two(f, f + 1)
    arrive("upper")
    for f in range(SPAN, PLANES):
        operand(f)
    for f in (13, 15, 17):
        layer_one(f, f + 1)
    for f in (11, 13, 15):
        layer_two(f, f + 1)
    for n in range(5):
        joined(x3_upper, n, 8 + n)
    third_matmul(x3_upper, 0, w3, bias3, upper)
    arrive("lower near")
    operand(3)
    operand(4)
    layer_one(3, 4)
    layer_two(3, 4)
    joined(x3, 3, 3)
    joined(x3, 4, 4)
    arrive("lower far")
    for f in range(3):
        operand(f)
    layer_one(1, 2)
    layer_one(0)
    layer_two(1, 2)
    layer_two(0)
    for n in range(3):
        joined(x3, n, n)


def spread_kernel(
    sky, k1_in, k2_in, k3_in, b1_in, b2_in, b3_in,
    x3, w3, bias3, upper,
    raw, moved, slab, cube, k1, k2, k3, b1, b2, b3, stack1, base2, stack3, w1, w2, x1, x2, l2, x3_upper,
    in_sem, send_sem, recv_sem,
):
    groups, strips = lax.axis_size("freq"), lax.axis_size("tile")
    g, t = lax.axis_index("freq"), lax.axis_index("tile")
    height = raw.shape[0]

    quarter = height // 4
    pairs = [(sky.at[0, pl.ds(n * quarter, quarter)], raw.at[pl.ds(n * quarter, quarter)]) for n in range(4)]
    pairs += [(k1_in, k1), (k2_in, k2), (k3_in, k3), (b1_in, b1), (b2_in, b2), (b3_in, b3)]
    loads = [pltpu.make_async_copy(a, b, in_sem.at[n]) for n, (a, b) in enumerate(pairs)]
    for load in loads[:4]:
        load.start()

    barrier = pltpu.get_barrier_semaphore()

    def greet(group, strip):
        pl.semaphore_signal(barrier, inc=1, device_id=(group, strip), device_id_type=MESH)

    @pl.when(g < groups - 1)
    def _():
        for strip in (0, 1):
            greet(g + 1, strip)

    @pl.when(g > 0)
    def _():
        for strip in (strips - 3, strips - 2, strips - 1):
            greet(g - 1, strip)

    @pl.loop(1, strips)
    def _(k):
        greet(g, lax.rem(t + k, strips))

    lane = iota((128, 128), 1)
    column = jnp.where(lane < 64, 2 * lane, 2 * lane - 127)
    order = (iota((128, 128), 0) == column).astype(F32).astype(BF)
    moved[0:8, :] = jnp.zeros((8, 128), F32)
    moved[height : height + 16, :] = jnp.zeros((16, 128), F32)
    for load in loads[:4]:
        load.wait()
    for load in loads[4:]:
        load.start()
    values = jnp.dot(raw[...].astype(BF), order, preferred_element_type=F32)
    moved[4 : height + 4, :] = values
    slab[...] = moved[...].reshape(slab.shape).astype(BF)

    high = t >= strips - 3
    low = t < 2
    beyond = jnp.logical_or(jnp.logical_and(low, g > 0), jnp.logical_and(high, g < groups - 1))
    other = jnp.where(low, jnp.maximum(g - 1, 0), jnp.minimum(g + 1, groups - 1))
    plane = 3 + t
    far_plane = jnp.where(low, SPAN + 3 + t, jnp.maximum(t - (strips - 3), 0))

    @pl.when(beyond)
    def _():
        pl.semaphore_wait(barrier, 2 * strips - 1)

    @pl.when(jnp.logical_not(beyond))
    def _():
        pl.semaphore_wait(barrier, strips - 1)

    def near(k):
        strip = lax.rem(t + k, strips)
        return pltpu.make_async_remote_copy(
            src_ref=slab.at[pl.ds(2 * strip, 3)],
            dst_ref=cube.at[plane],
            send_sem=send_sem.at[k],
            recv_sem=recv_sem.at[plane],
            device_id=(g, strip),
            device_id_type=MESH,
        )

    def far(k):
        strip = lax.rem(t + k, strips)
        return pltpu.make_async_remote_copy(
            src_ref=slab.at[pl.ds(2 * strip, 3)],
            dst_ref=cube.at[far_plane],
            send_sem=send_sem.at[strips + k],
            recv_sem=recv_sem.at[far_plane],
            device_id=(other, strip),
            device_id_type=MESH,
        )

    @pl.when(beyond)
    def _():
        @pl.loop(0, strips)
        def _(k):
            far(k).start()

    @pl.loop(1, strips)
    def _(k):
        near(k).start()

    pltpu.make_async_copy(slab.at[pl.ds(2 * t, 3)], cube.at[plane], recv_sem.at[plane]).start()

    for load in loads[4:]:
        load.wait()
    banded_weights(k1, k2, k3, stack1, base2, stack3, w1, w2, w3)
    for o in range(16):
        bias3[8 * o : 8 * o + 8, :] = jnp.full((8, 128), b3[o], F32)

    def arrived(p):
        pltpu.make_async_copy(cube.at[p], cube.at[p], recv_sem.at[p]).wait()

    def arrive(side):
        if side == "inner":
            @pl.loop(5, SPAN)
            def _(p):
                arrived(p)
        elif side == "upper":
            for p in (SPAN, SPAN + 1, SPAN + 2):
                arrived(p)

            @pl.when(g < groups - 1)
            def _():
                for p in (SPAN + 3, SPAN + 4):
                    arrived(p)

            @pl.when(g == groups - 1)
            def _():
                cube[SPAN + 3 : SPAN + 5] = jnp.zeros((2, 3, 8, 128), BF)
        elif side == "lower near":
            for p in (3, 4):
                arrived(p)
        else:
            @pl.when(g > 0)
            def _():
                for p in range(3):
                    arrived(p)

            @pl.when(g == 0)
            def _():
                cube[0:3] = jnp.zeros((3, 3, 8, 128), BF)

    all_layers(
        (groups, strips, g, t), cube, arrive, b1, b2, bias3, x1, x2, l2, x3_upper, x3, w1, w2, w3, upper
    )

    @pl.loop(1, strips)
    def _(k):
        near(k).wait_send()

    @pl.when(beyond)
    def _():
        @pl.loop(0, strips)
        def _(k):
            far(k).wait_send()


X3_SHAPE = (5 * K3, 128)
HALF_SHAPE = (16, SPAN // 4, SPAN // 2, 64)
WEIGHT_SCRATCH = [
    pltpu.VMEM((128, 128), F32),
    pltpu.VMEM((8, 1408), F32),
    pltpu.VMEM((256, 128), F32),
    pltpu.VMEM((160, 256), BF),
    pltpu.VMEM((144, 1408), BF),
]
LAYER_SCRATCH = [
    pltpu.VMEM((PLANES * K1, 128), BF),
    pltpu.VMEM((F1 * K2, 128), BF),
    pltpu.VMEM((F2, 8 * Y2, 128), F32),
    pltpu.VMEM(X3_SHAPE, BF),
]


def first_layers(sky_cube, k1, k2, k3, b1, b2, b3):
    height = sky_cube.shape[1]
    strips = height // SPAN
    operands = [
        pltpu.with_memory_space_constraint(x, pltpu.HBM)
        for x in (sky_cube, k1, k2, k3, b1, b2, b3)
    ]
    vmem = pl.BlockSpec(memory_space=pltpu.VMEM)
    return pl.pallas_call(
        spread_kernel,
        out_shape=[
            jax.ShapeDtypeStruct(X3_SHAPE, BF),
            jax.ShapeDtypeStruct((128, 1280), BF),
            jax.ShapeDtypeStruct((128, 128), F32),
            jax.ShapeDtypeStruct(HALF_SHAPE, BF),
        ],
        in_specs=[pl.BlockSpec(memory_space=pltpu.HBM)] * len(operands),
        out_specs=[vmem] * 4,
        scratch_shapes=[
            pltpu.VMEM((height, 128), F32),
            pltpu.VMEM((height + 16, 128), F32),
            pltpu.VMEM(((height + 16) // 8, 8, 128), BF),
            pltpu.VMEM((PLANES, 3, 8, 128), BF),
            pltpu.VMEM(k1.shape, BF),
            pltpu.VMEM(k2.shape, BF),
            pltpu.VMEM(k3.shape, BF),
            pltpu.SMEM(b1.shape, F32),
            pltpu.SMEM(b2.shape, F32),
            pltpu.SMEM(b3.shape, F32),
            *WEIGHT_SCRATCH,
            *LAYER_SCRATCH,
            pltpu.SemaphoreType.DMA((len(operands) + 3,)),
            pltpu.SemaphoreType.DMA((2 * strips,)),
            pltpu.SemaphoreType.DMA((PLANES,)),
        ],
        compiler_params=pltpu.CompilerParams(
            collective_id=0, has_side_effects=True, vmem_limit_bytes=24 << 20
        ),
        name="first_layers",
    )(*operands)


def third_kernel(x3, w3, bias3, upper, out, lower, sem):
    quarter = SPAN // 4
    done = pltpu.make_async_copy(upper, out.at[:, quarter : 2 * quarter], sem.at[0])
    done.start()
    third_matmul(x3, 0, w3, bias3, lower)
    rest = pltpu.make_async_copy(lower, out.at[:, 0:quarter], sem.at[1])
    rest.start()
    done.wait()
    rest.wait()


def third_layer(x3, w3, bias3, upper):
    vmem = pl.BlockSpec(memory_space=pltpu.VMEM)
    half = SPAN // 2
    return pl.pallas_call(
        third_kernel,
        out_shape=jax.ShapeDtypeStruct((16, half, half, 64), BF),
        in_specs=[vmem] * 4,
        out_specs=pl.BlockSpec(memory_space=pl.ANY),
        scratch_shapes=[pltpu.VMEM(HALF_SHAPE, BF), pltpu.SemaphoreType.DMA((2,))],
        compiler_params=pltpu.CompilerParams(vmem_limit_bytes=8 << 20),
        name="third_layer",
    )(x3, w3, bias3, upper)


def body(sky_cube, kernel_one, bias_one, kernel_two, bias_two, kernel_three, bias_three):
    return third_layer(
        *first_layers(
            sky_cube,
            kernel_one.transpose(1, 2, 3, 4, 0),
            kernel_two.transpose(2, 3, 4, 0, 1),
            kernel_three.transpose(2, 3, 4, 1, 0),
            bias_one,
            bias_two,
            bias_three,
        )
    )


def solution(mesh):
    return jax.shard_map(
        body,
        mesh=mesh,
        in_specs=(P(("freq", "tile"), None, None), P(), P(), P(), P(), P(), P()),
        out_specs=P(None, "freq", "tile", None),
        check_vma=False,
    )
```

```python
import jax
import jax.numpy as jnp
from jax import lax
from jax.experimental import pallas as pl
from jax.experimental.pallas import tpu as pltpu
from jax.sharding import PartitionSpec as P

MESH = pl.DeviceIdType.MESH
BF = jnp.bfloat16
F32 = jnp.float32

SPAN = 16
PLANES = SPAN + 5
ROWS = 24
F1, Y1 = SPAN + 3, SPAN + 3
F2, Y2 = SPAN + 1, SPAN + 1
K1 = 80
K2 = 464
K3 = 416


def iota(shape, dim):
    return lax.broadcasted_iota(jnp.int32, shape, dim)


def leaky(values):
    return jnp.maximum(values, 0.1 * values)


def beside(values):
    lane = iota(values.shape, 1)
    swapped = pltpu.roll(values, 64, 1)
    before = jnp.where(lane < 64, pltpu.roll(values, 65, 1), swapped)
    after = jnp.where(lane < 64, swapped, pltpu.roll(values, 63, 1))
    return (
        jnp.where(lane == 0, 0.0, before),
        values,
        jnp.where(lane == 127, 0.0, after),
    )


def column_of(bias, rows, count):
    row = iota((count, 128), 0)
    block = jnp.zeros((count, 128), F32)
    for o in range(count):
        block = jnp.where(row == o, bias[o], block)
    return jnp.concatenate([block] * (rows // count), axis=0)


def taps():
    return [(a, b, c) for a in range(3) for b in range(3) for c in range(3)]


def one_if(inside):
    return jnp.where(inside, 1.0, 0.0).astype(F32)


def banded_weights(k1, k2, k3, stack1, base2, stack3, w1, w2, w3):
    stack1[...] = jnp.zeros(stack1.shape, F32)
    for a in range(3):
        for b in range(3):
            at = 8 * (3 * a + b)
            stack1[at : at + 3, 0:8] = k1[0, a, b].astype(F32)
    source = iota((128, 256), 0)
    tap, c = source >> 3, source & 7
    a = (tap * 21846) >> 16
    target = jnp.where((tap < 9) & (c < 3), a * K1 + c * ROWS + 1 + tap - 3 * a, -1)
    base = jnp.dot(
        stack1[...].T[0:8].astype(BF),
        (iota((128, 256), 1) == target).astype(F32).astype(BF),
        preferred_element_type=F32,
    )
    for y in range(0, Y1, 2):
        both = [pltpu.roll(base, s, 1) if s else base for s in (y, y + 1)]
        w1[8 * y : 8 * y + 16, :] = jnp.concatenate(both, axis=0).astype(BF)

    base2[...] = jnp.zeros(base2.shape, F32)
    for a, b, c in taps():
        at = a * K2 + c * (8 * Y1) + 8 * b
        base2[:, at : at + 8] = k2[a, b, c].astype(F32)
    base = base2[...]
    for y in range(0, Y2, 2):
        both = [pltpu.roll(base, 8 * s, 1) if s else base for s in (y, min(y + 1, Y2 - 1))]
        w2[8 * y : 8 * y + 16, :] = jnp.concatenate(both, axis=0).astype(BF)

    stack3[...] = jnp.zeros(stack3.shape, F32)
    for n, (a, b, c) in enumerate(taps()):
        stack3[8 * n : 8 * n + 8, 0:16] = k3[a, b, c].astype(F32)
    source = iota((256, 1280), 0)
    tap, i = source >> 3, source & 7
    a = (tap * 7282) >> 16
    rest = tap - 9 * a
    b = (rest * 21846) >> 16
    target = jnp.where(tap < 27, a * K3 + (rest - 3 * b) * (8 * Y2) + 8 * b + i, -1)
    base = jnp.dot(
        stack3[...].T[0:16].astype(BF),
        (iota((256, 1280), 1) == target).astype(F32).astype(BF),
        preferred_element_type=F32,
    )
    rows = [pltpu.roll(base, 16 * y, 1) if y else base for y in range(SPAN // 2)]
    by_row = jnp.concatenate(rows, axis=0).astype(BF)
    r = iota((128, 128), 0)
    swap = iota((128, 128), 1) == (r & 7) * 16 + (r >> 3)
    w3[...] = jnp.dot(
        swap.astype(F32).astype(BF), by_row, preferred_element_type=F32
    ).astype(BF)


def third_matmul(x3, first, w3, bias3, out):
    data = jnp.concatenate(
        [x3[h * K3 : (h + 3) * K3, :] for h in (first, first + 2)], axis=1
    )
    sums = jnp.dot(w3[:, 0 : 3 * K3], data, preferred_element_type=F32)
    for n in range(2):
        values = leaky(sums[:, 128 * n : 128 * (n + 1)] + bias3[...])
        out[:, n, :, :] = values[:, 0:64].reshape(16, 8, 64).astype(BF)
        swapped = pltpu.roll(values, 64, 1)
        out[:, n + 2, :, :] = swapped[:, 0:64].reshape(16, 8, 64).astype(BF)


def all_layers(place, cube, arrive, b1, b2, bias3, x1, x2, l2, x3_upper, x3, w1, w2, w3, upper):
    groups, strips, g, t = place
    first_g, last_g = one_if(g > 0), one_if(g < groups - 1)
    first_t, last_t = one_if(t > 0), one_if(t < strips - 1)

    def operand(f):
        pieces = beside(cube[f].reshape(ROWS, 128).astype(F32))
        block = jnp.concatenate([*pieces, jnp.zeros((K1 - 3 * ROWS, 128), F32)], axis=0)
        x1[f * K1 : (f + 1) * K1, :] = block.astype(BF)

    bias1 = column_of(b1, 8 * Y1, 8)
    row = iota((8 * Y1, 128), 0)
    keep1 = jnp.where(row < 16, first_t, jnp.where(row >= 8 * (Y1 - 1), last_t, 1.0))

    def layer_one(*fs):
        data = jnp.concatenate([x1[h * K1 : (h + 3) * K1, :] for h in fs], axis=1)
        sums = jnp.dot(w1[0 : 8 * Y1, 0 : 3 * K1], data, preferred_element_type=F32)
        for n, h in enumerate(fs):
            values = leaky(sums[:, 128 * n : 128 * (n + 1)] + bias1) * keep1
            if h < 2:
                values = values * first_g
            if h == F1 - 1:
                values = values * last_g
            block = jnp.concatenate(
                [*beside(values), jnp.zeros((K2 - 24 * Y1, 128), F32)], axis=0
            )
            x2[h * K2 : (h + 1) * K2, :] = block.astype(BF)

    bias2 = column_of(b2, 8 * Y2, 8)
    keep2 = jnp.where(iota((8 * Y2, 128), 0) < 8, first_t, 1.0)

    def layer_two(*fs):
        data = jnp.concatenate([x2[h * K2 : (h + 3) * K2, :] for h in fs], axis=1)
        sums = jnp.dot(w2[0 : 8 * Y2, 0 : 3 * K2], data, preferred_element_type=F32)
        for n, h in enumerate(fs):
            values = leaky(sums[:, 128 * n : 128 * (n + 1)] + bias2) * keep2
            if h == 0:
                values = values * first_g
            l2[h] = values

    lane = iota((8 * Y2, 128), 1)

    def joined(to, at, f):
        lower, upper = l2[f], l2[f + 4]
        before = jnp.where(lane < 64, pltpu.roll(lower, 65, 1), pltpu.roll(upper, 1, 1))
        block = jnp.concatenate(
            [
                jnp.where((lane & 63) == 0, 0.0, before),
                jnp.where(lane < 64, lower, pltpu.roll(upper, 64, 1)),
                jnp.where(lane < 64, pltpu.roll(lower, 64, 1), upper),
                jnp.zeros((K3 - 24 * Y2, 128), F32),
            ],
            axis=0,
        )
        to[at * K3 : (at + 1) * K3, :] = block.astype(BF)

    arrive("inner")
    for f in range(5, SPAN):
        operand(f)
    for f in (5, 7, 9, 11):
        layer_one(f, f + 1)
    for f in (5, 7, 9):
        layer_two(f, f + 1)
    arrive("upper")
    for f in range(SPAN, PLANES):
        operand(f)
    for f in (13, 15, 17):
        layer_one(f, f + 1)
    for f in (11, 13, 15):
        layer_two(f, f + 1)
    for n in range(5):
        joined(x3_upper, n, 8 + n)
    third_matmul(x3_upper, 0, w3, bias3, upper)
    arrive("lower")
    for f in range(5):
        operand(f)
    layer_one(0, 1)
    layer_one(2, 3)
    layer_one(4)
    layer_two(0, 1)
    layer_two(2, 3)
    layer_two(4)
    for n in range(5):
        joined(x3, n, n)


def spread_kernel(
    sky, k1_in, k2_in, k3_in, b1_in, b2_in, b3_in,
    x3, w3, bias3, upper,
    raw, moved, slab, cube, k1, k2, k3, b1, b2, b3, stack1, base2, stack3, w1, w2, x1, x2, l2, x3_upper,
    in_sem, send_sem, recv_sem,
):
    groups, strips = lax.axis_size("freq"), lax.axis_size("tile")
    g, t = lax.axis_index("freq"), lax.axis_index("tile")
    height = raw.shape[0]

    quarter = height // 4
    pairs = [(sky.at[0, pl.ds(n * quarter, quarter)], raw.at[pl.ds(n * quarter, quarter)]) for n in range(4)]
    pairs += [(k1_in, k1), (k2_in, k2), (k3_in, k3), (b1_in, b1), (b2_in, b2), (b3_in, b3)]
    loads = [pltpu.make_async_copy(a, b, in_sem.at[n]) for n, (a, b) in enumerate(pairs)]
    for load in loads[:4]:
        load.start()

    barrier = pltpu.get_barrier_semaphore()

    def greet(group, strip):
        pl.semaphore_signal(barrier, inc=1, device_id=(group, strip), device_id_type=MESH)

    @pl.when(g < groups - 1)
    def _():
        for strip in (0, 1):
            greet(g + 1, strip)

    @pl.when(g > 0)
    def _():
        for strip in (strips - 3, strips - 2, strips - 1):
            greet(g - 1, strip)

    @pl.loop(1, strips)
    def _(k):
        greet(g, lax.rem(t + k, strips))

    lane = iota((128, 128), 1)
    column = jnp.where(lane < 64, 2 * lane, 2 * lane - 127)
    order = (iota((128, 128), 0) == column).astype(F32).astype(BF)
    moved[0:8, :] = jnp.zeros((8, 128), F32)
    moved[height : height + 16, :] = jnp.zeros((16, 128), F32)
    for load in loads[:4]:
        load.wait()
    for load in loads[4:]:
        load.start()
    values = jnp.dot(raw[...].astype(BF), order, preferred_element_type=F32)
    moved[4 : height + 4, :] = values
    slab[...] = moved[...].reshape(slab.shape).astype(BF)

    high = t >= strips - 3
    low = t < 2
    beyond = jnp.logical_or(jnp.logical_and(low, g > 0), jnp.logical_and(high, g < groups - 1))
    other = jnp.where(low, jnp.maximum(g - 1, 0), jnp.minimum(g + 1, groups - 1))
    plane = 3 + t
    far_plane = jnp.where(low, SPAN + 3 + t, jnp.maximum(t - (strips - 3), 0))

    @pl.when(beyond)
    def _():
        pl.semaphore_wait(barrier, 2 * strips - 1)

    @pl.when(jnp.logical_not(beyond))
    def _():
        pl.semaphore_wait(barrier, strips - 1)

    def near(k):
        strip = lax.rem(t + k, strips)
        return pltpu.make_async_remote_copy(
            src_ref=slab.at[pl.ds(2 * strip, 3)],
            dst_ref=cube.at[plane],
            send_sem=send_sem.at[k],
            recv_sem=recv_sem.at[plane],
            device_id=(g, strip),
            device_id_type=MESH,
        )

    def far(k):
        strip = lax.rem(t + k, strips)
        return pltpu.make_async_remote_copy(
            src_ref=slab.at[pl.ds(2 * strip, 3)],
            dst_ref=cube.at[far_plane],
            send_sem=send_sem.at[strips + k],
            recv_sem=recv_sem.at[far_plane],
            device_id=(other, strip),
            device_id_type=MESH,
        )

    @pl.when(beyond)
    def _():
        @pl.loop(0, strips)
        def _(k):
            far(k).start()

    @pl.loop(1, strips)
    def _(k):
        near(k).start()

    pltpu.make_async_copy(slab.at[pl.ds(2 * t, 3)], cube.at[plane], recv_sem.at[plane]).start()

    for load in loads[4:]:
        load.wait()
    banded_weights(k1, k2, k3, stack1, base2, stack3, w1, w2, w3)
    for o in range(16):
        bias3[8 * o : 8 * o + 8, :] = jnp.full((8, 128), b3[o], F32)

    def arrived(p):
        pltpu.make_async_copy(cube.at[p], cube.at[p], recv_sem.at[p]).wait()

    def arrive(side):
        if side == "inner":
            @pl.loop(5, SPAN)
            def _(p):
                arrived(p)
        elif side == "upper":
            for p in (SPAN, SPAN + 1, SPAN + 2):
                arrived(p)

            @pl.when(g < groups - 1)
            def _():
                for p in (SPAN + 3, SPAN + 4):
                    arrived(p)

            @pl.when(g == groups - 1)
            def _():
                cube[SPAN + 3 : SPAN + 5] = jnp.zeros((2, 3, 8, 128), BF)
        else:
            for p in (3, 4):
                arrived(p)

            @pl.when(g > 0)
            def _():
                for p in range(3):
                    arrived(p)

            @pl.when(g == 0)
            def _():
                cube[0:3] = jnp.zeros((3, 3, 8, 128), BF)

    all_layers(
        (groups, strips, g, t), cube, arrive, b1, b2, bias3, x1, x2, l2, x3_upper, x3, w1, w2, w3, upper
    )

    @pl.loop(1, strips)
    def _(k):
        near(k).wait_send()

    @pl.when(beyond)
    def _():
        @pl.loop(0, strips)
        def _(k):
            far(k).wait_send()


X3_SHAPE = (5 * K3, 128)
HALF_SHAPE = (16, SPAN // 4, SPAN // 2, 64)
WEIGHT_SCRATCH = [
    pltpu.VMEM((128, 128), F32),
    pltpu.VMEM((8, 1408), F32),
    pltpu.VMEM((256, 128), F32),
    pltpu.VMEM((160, 256), BF),
    pltpu.VMEM((144, 1408), BF),
]
LAYER_SCRATCH = [
    pltpu.VMEM((PLANES * K1, 128), BF),
    pltpu.VMEM((F1 * K2, 128), BF),
    pltpu.VMEM((F2, 8 * Y2, 128), F32),
    pltpu.VMEM(X3_SHAPE, BF),
]


def first_layers(sky_cube, k1, k2, k3, b1, b2, b3):
    height = sky_cube.shape[1]
    strips = height // SPAN
    operands = [
        pltpu.with_memory_space_constraint(x, pltpu.HBM)
        for x in (sky_cube, k1, k2, k3, b1, b2, b3)
    ]
    vmem = pl.BlockSpec(memory_space=pltpu.VMEM)
    return pl.pallas_call(
        spread_kernel,
        out_shape=[
            jax.ShapeDtypeStruct(X3_SHAPE, BF),
            jax.ShapeDtypeStruct((128, 1280), BF),
            jax.ShapeDtypeStruct((128, 128), F32),
            jax.ShapeDtypeStruct(HALF_SHAPE, BF),
        ],
        in_specs=[pl.BlockSpec(memory_space=pltpu.HBM)] * len(operands),
        out_specs=[vmem] * 4,
        scratch_shapes=[
            pltpu.VMEM((height, 128), F32),
            pltpu.VMEM((height + 16, 128), F32),
            pltpu.VMEM(((height + 16) // 8, 8, 128), BF),
            pltpu.VMEM((PLANES, 3, 8, 128), BF),
            pltpu.VMEM(k1.shape, BF),
            pltpu.VMEM(k2.shape, BF),
            pltpu.VMEM(k3.shape, BF),
            pltpu.SMEM(b1.shape, F32),
            pltpu.SMEM(b2.shape, F32),
            pltpu.SMEM(b3.shape, F32),
            *WEIGHT_SCRATCH,
            *LAYER_SCRATCH,
            pltpu.SemaphoreType.DMA((len(operands) + 3,)),
            pltpu.SemaphoreType.DMA((2 * strips,)),
            pltpu.SemaphoreType.DMA((PLANES,)),
        ],
        compiler_params=pltpu.CompilerParams(
            collective_id=0, has_side_effects=True, vmem_limit_bytes=24 << 20
        ),
        name="first_layers",
    )(*operands)


def third_kernel(x3, w3, bias3, upper, out, lower, sem):
    quarter = SPAN // 4
    done = pltpu.make_async_copy(upper, out.at[:, quarter : 2 * quarter], sem.at[0])
    done.start()
    third_matmul(x3, 0, w3, bias3, lower)
    rest = pltpu.make_async_copy(lower, out.at[:, 0:quarter], sem.at[1])
    rest.start()
    done.wait()
    rest.wait()


def third_layer(x3, w3, bias3, upper):
    vmem = pl.BlockSpec(memory_space=pltpu.VMEM)
    half = SPAN // 2
    return pl.pallas_call(
        third_kernel,
        out_shape=jax.ShapeDtypeStruct((16, half, half, 64), BF),
        in_specs=[vmem] * 4,
        out_specs=pl.BlockSpec(memory_space=pl.ANY),
        scratch_shapes=[pltpu.VMEM(HALF_SHAPE, BF), pltpu.SemaphoreType.DMA((2,))],
        compiler_params=pltpu.CompilerParams(vmem_limit_bytes=8 << 20),
        name="third_layer",
    )(x3, w3, bias3, upper)


def body(sky_cube, kernel_one, bias_one, kernel_two, bias_two, kernel_three, bias_three):
    return third_layer(
        *first_layers(
            sky_cube,
            kernel_one.transpose(1, 2, 3, 4, 0),
            kernel_two.transpose(2, 3, 4, 0, 1),
            kernel_three.transpose(2, 3, 4, 1, 0),
            bias_one,
            bias_two,
            bias_three,
        )
    )


def solution(mesh):
    return jax.shard_map(
        body,
        mesh=mesh,
        in_specs=(P(("freq", "tile"), None, None), P(), P(), P(), P(), P(), P()),
        out_specs=P(None, "freq", "tile", None),
        check_vma=False,
    )
```

```python
import jax
import jax.numpy as jnp
from jax import lax
from jax.experimental import pallas as pl
from jax.experimental.pallas import tpu as pltpu
from jax.sharding import PartitionSpec as P

MESH = pl.DeviceIdType.MESH
BF = jnp.bfloat16
F32 = jnp.float32

SPAN = 16
PLANES = SPAN + 5
ROWS = 24
F1, Y1 = SPAN + 3, SPAN + 3
F2, Y2 = SPAN + 1, SPAN + 1
K1 = 80
K2 = 464
K3 = 416


def iota(shape, dim):
    return lax.broadcasted_iota(jnp.int32, shape, dim)


def leaky(values):
    return jnp.maximum(values, 0.1 * values)


def beside(values):
    lane = iota(values.shape, 1)
    swapped = pltpu.roll(values, 64, 1)
    before = jnp.where(lane < 64, pltpu.roll(values, 65, 1), swapped)
    after = jnp.where(lane < 64, swapped, pltpu.roll(values, 63, 1))
    return (
        jnp.where(lane == 0, 0.0, before),
        values,
        jnp.where(lane == 127, 0.0, after),
    )


def column_of(bias, rows, count):
    row = iota((count, 128), 0)
    block = jnp.zeros((count, 128), F32)
    for o in range(count):
        block = jnp.where(row == o, bias[o], block)
    return jnp.concatenate([block] * (rows // count), axis=0)


def taps():
    return [(a, b, c) for a in range(3) for b in range(3) for c in range(3)]


def one_if(inside):
    return jnp.where(inside, 1.0, 0.0).astype(F32)


def first_weights(k1, k2, stack1, base2, w1, w2):
    stack1[...] = jnp.zeros(stack1.shape, F32)
    for a in range(3):
        for b in range(3):
            at = 8 * (3 * a + b)
            stack1[at : at + 3, 0:8] = k1[0, a, b].astype(F32)
    source = iota((128, 256), 0)
    tap, c = source >> 3, source & 7
    a = (tap * 21846) >> 16
    target = jnp.where((tap < 9) & (c < 3), a * K1 + c * ROWS + 1 + tap - 3 * a, -1)
    base = jnp.dot(
        stack1[...].T[0:8].astype(BF),
        (iota((128, 256), 1) == target).astype(F32).astype(BF),
        preferred_element_type=F32,
    )
    for y in range(0, Y1, 2):
        both = [pltpu.roll(base, s, 1) if s else base for s in (y, y + 1)]
        w1[8 * y : 8 * y + 16, :] = jnp.concatenate(both, axis=0).astype(BF)

    base2[...] = jnp.zeros(base2.shape, F32)
    for a, b, c in taps():
        at = a * K2 + c * (8 * Y1) + 8 * b
        base2[:, at : at + 8] = k2[a, b, c].astype(F32)
    base = base2[...]
    for y in range(0, Y2, 2):
        both = [pltpu.roll(base, 8 * s, 1) if s else base for s in (y, min(y + 1, Y2 - 1))]
        w2[8 * y : 8 * y + 16, :] = jnp.concatenate(both, axis=0).astype(BF)


def third_weights(k3, stack3, w3):
    stack3[...] = jnp.zeros(stack3.shape, F32)
    for n, (a, b, c) in enumerate(taps()):
        stack3[8 * n : 8 * n + 8, 0:16] = k3[a, b, c].astype(F32)
    source = iota((256, 1280), 0)
    tap, i = source >> 3, source & 7
    a = (tap * 7282) >> 16
    rest = tap - 9 * a
    b = (rest * 21846) >> 16
    target = jnp.where(tap < 27, a * K3 + (rest - 3 * b) * (8 * Y2) + 8 * b + i, -1)
    base = jnp.dot(
        stack3[...].T[0:16].astype(BF),
        (iota((256, 1280), 1) == target).astype(F32).astype(BF),
        preferred_element_type=F32,
    )
    rows = [pltpu.roll(base, 16 * y, 1) if y else base for y in range(SPAN // 2)]
    by_row = jnp.concatenate(rows, axis=0).astype(BF)
    r = iota((128, 128), 0)
    swap = iota((128, 128), 1) == (r & 7) * 16 + (r >> 3)
    w3[...] = jnp.dot(
        swap.astype(F32).astype(BF), by_row, preferred_element_type=F32
    ).astype(BF)


def third_matmul(x3, first, w3, bias3, out):
    data = jnp.concatenate(
        [x3[h * K3 : (h + 3) * K3, :] for h in (first, first + 2)], axis=1
    )
    sums = jnp.dot(w3[:, 0 : 3 * K3], data, preferred_element_type=F32)
    for n in range(2):
        values = leaky(sums[:, 128 * n : 128 * (n + 1)] + bias3[...])
        out[:, n, :, :] = values[:, 0:64].reshape(16, 8, 64).astype(BF)
        swapped = pltpu.roll(values, 64, 1)
        out[:, n + 2, :, :] = swapped[:, 0:64].reshape(16, 8, 64).astype(BF)


def all_layers(place, cube, arrive, b1, b2, bias3, x1, x2, l2, x3_upper, x3, w1, w2, w3, upper):
    groups, strips, g, t = place
    first_g, last_g = one_if(g > 0), one_if(g < groups - 1)
    first_t, last_t = one_if(t > 0), one_if(t < strips - 1)

    def operand(f):
        pieces = beside(cube[f].reshape(ROWS, 128).astype(F32))
        block = jnp.concatenate([*pieces, jnp.zeros((K1 - 3 * ROWS, 128), F32)], axis=0)
        x1[f * K1 : (f + 1) * K1, :] = block.astype(BF)

    bias1 = column_of(b1, 8 * Y1, 8)
    row = iota((8 * Y1, 128), 0)
    keep1 = jnp.where(row < 16, first_t, jnp.where(row >= 8 * (Y1 - 1), last_t, 1.0))

    def layer_one(*fs):
        data = jnp.concatenate([x1[h * K1 : (h + 3) * K1, :] for h in fs], axis=1)
        sums = jnp.dot(w1[0 : 8 * Y1, 0 : 3 * K1], data, preferred_element_type=F32)
        for n, h in enumerate(fs):
            values = leaky(sums[:, 128 * n : 128 * (n + 1)] + bias1) * keep1
            if h < 2:
                values = values * first_g
            if h == F1 - 1:
                values = values * last_g
            block = jnp.concatenate(
                [*beside(values), jnp.zeros((K2 - 24 * Y1, 128), F32)], axis=0
            )
            x2[h * K2 : (h + 1) * K2, :] = block.astype(BF)

    bias2 = column_of(b2, 8 * Y2, 8)
    keep2 = jnp.where(iota((8 * Y2, 128), 0) < 8, first_t, 1.0)

    def layer_two(*fs):
        data = jnp.concatenate([x2[h * K2 : (h + 3) * K2, :] for h in fs], axis=1)
        sums = jnp.dot(w2[0 : 8 * Y2, 0 : 3 * K2], data, preferred_element_type=F32)
        for n, h in enumerate(fs):
            values = leaky(sums[:, 128 * n : 128 * (n + 1)] + bias2) * keep2
            if h == 0:
                values = values * first_g
            l2[h] = values

    lane = iota((8 * Y2, 128), 1)

    def joined(to, at, f):
        lower, upper = l2[f], l2[f + 4]
        before = jnp.where(lane < 64, pltpu.roll(lower, 65, 1), pltpu.roll(upper, 1, 1))
        block = jnp.concatenate(
            [
                jnp.where((lane & 63) == 0, 0.0, before),
                jnp.where(lane < 64, lower, pltpu.roll(upper, 64, 1)),
                jnp.where(lane < 64, pltpu.roll(lower, 64, 1), upper),
                jnp.zeros((K3 - 24 * Y2, 128), F32),
            ],
            axis=0,
        )
        to[at * K3 : (at + 1) * K3, :] = block.astype(BF)

    arrive("inner")
    for f in range(5, SPAN):
        operand(f)
    for f in (5, 7, 9, 11):
        layer_one(f, f + 1)
    for f in (5, 7, 9):
        layer_two(f, f + 1)
    arrive("upper")
    for f in range(SPAN, PLANES):
        operand(f)
    for f in (13, 15, 17):
        layer_one(f, f + 1)
    for f in (11, 13, 15):
        layer_two(f, f + 1)
    for n in range(5):
        joined(x3_upper, n, 8 + n)
    third_matmul(x3_upper, 0, w3, bias3, upper)
    arrive("lower")
    for f in range(5):
        operand(f)
    layer_one(0, 1)
    layer_one(2, 3)
    layer_one(4)
    layer_two(0, 1)
    layer_two(2, 3)
    layer_two(4)
    for n in range(5):
        joined(x3, n, n)


def spread_kernel(
    sky, k1_in, k2_in, k3_in, b1_in, b2_in, b3_in,
    x3, w3, bias3, upper,
    raw, moved, slab, cube, k1, k2, k3, b1, b2, b3, stack1, base2, stack3, w1, w2, x1, x2, l2, x3_upper,
    in_sem, send_sem, recv_sem,
):
    groups, strips = lax.axis_size("freq"), lax.axis_size("tile")
    g, t = lax.axis_index("freq"), lax.axis_index("tile")
    height = raw.shape[0]

    barrier = pltpu.get_barrier_semaphore()

    def greet(group, strip):
        pl.semaphore_signal(barrier, inc=1, device_id=(group, strip), device_id_type=MESH)

    @pl.when(g < groups - 1)
    def _():
        for strip in (0, 1):
            greet(g + 1, strip)

    @pl.when(g > 0)
    def _():
        for strip in (strips - 3, strips - 2, strips - 1):
            greet(g - 1, strip)

    @pl.loop(1, strips)
    def _(k):
        greet(g, lax.rem(t + k, strips))

    pairs = [(k1_in, k1), (k2_in, k2), (sky.at[0], raw), (k3_in, k3), (b1_in, b1), (b2_in, b2), (b3_in, b3)]
    loads = [pltpu.make_async_copy(a, b, in_sem.at[n]) for n, (a, b) in enumerate(pairs)]
    for load in loads:
        load.start()

    lane = iota((128, 128), 1)
    column = jnp.where(lane < 64, 2 * lane, 2 * lane - 127)
    order = (iota((128, 128), 0) == column).astype(F32).astype(BF)
    moved[0:8, :] = jnp.zeros((8, 128), F32)
    moved[height : height + 16, :] = jnp.zeros((16, 128), F32)
    loads[0].wait()
    loads[1].wait()
    first_weights(k1, k2, stack1, base2, w1, w2)
    loads[2].wait()
    values = jnp.dot(raw[...].astype(BF), order, preferred_element_type=F32)
    moved[4 : height + 4, :] = values
    slab[...] = moved[...].reshape(slab.shape).astype(BF)

    high = t >= strips - 3
    low = t < 2
    beyond = jnp.logical_or(jnp.logical_and(low, g > 0), jnp.logical_and(high, g < groups - 1))
    other = jnp.where(low, jnp.maximum(g - 1, 0), jnp.minimum(g + 1, groups - 1))
    plane = 3 + t
    far_plane = jnp.where(low, SPAN + 3 + t, jnp.maximum(t - (strips - 3), 0))

    @pl.when(beyond)
    def _():
        pl.semaphore_wait(barrier, 2 * strips - 1)

    @pl.when(jnp.logical_not(beyond))
    def _():
        pl.semaphore_wait(barrier, strips - 1)

    def near(k):
        strip = lax.rem(t + k, strips)
        return pltpu.make_async_remote_copy(
            src_ref=slab.at[pl.ds(2 * strip, 3)],
            dst_ref=cube.at[plane],
            send_sem=send_sem.at[k],
            recv_sem=recv_sem.at[plane],
            device_id=(g, strip),
            device_id_type=MESH,
        )

    def far(k):
        pair = k // 2
        strip = lax.rem(pair, 2) * (strips // 2) + pair // 2 * 2 + lax.rem(k, 2)
        return pltpu.make_async_remote_copy(
            src_ref=slab.at[pl.ds(2 * strip, 3)],
            dst_ref=cube.at[far_plane],
            send_sem=send_sem.at[strips + k],
            recv_sem=recv_sem.at[far_plane],
            device_id=(other, strip),
            device_id_type=MESH,
        )

    @pl.when(beyond)
    def _():
        @pl.loop(0, strips)
        def _(k):
            far(k).start()

    @pl.loop(1, strips)
    def _(k):
        near(k).start()

    pltpu.make_async_copy(slab.at[pl.ds(2 * t, 3)], cube.at[plane], recv_sem.at[plane]).start()

    for load in loads[3:]:
        load.wait()
    third_weights(k3, stack3, w3)
    for o in range(16):
        bias3[8 * o : 8 * o + 8, :] = jnp.full((8, 128), b3[o], F32)

    def arrived(p):
        pltpu.make_async_copy(cube.at[p], cube.at[p], recv_sem.at[p]).wait()

    def arrive(side):
        if side == "inner":
            @pl.loop(5, SPAN)
            def _(p):
                arrived(p)
        elif side == "upper":
            for p in (SPAN, SPAN + 1, SPAN + 2):
                arrived(p)

            @pl.when(g < groups - 1)
            def _():
                for p in (SPAN + 3, SPAN + 4):
                    arrived(p)

            @pl.when(g == groups - 1)
            def _():
                cube[SPAN + 3 : SPAN + 5] = jnp.zeros((2, 3, 8, 128), BF)
        else:
            for p in (3, 4):
                arrived(p)

            @pl.when(g > 0)
            def _():
                for p in range(3):
                    arrived(p)

            @pl.when(g == 0)
            def _():
                cube[0:3] = jnp.zeros((3, 3, 8, 128), BF)

    all_layers(
        (groups, strips, g, t), cube, arrive, b1, b2, bias3, x1, x2, l2, x3_upper, x3, w1, w2, w3, upper
    )

    @pl.loop(1, strips)
    def _(k):
        near(k).wait_send()

    @pl.when(beyond)
    def _():
        @pl.loop(0, strips)
        def _(k):
            far(k).wait_send()


X3_SHAPE = (5 * K3, 128)
HALF_SHAPE = (16, SPAN // 4, SPAN // 2, 64)
WEIGHT_SCRATCH = [
    pltpu.VMEM((128, 128), F32),
    pltpu.VMEM((8, 1408), F32),
    pltpu.VMEM((256, 128), F32),
    pltpu.VMEM((160, 256), BF),
    pltpu.VMEM((144, 1408), BF),
]
LAYER_SCRATCH = [
    pltpu.VMEM((PLANES * K1, 128), BF),
    pltpu.VMEM((F1 * K2, 128), BF),
    pltpu.VMEM((F2, 8 * Y2, 128), F32),
    pltpu.VMEM(X3_SHAPE, BF),
]


def first_layers(sky_cube, k1, k2, k3, b1, b2, b3):
    height = sky_cube.shape[1]
    strips = height // SPAN
    operands = [
        pltpu.with_memory_space_constraint(x, pltpu.HBM)
        for x in (sky_cube, k1, k2, k3, b1, b2, b3)
    ]
    vmem = pl.BlockSpec(memory_space=pltpu.VMEM)
    return pl.pallas_call(
        spread_kernel,
        out_shape=[
            jax.ShapeDtypeStruct(X3_SHAPE, BF),
            jax.ShapeDtypeStruct((128, 1280), BF),
            jax.ShapeDtypeStruct((128, 128), F32),
            jax.ShapeDtypeStruct(HALF_SHAPE, BF),
        ],
        in_specs=[pl.BlockSpec(memory_space=pltpu.HBM)] * len(operands),
        out_specs=[vmem] * 4,
        scratch_shapes=[
            pltpu.VMEM((height, 128), F32),
            pltpu.VMEM((height + 16, 128), F32),
            pltpu.VMEM(((height + 16) // 8, 8, 128), BF),
            pltpu.VMEM((PLANES, 3, 8, 128), BF),
            pltpu.VMEM(k1.shape, BF),
            pltpu.VMEM(k2.shape, BF),
            pltpu.VMEM(k3.shape, BF),
            pltpu.SMEM(b1.shape, F32),
            pltpu.SMEM(b2.shape, F32),
            pltpu.SMEM(b3.shape, F32),
            *WEIGHT_SCRATCH,
            *LAYER_SCRATCH,
            pltpu.SemaphoreType.DMA((len(operands),)),
            pltpu.SemaphoreType.DMA((2 * strips,)),
            pltpu.SemaphoreType.DMA((PLANES,)),
        ],
        compiler_params=pltpu.CompilerParams(
            collective_id=0, has_side_effects=True, vmem_limit_bytes=24 << 20
        ),
        name="first_layers",
    )(*operands)


def third_kernel(x3, w3, bias3, upper, out, lower, sem):
    quarter = SPAN // 4
    done = pltpu.make_async_copy(upper, out.at[:, quarter : 2 * quarter], sem.at[0])
    done.start()
    third_matmul(x3, 0, w3, bias3, lower)
    rest = pltpu.make_async_copy(lower, out.at[:, 0:quarter], sem.at[1])
    rest.start()
    done.wait()
    rest.wait()


def third_layer(x3, w3, bias3, upper):
    vmem = pl.BlockSpec(memory_space=pltpu.VMEM)
    half = SPAN // 2
    return pl.pallas_call(
        third_kernel,
        out_shape=jax.ShapeDtypeStruct((16, half, half, 64), BF),
        in_specs=[vmem] * 4,
        out_specs=pl.BlockSpec(memory_space=pl.ANY),
        scratch_shapes=[pltpu.VMEM(HALF_SHAPE, BF), pltpu.SemaphoreType.DMA((2,))],
        compiler_params=pltpu.CompilerParams(vmem_limit_bytes=8 << 20),
        name="third_layer",
    )(x3, w3, bias3, upper)


def body(sky_cube, kernel_one, bias_one, kernel_two, bias_two, kernel_three, bias_three):
    return third_layer(
        *first_layers(
            sky_cube,
            kernel_one.transpose(1, 2, 3, 4, 0),
            kernel_two.transpose(2, 3, 4, 0, 1),
            kernel_three.transpose(2, 3, 4, 1, 0),
            bias_one,
            bias_two,
            bias_three,
        )
    )


def solution(mesh):
    return jax.shard_map(
        body,
        mesh=mesh,
        in_specs=(P(("freq", "tile"), None, None), P(), P(), P(), P(), P(), P()),
        out_specs=P(None, "freq", "tile", None),
        check_vma=False,
    )
```

```python
import jax
import jax.numpy as jnp
from jax import lax
from jax.experimental import pallas as pl
from jax.experimental.pallas import tpu as pltpu
from jax.sharding import PartitionSpec as P

MESH = pl.DeviceIdType.MESH
BF = jnp.bfloat16
F32 = jnp.float32

SPAN = 16
PLANES = SPAN + 5
ROWS = 24
F1, Y1 = SPAN + 3, SPAN + 3
F2, Y2 = SPAN + 1, SPAN + 1
K1 = 80
K2 = 464
K3 = 416


def iota(shape, dim):
    return lax.broadcasted_iota(jnp.int32, shape, dim)


def leaky(values):
    return jnp.maximum(values, 0.1 * values)


def beside(values):
    lane = iota(values.shape, 1)
    swapped = pltpu.roll(values, 64, 1)
    before = jnp.where(lane < 64, pltpu.roll(values, 65, 1), swapped)
    after = jnp.where(lane < 64, swapped, pltpu.roll(values, 63, 1))
    return (
        jnp.where(lane == 0, 0.0, before),
        values,
        jnp.where(lane == 127, 0.0, after),
    )


def column_of(bias, rows, count):
    row = iota((count, 128), 0)
    block = jnp.zeros((count, 128), F32)
    for o in range(count):
        block = jnp.where(row == o, bias[o], block)
    return jnp.concatenate([block] * (rows // count), axis=0)


def taps():
    return [(a, b, c) for a in range(3) for b in range(3) for c in range(3)]


def one_if(inside):
    return jnp.where(inside, 1.0, 0.0).astype(F32)


def banded_weights(k1, k2, k3, stack1, base2, stack3, w1, w2, w3):
    stack1[...] = jnp.zeros(stack1.shape, F32)
    for a in range(3):
        for b in range(3):
            at = 8 * (3 * a + b)
            stack1[at : at + 3, 0:8] = k1[0, a, b].astype(F32)
    source = iota((128, 256), 0)
    tap, c = source >> 3, source & 7
    a = (tap * 21846) >> 16
    target = jnp.where((tap < 9) & (c < 3), a * K1 + c * ROWS + 1 + tap - 3 * a, -1)
    base = jnp.dot(
        stack1[...].T[0:8].astype(BF),
        (iota((128, 256), 1) == target).astype(F32).astype(BF),
        preferred_element_type=F32,
    )
    for y in range(0, Y1, 2):
        both = [pltpu.roll(base, s, 1) if s else base for s in (y, y + 1)]
        w1[8 * y : 8 * y + 16, :] = jnp.concatenate(both, axis=0).astype(BF)

    base2[...] = jnp.zeros(base2.shape, F32)
    for a, b, c in taps():
        at = a * K2 + c * (8 * Y1) + 8 * b
        base2[:, at : at + 8] = k2[a, b, c].astype(F32)
    base = base2[...]
    for y in range(0, Y2, 2):
        both = [pltpu.roll(base, 8 * s, 1) if s else base for s in (y, min(y + 1, Y2 - 1))]
        w2[8 * y : 8 * y + 16, :] = jnp.concatenate(both, axis=0).astype(BF)

    stack3[...] = jnp.zeros(stack3.shape, F32)
    for n, (a, b, c) in enumerate(taps()):
        stack3[8 * n : 8 * n + 8, 0:16] = k3[a, b, c].astype(F32)
    source = iota((256, 1280), 0)
    tap, i = source >> 3, source & 7
    a = (tap * 7282) >> 16
    rest = tap - 9 * a
    b = (rest * 21846) >> 16
    target = jnp.where(tap < 27, a * K3 + (rest - 3 * b) * (8 * Y2) + 8 * b + i, -1)
    base = jnp.dot(
        stack3[...].T[0:16].astype(BF),
        (iota((256, 1280), 1) == target).astype(F32).astype(BF),
        preferred_element_type=F32,
    )
    rows = [pltpu.roll(base, 16 * y, 1) if y else base for y in range(SPAN // 2)]
    by_row = jnp.concatenate(rows, axis=0).astype(BF)
    r = iota((128, 128), 0)
    swap = iota((128, 128), 1) == (r & 7) * 16 + (r >> 3)
    w3[...] = jnp.dot(
        swap.astype(F32).astype(BF), by_row, preferred_element_type=F32
    ).astype(BF)


def third_matmul(x3, first, w3, bias3, out):
    data = jnp.concatenate(
        [x3[h * K3 : (h + 3) * K3, :] for h in (first, first + 2)], axis=1
    )
    sums = jnp.dot(w3[:, 0 : 3 * K3], data, preferred_element_type=F32)
    for n in range(2):
        values = leaky(sums[:, 128 * n : 128 * (n + 1)] + bias3[...])
        out[:, n, :, :] = values[:, 0:64].reshape(16, 8, 64).astype(BF)
        swapped = pltpu.roll(values, 64, 1)
        out[:, n + 2, :, :] = swapped[:, 0:64].reshape(16, 8, 64).astype(BF)


def all_layers(place, cube, arrive, b1, b2, bias3, x1, x2, l2, x3_upper, x3, w1, w2, w3, upper):
    groups, strips, g, t = place
    first_g, last_g = one_if(g > 0), one_if(g < groups - 1)
    first_t, last_t = one_if(t > 0), one_if(t < strips - 1)

    def operand(f):
        pieces = beside(cube[f].reshape(ROWS, 128).astype(F32))
        block = jnp.concatenate([*pieces, jnp.zeros((K1 - 3 * ROWS, 128), F32)], axis=0)
        x1[f * K1 : (f + 1) * K1, :] = block.astype(BF)

    bias1 = column_of(b1, 8 * Y1, 8)
    row = iota((8 * Y1, 128), 0)
    keep1 = jnp.where(row < 16, first_t, jnp.where(row >= 8 * (Y1 - 1), last_t, 1.0))

    def layer_one(*fs):
        data = jnp.concatenate([x1[h * K1 : (h + 3) * K1, :] for h in fs], axis=1)
        sums = jnp.dot(w1[0 : 8 * Y1, 0 : 3 * K1], data, preferred_element_type=F32)
        for n, h in enumerate(fs):
            values = leaky(sums[:, 128 * n : 128 * (n + 1)] + bias1) * keep1
            if h < 2:
                values = values * first_g
            if h == F1 - 1:
                values = values * last_g
            block = jnp.concatenate(
                [*beside(values), jnp.zeros((K2 - 24 * Y1, 128), F32)], axis=0
            )
            x2[h * K2 : (h + 1) * K2, :] = block.astype(BF)

    bias2 = column_of(b2, 8 * Y2, 8)
    keep2 = jnp.where(iota((8 * Y2, 128), 0) < 8, first_t, 1.0)

    def layer_two(*fs):
        data = jnp.concatenate([x2[h * K2 : (h + 3) * K2, :] for h in fs], axis=1)
        sums = jnp.dot(w2[0 : 8 * Y2, 0 : 3 * K2], data, preferred_element_type=F32)
        for n, h in enumerate(fs):
            values = leaky(sums[:, 128 * n : 128 * (n + 1)] + bias2) * keep2
            if h == 0:
                values = values * first_g
            l2[h] = values

    lane = iota((8 * Y2, 128), 1)

    def joined(to, at, f):
        lower, upper = l2[f], l2[f + 4]
        before = jnp.where(lane < 64, pltpu.roll(lower, 65, 1), pltpu.roll(upper, 1, 1))
        block = jnp.concatenate(
            [
                jnp.where((lane & 63) == 0, 0.0, before),
                jnp.where(lane < 64, lower, pltpu.roll(upper, 64, 1)),
                jnp.where(lane < 64, pltpu.roll(lower, 64, 1), upper),
                jnp.zeros((K3 - 24 * Y2, 128), F32),
            ],
            axis=0,
        )
        to[at * K3 : (at + 1) * K3, :] = block.astype(BF)

    arrive("inner")
    for f in range(5, SPAN):
        operand(f)
    for f in (5, 7, 9, 11):
        layer_one(f, f + 1)
    for f in (5, 7, 9):
        layer_two(f, f + 1)
    arrive("upper")
    for f in range(SPAN, PLANES):
        operand(f)
    for f in (13, 15, 17):
        layer_one(f, f + 1)
    for f in (11, 13, 15):
        layer_two(f, f + 1)
    for n in range(5):
        joined(x3_upper, n, 8 + n)
    third_matmul(x3_upper, 0, w3, bias3, upper)
    arrive("lower")
    for f in range(5):
        operand(f)
    layer_one(0, 1)
    layer_one(2, 3)
    layer_one(4)
    layer_two(0, 1)
    layer_two(2, 3)
    layer_two(4)
    for n in range(5):
        joined(x3, n, n)


def spread_kernel(
    sky, k1_in, k2_in, k3_in, b1_in, b2_in, b3_in,
    x3, w3, bias3, upper,
    raw, moved, slab, cube, k1, k2, k3, b1, b2, b3, stack1, base2, stack3, w1, w2, x1, x2, l2, x3_upper,
    in_sem, send_sem, recv_sem,
):
    groups, strips = lax.axis_size("freq"), lax.axis_size("tile")
    g, t = lax.axis_index("freq"), lax.axis_index("tile")
    height = raw.shape[0]

    barrier = pltpu.get_barrier_semaphore()

    def greet(group, strip):
        pl.semaphore_signal(barrier, inc=1, device_id=(group, strip), device_id_type=MESH)

    @pl.when(g < groups - 1)
    def _():
        for strip in (0, 1):
            greet(g + 1, strip)

    @pl.when(g > 0)
    def _():
        for strip in (strips - 3, strips - 2, strips - 1):
            greet(g - 1, strip)

    @pl.loop(1, strips)
    def _(k):
        greet(g, lax.rem(t + k, strips))

    pairs = [(sky.at[0], raw), (k1_in, k1), (k2_in, k2), (k3_in, k3), (b1_in, b1), (b2_in, b2), (b3_in, b3)]
    loads = [pltpu.make_async_copy(a, b, in_sem.at[n]) for n, (a, b) in enumerate(pairs)]
    for load in loads:
        load.start()

    lane = iota((128, 128), 1)
    column = jnp.where(lane < 64, 2 * lane, 2 * lane - 127)
    order = (iota((128, 128), 0) == column).astype(F32).astype(BF)
    moved[0:8, :] = jnp.zeros((8, 128), F32)
    moved[height : height + 16, :] = jnp.zeros((16, 128), F32)
    loads[0].wait()
    values = jnp.dot(raw[...].astype(BF), order, preferred_element_type=F32)
    moved[4 : height + 4, :] = values
    slab[...] = moved[...].reshape(slab.shape).astype(BF)

    high = t >= strips - 3
    low = t < 2
    beyond = jnp.logical_or(jnp.logical_and(low, g > 0), jnp.logical_and(high, g < groups - 1))
    other = jnp.where(low, jnp.maximum(g - 1, 0), jnp.minimum(g + 1, groups - 1))
    plane = 3 + t
    far_plane = jnp.where(low, SPAN + 3 + t, jnp.maximum(t - (strips - 3), 0))

    def near(k):
        strip = lax.rem(t + k, strips)
        return pltpu.make_async_remote_copy(
            src_ref=slab.at[pl.ds(2 * strip, 3)],
            dst_ref=cube.at[plane],
            send_sem=send_sem.at[k],
            recv_sem=recv_sem.at[plane],
            device_id=(g, strip),
            device_id_type=MESH,
        )

    def far(k):
        pair = k // 2
        strip = lax.rem(pair, 2) * (strips // 2) + pair // 2 * 2 + lax.rem(k, 2)
        return pltpu.make_async_remote_copy(
            src_ref=slab.at[pl.ds(2 * strip, 3)],
            dst_ref=cube.at[far_plane],
            send_sem=send_sem.at[strips + k],
            recv_sem=recv_sem.at[far_plane],
            device_id=(other, strip),
            device_id_type=MESH,
        )

    late = jnp.logical_and(jnp.logical_and(low, g > 0), lax.rem(g, 4) == 0)
    expand_at = jnp.where(late, 0, 1)

    @pl.loop(0, 2)
    def _(turn):
        @pl.when(turn == expand_at)
        def _():
            for load in loads[1:]:
                load.wait()
            banded_weights(k1, k2, k3, stack1, base2, stack3, w1, w2, w3)
            for o in range(16):
                bias3[8 * o : 8 * o + 8, :] = jnp.full((8, 128), b3[o], F32)

        @pl.when(jnp.logical_and(turn == 0, beyond))
        def _():
            pl.semaphore_wait(barrier, 2 * strips - 1)

            @pl.loop(0, strips)
            def _(k):
                far(k).start()

        @pl.when(jnp.logical_and(turn == 0, jnp.logical_not(beyond)))
        def _():
            pl.semaphore_wait(barrier, strips - 1)

        @pl.when(turn == 0)
        def _():
            @pl.loop(1, strips)
            def _(k):
                near(k).start()

            own = slab.at[pl.ds(2 * t, 3)]
            pltpu.make_async_copy(own, cube.at[plane], recv_sem.at[plane]).start()

    def arrived(p):
        pltpu.make_async_copy(cube.at[p], cube.at[p], recv_sem.at[p]).wait()

    def arrive(side):
        if side == "inner":
            @pl.loop(5, SPAN)
            def _(p):
                arrived(p)
        elif side == "upper":
            for p in (SPAN, SPAN + 1, SPAN + 2):
                arrived(p)

            @pl.when(g < groups - 1)
            def _():
                for p in (SPAN + 3, SPAN + 4):
                    arrived(p)

            @pl.when(g == groups - 1)
            def _():
                cube[SPAN + 3 : SPAN + 5] = jnp.zeros((2, 3, 8, 128), BF)
        else:
            for p in (3, 4):
                arrived(p)

            @pl.when(g > 0)
            def _():
                for p in range(3):
                    arrived(p)

            @pl.when(g == 0)
            def _():
                cube[0:3] = jnp.zeros((3, 3, 8, 128), BF)

    all_layers(
        (groups, strips, g, t), cube, arrive, b1, b2, bias3, x1, x2, l2, x3_upper, x3, w1, w2, w3, upper
    )

    @pl.loop(1, strips)
    def _(k):
        near(k).wait_send()

    @pl.when(beyond)
    def _():
        @pl.loop(0, strips)
        def _(k):
            far(k).wait_send()


X3_SHAPE = (5 * K3, 128)
HALF_SHAPE = (16, SPAN // 4, SPAN // 2, 64)
WEIGHT_SCRATCH = [
    pltpu.VMEM((128, 128), F32),
    pltpu.VMEM((8, 1408), F32),
    pltpu.VMEM((256, 128), F32),
    pltpu.VMEM((160, 256), BF),
    pltpu.VMEM((144, 1408), BF),
]
LAYER_SCRATCH = [
    pltpu.VMEM((PLANES * K1, 128), BF),
    pltpu.VMEM((F1 * K2, 128), BF),
    pltpu.VMEM((F2, 8 * Y2, 128), F32),
    pltpu.VMEM(X3_SHAPE, BF),
]


def first_layers(sky_cube, k1, k2, k3, b1, b2, b3):
    height = sky_cube.shape[1]
    strips = height // SPAN
    operands = [
        pltpu.with_memory_space_constraint(x, pltpu.HBM)
        for x in (sky_cube, k1, k2, k3, b1, b2, b3)
    ]
    vmem = pl.BlockSpec(memory_space=pltpu.VMEM)
    return pl.pallas_call(
        spread_kernel,
        out_shape=[
            jax.ShapeDtypeStruct(X3_SHAPE, BF),
            jax.ShapeDtypeStruct((128, 1280), BF),
            jax.ShapeDtypeStruct((128, 128), F32),
            jax.ShapeDtypeStruct(HALF_SHAPE, BF),
        ],
        in_specs=[pl.BlockSpec(memory_space=pltpu.HBM)] * len(operands),
        out_specs=[vmem] * 4,
        scratch_shapes=[
            pltpu.VMEM((height, 128), F32),
            pltpu.VMEM((height + 16, 128), F32),
            pltpu.VMEM(((height + 16) // 8, 8, 128), BF),
            pltpu.VMEM((PLANES, 3, 8, 128), BF),
            pltpu.VMEM(k1.shape, BF),
            pltpu.VMEM(k2.shape, BF),
            pltpu.VMEM(k3.shape, BF),
            pltpu.SMEM(b1.shape, F32),
            pltpu.SMEM(b2.shape, F32),
            pltpu.SMEM(b3.shape, F32),
            *WEIGHT_SCRATCH,
            *LAYER_SCRATCH,
            pltpu.SemaphoreType.DMA((len(operands),)),
            pltpu.SemaphoreType.DMA((2 * strips,)),
            pltpu.SemaphoreType.DMA((PLANES,)),
        ],
        compiler_params=pltpu.CompilerParams(
            collective_id=0, has_side_effects=True, vmem_limit_bytes=24 << 20
        ),
        name="first_layers",
    )(*operands)


def third_kernel(x3, w3, bias3, upper, out, lower, sem):
    quarter = SPAN // 4
    done = pltpu.make_async_copy(upper, out.at[:, quarter : 2 * quarter], sem.at[0])
    done.start()
    third_matmul(x3, 0, w3, bias3, lower)
    rest = pltpu.make_async_copy(lower, out.at[:, 0:quarter], sem.at[1])
    rest.start()
    done.wait()
    rest.wait()


def third_layer(x3, w3, bias3, upper):
    vmem = pl.BlockSpec(memory_space=pltpu.VMEM)
    half = SPAN // 2
    return pl.pallas_call(
        third_kernel,
        out_shape=jax.ShapeDtypeStruct((16, half, half, 64), BF),
        in_specs=[vmem] * 4,
        out_specs=pl.BlockSpec(memory_space=pl.ANY),
        scratch_shapes=[pltpu.VMEM(HALF_SHAPE, BF), pltpu.SemaphoreType.DMA((2,))],
        compiler_params=pltpu.CompilerParams(vmem_limit_bytes=8 << 20),
        name="third_layer",
    )(x3, w3, bias3, upper)


def body(sky_cube, kernel_one, bias_one, kernel_two, bias_two, kernel_three, bias_three):
    return third_layer(
        *first_layers(
            sky_cube,
            kernel_one.transpose(1, 2, 3, 4, 0),
            kernel_two.transpose(2, 3, 4, 0, 1),
            kernel_three.transpose(2, 3, 4, 1, 0),
            bias_one,
            bias_two,
            bias_three,
        )
    )


def solution(mesh):
    return jax.shard_map(
        body,
        mesh=mesh,
        in_specs=(P(("freq", "tile"), None, None), P(), P(), P(), P(), P(), P()),
        out_specs=P(None, "freq", "tile", None),
        check_vma=False,
    )
```

```python
import jax
import jax.numpy as jnp
from jax import lax
from jax.experimental import pallas as pl
from jax.experimental.pallas import tpu as pltpu
from jax.sharding import PartitionSpec as P

MESH = pl.DeviceIdType.MESH
BF = jnp.bfloat16
F32 = jnp.float32

SPAN = 16
PLANES = SPAN + 5
ROWS = 24
F1, Y1 = SPAN + 3, SPAN + 3
F2, Y2 = SPAN + 1, SPAN + 1
K1 = 80
K2 = 464
K3 = 416


def iota(shape, dim):
    return lax.broadcasted_iota(jnp.int32, shape, dim)


def leaky(values):
    return jnp.maximum(values, 0.1 * values)


def beside(values):
    lane = iota(values.shape, 1)
    swapped = pltpu.roll(values, 64, 1)
    before = jnp.where(lane < 64, pltpu.roll(values, 65, 1), swapped)
    after = jnp.where(lane < 64, swapped, pltpu.roll(values, 63, 1))
    return (
        jnp.where(lane == 0, 0.0, before),
        values,
        jnp.where(lane == 127, 0.0, after),
    )


def column_of(bias, rows, count):
    row = iota((count, 128), 0)
    block = jnp.zeros((count, 128), F32)
    for o in range(count):
        block = jnp.where(row == o, bias[o], block)
    return jnp.concatenate([block] * (rows // count), axis=0)


def taps():
    return [(a, b, c) for a in range(3) for b in range(3) for c in range(3)]


def one_if(inside):
    return jnp.where(inside, 1.0, 0.0).astype(F32)


def banded_weights(k1, k2, k3, stack1, base2, stack3, w1, w2, w3):
    stack1[...] = jnp.zeros(stack1.shape, F32)
    for a in range(3):
        for b in range(3):
            at = 8 * (3 * a + b)
            stack1[at : at + 3, 0:8] = k1[0, a, b].astype(F32)
    source = iota((128, 256), 0)
    tap, c = source >> 3, source & 7
    a = (tap * 21846) >> 16
    target = jnp.where((tap < 9) & (c < 3), a * K1 + c * ROWS + 1 + tap - 3 * a, -1)
    base = jnp.dot(
        stack1[...].T[0:8].astype(BF),
        (iota((128, 256), 1) == target).astype(F32).astype(BF),
        preferred_element_type=F32,
    )
    for y in range(0, Y1, 2):
        both = [pltpu.roll(base, s, 1) if s else base for s in (y, y + 1)]
        w1[8 * y : 8 * y + 16, :] = jnp.concatenate(both, axis=0).astype(BF)

    base2[...] = jnp.zeros(base2.shape, F32)
    for a, b, c in taps():
        at = a * K2 + c * (8 * Y1) + 8 * b
        base2[:, at : at + 8] = k2[a, b, c].astype(F32)
    base = base2[...]
    for y in range(0, Y2, 2):
        both = [pltpu.roll(base, 8 * s, 1) if s else base for s in (y, min(y + 1, Y2 - 1))]
        w2[8 * y : 8 * y + 16, :] = jnp.concatenate(both, axis=0).astype(BF)

    stack3[...] = jnp.zeros(stack3.shape, F32)
    for n, (a, b, c) in enumerate(taps()):
        stack3[8 * n : 8 * n + 8, 0:16] = k3[a, b, c].astype(F32)
    source = iota((256, 1280), 0)
    tap, i = source >> 3, source & 7
    a = (tap * 7282) >> 16
    rest = tap - 9 * a
    b = (rest * 21846) >> 16
    target = jnp.where(tap < 27, a * K3 + (rest - 3 * b) * (8 * Y2) + 8 * b + i, -1)
    base = jnp.dot(
        stack3[...].T[0:16].astype(BF),
        (iota((256, 1280), 1) == target).astype(F32).astype(BF),
        preferred_element_type=F32,
    )
    rows = [pltpu.roll(base, 16 * y, 1) if y else base for y in range(SPAN // 2)]
    by_row = jnp.concatenate(rows, axis=0).astype(BF)
    r = iota((128, 128), 0)
    swap = iota((128, 128), 1) == (r & 7) * 16 + (r >> 3)
    w3[...] = jnp.dot(
        swap.astype(F32).astype(BF), by_row, preferred_element_type=F32
    ).astype(BF)


def third_matmul(x3, first, w3, bias3, out):
    data = jnp.concatenate(
        [x3[h * K3 : (h + 3) * K3, :] for h in (first, first + 2)], axis=1
    )
    sums = jnp.dot(w3[:, 0 : 3 * K3], data, preferred_element_type=F32)
    for n in range(2):
        values = leaky(sums[:, 128 * n : 128 * (n + 1)] + bias3[...])
        out[:, n, :, :] = values[:, 0:64].reshape(16, 8, 64).astype(BF)
        swapped = pltpu.roll(values, 64, 1)
        out[:, n + 2, :, :] = swapped[:, 0:64].reshape(16, 8, 64).astype(BF)


def all_layers(place, cube, arrive, b1, b2, bias3, x1, x2, l2, x3_upper, x3, w1, w2, w3, upper):
    groups, strips, g, t = place
    first_g, last_g = one_if(g > 0), one_if(g < groups - 1)
    first_t, last_t = one_if(t > 0), one_if(t < strips - 1)

    def operand(f):
        pieces = beside(cube[f].reshape(ROWS, 128).astype(F32))
        block = jnp.concatenate([*pieces, jnp.zeros((K1 - 3 * ROWS, 128), F32)], axis=0)
        x1[f * K1 : (f + 1) * K1, :] = block.astype(BF)

    bias1 = column_of(b1, 8 * Y1, 8)
    row = iota((8 * Y1, 128), 0)
    keep1 = jnp.where(row < 16, first_t, jnp.where(row >= 8 * (Y1 - 1), last_t, 1.0))

    def layer_one(*fs):
        data = jnp.concatenate([x1[h * K1 : (h + 3) * K1, :] for h in fs], axis=1)
        sums = jnp.dot(w1[0 : 8 * Y1, 0 : 3 * K1], data, preferred_element_type=F32)
        for n, h in enumerate(fs):
            values = leaky(sums[:, 128 * n : 128 * (n + 1)] + bias1) * keep1
            if h < 2:
                values = values * first_g
            if h == F1 - 1:
                values = values * last_g
            block = jnp.concatenate(
                [*beside(values), jnp.zeros((K2 - 24 * Y1, 128), F32)], axis=0
            )
            x2[h * K2 : (h + 1) * K2, :] = block.astype(BF)

    bias2 = column_of(b2, 8 * Y2, 8)
    keep2 = jnp.where(iota((8 * Y2, 128), 0) < 8, first_t, 1.0)

    def layer_two(*fs):
        data = jnp.concatenate([x2[h * K2 : (h + 3) * K2, :] for h in fs], axis=1)
        sums = jnp.dot(w2[0 : 8 * Y2, 0 : 3 * K2], data, preferred_element_type=F32)
        for n, h in enumerate(fs):
            values = leaky(sums[:, 128 * n : 128 * (n + 1)] + bias2) * keep2
            if h == 0:
                values = values * first_g
            l2[h] = values

    lane = iota((8 * Y2, 128), 1)

    def joined(to, at, f):
        lower, upper = l2[f], l2[f + 4]
        before = jnp.where(lane < 64, pltpu.roll(lower, 65, 1), pltpu.roll(upper, 1, 1))
        block = jnp.concatenate(
            [
                jnp.where((lane & 63) == 0, 0.0, before),
                jnp.where(lane < 64, lower, pltpu.roll(upper, 64, 1)),
                jnp.where(lane < 64, pltpu.roll(lower, 64, 1), upper),
                jnp.zeros((K3 - 24 * Y2, 128), F32),
            ],
            axis=0,
        )
        to[at * K3 : (at + 1) * K3, :] = block.astype(BF)

    arrive("inner")
    for f in range(5, SPAN):
        operand(f)
    for f in (5, 7, 9, 11):
        layer_one(f, f + 1)
    for f in (5, 7, 9):
        layer_two(f, f + 1)
    arrive("upper")
    for f in range(SPAN, PLANES):
        operand(f)
    for f in (13, 15, 17):
        layer_one(f, f + 1)
    for f in (11, 13, 15):
        layer_two(f, f + 1)
    for n in range(5):
        joined(x3_upper, n, 8 + n)
    third_matmul(x3_upper, 0, w3, bias3, upper)
    arrive("lower")
    for f in range(5):
        operand(f)
    layer_one(0, 1)
    layer_one(2, 3)
    layer_one(4)
    layer_two(0, 1)
    layer_two(2, 3)
    layer_two(4)
    for n in range(5):
        joined(x3, n, n)


def spread_kernel(
    sky, k1_in, k2_in, k3_in, b1_in, b2_in, b3_in,
    x3, w3, bias3, upper,
    raw, moved, slab, cube, k1, k2, k3, b1, b2, b3, stack1, base2, stack3, w1, w2, x1, x2, l2, x3_upper,
    in_sem, send_sem, recv_sem,
):
    groups, strips = lax.axis_size("freq"), lax.axis_size("tile")
    g, t = lax.axis_index("freq"), lax.axis_index("tile")
    height = raw.shape[0]

    barrier = pltpu.get_barrier_semaphore()

    def greet(group, strip):
        pl.semaphore_signal(barrier, inc=1, device_id=(group, strip), device_id_type=MESH)

    @pl.when(g < groups - 1)
    def _():
        for strip in (0, 1):
            greet(g + 1, strip)

    @pl.when(g > 0)
    def _():
        for strip in (strips - 3, strips - 2, strips - 1):
            greet(g - 1, strip)

    @pl.loop(1, strips)
    def _(k):
        greet(g, lax.rem(t + k, strips))

    pairs = [(sky.at[0], raw), (k1_in, k1), (k2_in, k2), (k3_in, k3), (b1_in, b1), (b2_in, b2), (b3_in, b3)]
    loads = [pltpu.make_async_copy(a, b, in_sem.at[n]) for n, (a, b) in enumerate(pairs)]
    for load in loads:
        load.start()

    lane = iota((128, 128), 1)
    column = jnp.where(lane < 64, 2 * lane, 2 * lane - 127)
    order = (iota((128, 128), 0) == column).astype(F32).astype(BF)
    moved[0:8, :] = jnp.zeros((8, 128), F32)
    moved[height : height + 16, :] = jnp.zeros((16, 128), F32)
    loads[0].wait()
    values = jnp.dot(raw[...].astype(BF), order, preferred_element_type=F32)
    moved[4 : height + 4, :] = values
    slab[...] = moved[...].reshape(slab.shape).astype(BF)

    high = t >= strips - 3
    low = t < 2
    beyond = jnp.logical_or(jnp.logical_and(low, g > 0), jnp.logical_and(high, g < groups - 1))
    other = jnp.where(low, jnp.maximum(g - 1, 0), jnp.minimum(g + 1, groups - 1))
    plane = 3 + t
    far_plane = jnp.where(low, SPAN + 3 + t, jnp.maximum(t - (strips - 3), 0))

    def near(k):
        strip = lax.rem(t + k, strips)
        return pltpu.make_async_remote_copy(
            src_ref=slab.at[pl.ds(2 * strip, 3)],
            dst_ref=cube.at[plane],
            send_sem=send_sem.at[k],
            recv_sem=recv_sem.at[plane],
            device_id=(g, strip),
            device_id_type=MESH,
        )

    def far(k):
        pair = k // 2
        far_z = jnp.logical_or(pair == 1, pair >= 5)
        y = pair - jnp.where(pair >= 5, 4, jnp.where(pair >= 1, 1, 0))
        strip = jnp.where(far_z, strips // 2, 0) + 2 * y + lax.rem(k, 2)
        return pltpu.make_async_remote_copy(
            src_ref=slab.at[pl.ds(2 * strip, 3)],
            dst_ref=cube.at[far_plane],
            send_sem=send_sem.at[strips + k],
            recv_sem=recv_sem.at[far_plane],
            device_id=(other, strip),
            device_id_type=MESH,
        )

    late = jnp.logical_and(jnp.logical_and(low, g > 0), lax.rem(g, 4) == 0)
    expand_at = jnp.where(late, 0, 1)

    @pl.loop(0, 2)
    def _(turn):
        @pl.when(turn == expand_at)
        def _():
            for load in loads[1:]:
                load.wait()
            banded_weights(k1, k2, k3, stack1, base2, stack3, w1, w2, w3)
            for o in range(16):
                bias3[8 * o : 8 * o + 8, :] = jnp.full((8, 128), b3[o], F32)

        @pl.when(jnp.logical_and(turn == 0, beyond))
        def _():
            pl.semaphore_wait(barrier, 2 * strips - 1)

            @pl.loop(0, strips)
            def _(k):
                far(k).start()

        @pl.when(jnp.logical_and(turn == 0, jnp.logical_not(beyond)))
        def _():
            pl.semaphore_wait(barrier, strips - 1)

        @pl.when(turn == 0)
        def _():
            @pl.loop(1, strips)
            def _(k):
                near(k).start()

            own = slab.at[pl.ds(2 * t, 3)]
            pltpu.make_async_copy(own, cube.at[plane], recv_sem.at[plane]).start()

    def arrived(p):
        pltpu.make_async_copy(cube.at[p], cube.at[p], recv_sem.at[p]).wait()

    def arrive(side):
        if side == "inner":
            @pl.loop(5, SPAN)
            def _(p):
                arrived(p)
        elif side == "upper":
            for p in (SPAN, SPAN + 1, SPAN + 2):
                arrived(p)

            @pl.when(g < groups - 1)
            def _():
                for p in (SPAN + 3, SPAN + 4):
                    arrived(p)

            @pl.when(g == groups - 1)
            def _():
                cube[SPAN + 3 : SPAN + 5] = jnp.zeros((2, 3, 8, 128), BF)
        else:
            for p in (3, 4):
                arrived(p)

            @pl.when(g > 0)
            def _():
                for p in range(3):
                    arrived(p)

            @pl.when(g == 0)
            def _():
                cube[0:3] = jnp.zeros((3, 3, 8, 128), BF)

    all_layers(
        (groups, strips, g, t), cube, arrive, b1, b2, bias3, x1, x2, l2, x3_upper, x3, w1, w2, w3, upper
    )

    @pl.loop(1, strips)
    def _(k):
        near(k).wait_send()

    @pl.when(beyond)
    def _():
        @pl.loop(0, strips)
        def _(k):
            far(k).wait_send()


X3_SHAPE = (5 * K3, 128)
HALF_SHAPE = (16, SPAN // 4, SPAN // 2, 64)
WEIGHT_SCRATCH = [
    pltpu.VMEM((128, 128), F32),
    pltpu.VMEM((8, 1408), F32),
    pltpu.VMEM((256, 128), F32),
    pltpu.VMEM((160, 256), BF),
    pltpu.VMEM((144, 1408), BF),
]
LAYER_SCRATCH = [
    pltpu.VMEM((PLANES * K1, 128), BF),
    pltpu.VMEM((F1 * K2, 128), BF),
    pltpu.VMEM((F2, 8 * Y2, 128), F32),
    pltpu.VMEM(X3_SHAPE, BF),
]


def first_layers(sky_cube, k1, k2, k3, b1, b2, b3):
    height = sky_cube.shape[1]
    strips = height // SPAN
    operands = [
        pltpu.with_memory_space_constraint(x, pltpu.HBM)
        for x in (sky_cube, k1, k2, k3, b1, b2, b3)
    ]
    vmem = pl.BlockSpec(memory_space=pltpu.VMEM)
    return pl.pallas_call(
        spread_kernel,
        out_shape=[
            jax.ShapeDtypeStruct(X3_SHAPE, BF),
            jax.ShapeDtypeStruct((128, 1280), BF),
            jax.ShapeDtypeStruct((128, 128), F32),
            jax.ShapeDtypeStruct(HALF_SHAPE, BF),
        ],
        in_specs=[pl.BlockSpec(memory_space=pltpu.HBM)] * len(operands),
        out_specs=[vmem] * 4,
        scratch_shapes=[
            pltpu.VMEM((height, 128), F32),
            pltpu.VMEM((height + 16, 128), F32),
            pltpu.VMEM(((height + 16) // 8, 8, 128), BF),
            pltpu.VMEM((PLANES, 3, 8, 128), BF),
            pltpu.VMEM(k1.shape, BF),
            pltpu.VMEM(k2.shape, BF),
            pltpu.VMEM(k3.shape, BF),
            pltpu.SMEM(b1.shape, F32),
            pltpu.SMEM(b2.shape, F32),
            pltpu.SMEM(b3.shape, F32),
            *WEIGHT_SCRATCH,
            *LAYER_SCRATCH,
            pltpu.SemaphoreType.DMA((len(operands),)),
            pltpu.SemaphoreType.DMA((2 * strips,)),
            pltpu.SemaphoreType.DMA((PLANES,)),
        ],
        compiler_params=pltpu.CompilerParams(
            collective_id=0, has_side_effects=True, vmem_limit_bytes=24 << 20
        ),
        name="first_layers",
    )(*operands)


def third_kernel(x3, w3, bias3, upper, out, lower, sem):
    quarter = SPAN // 4
    done = pltpu.make_async_copy(upper, out.at[:, quarter : 2 * quarter], sem.at[0])
    done.start()
    third_matmul(x3, 0, w3, bias3, lower)
    rest = pltpu.make_async_copy(lower, out.at[:, 0:quarter], sem.at[1])
    rest.start()
    done.wait()
    rest.wait()


def third_layer(x3, w3, bias3, upper):
    vmem = pl.BlockSpec(memory_space=pltpu.VMEM)
    half = SPAN // 2
    return pl.pallas_call(
        third_kernel,
        out_shape=jax.ShapeDtypeStruct((16, half, half, 64), BF),
        in_specs=[vmem] * 4,
        out_specs=pl.BlockSpec(memory_space=pl.ANY),
        scratch_shapes=[pltpu.VMEM(HALF_SHAPE, BF), pltpu.SemaphoreType.DMA((2,))],
        compiler_params=pltpu.CompilerParams(vmem_limit_bytes=8 << 20),
        name="third_layer",
    )(x3, w3, bias3, upper)


def body(sky_cube, kernel_one, bias_one, kernel_two, bias_two, kernel_three, bias_three):
    return third_layer(
        *first_layers(
            sky_cube,
            kernel_one.transpose(1, 2, 3, 4, 0),
            kernel_two.transpose(2, 3, 4, 0, 1),
            kernel_three.transpose(2, 3, 4, 1, 0),
            bias_one,
            bias_two,
            bias_three,
        )
    )


def solution(mesh):
    return jax.shard_map(
        body,
        mesh=mesh,
        in_specs=(P(("freq", "tile"), None, None), P(), P(), P(), P(), P(), P()),
        out_specs=P(None, "freq", "tile", None),
        check_vma=False,
    )
```

```python
import jax
import jax.numpy as jnp
from jax import lax
from jax.experimental import pallas as pl
from jax.experimental.pallas import tpu as pltpu
from jax.sharding import PartitionSpec as P

MESH = pl.DeviceIdType.MESH
BF = jnp.bfloat16
F32 = jnp.float32

SPAN = 16
PLANES = SPAN + 5
ROWS = 24
F1, Y1 = SPAN + 3, SPAN + 3
F2, Y2 = SPAN + 1, SPAN + 1
K1 = 80
K2 = 464
K3 = 416


def iota(shape, dim):
    return lax.broadcasted_iota(jnp.int32, shape, dim)


def leaky(values):
    return jnp.maximum(values, 0.1 * values)


def beside(values):
    lane = iota(values.shape, 1)
    swapped = pltpu.roll(values, 64, 1)
    before = jnp.where(lane < 64, pltpu.roll(values, 65, 1), swapped)
    after = jnp.where(lane < 64, swapped, pltpu.roll(values, 63, 1))
    return (
        jnp.where(lane == 0, 0.0, before),
        values,
        jnp.where(lane == 127, 0.0, after),
    )


def column_of(bias, rows, count):
    row = iota((count, 128), 0)
    block = jnp.zeros((count, 128), F32)
    for o in range(count):
        block = jnp.where(row == o, bias[o], block)
    return jnp.concatenate([block] * (rows // count), axis=0)


def taps():
    return [(a, b, c) for a in range(3) for b in range(3) for c in range(3)]


def one_if(inside):
    return jnp.where(inside, 1.0, 0.0).astype(F32)


def banded_weights(k1, k2, k3, stack1, base2, stack3, w1, w2, w3):
    stack1[...] = jnp.zeros(stack1.shape, F32)
    for a in range(3):
        for b in range(3):
            at = 8 * (3 * a + b)
            stack1[at : at + 3, 0:8] = k1[0, a, b].astype(F32)
    source = iota((128, 256), 0)
    tap, c = source >> 3, source & 7
    a = (tap * 21846) >> 16
    target = jnp.where((tap < 9) & (c < 3), a * K1 + c * ROWS + 1 + tap - 3 * a, -1)
    base = jnp.dot(
        stack1[...].T[0:8].astype(BF),
        (iota((128, 256), 1) == target).astype(F32).astype(BF),
        preferred_element_type=F32,
    )
    for y in range(0, Y1, 2):
        both = [pltpu.roll(base, s, 1) if s else base for s in (y, y + 1)]
        w1[8 * y : 8 * y + 16, :] = jnp.concatenate(both, axis=0).astype(BF)

    base2[...] = jnp.zeros(base2.shape, F32)
    for a, b, c in taps():
        at = a * K2 + c * (8 * Y1) + 8 * b
        base2[:, at : at + 8] = k2[a, b, c].astype(F32)
    base = base2[...]
    for y in range(0, Y2, 2):
        both = [pltpu.roll(base, 8 * s, 1) if s else base for s in (y, min(y + 1, Y2 - 1))]
        w2[8 * y : 8 * y + 16, :] = jnp.concatenate(both, axis=0).astype(BF)

    stack3[...] = jnp.zeros(stack3.shape, F32)
    for n, (a, b, c) in enumerate(taps()):
        stack3[8 * n : 8 * n + 8, 0:16] = k3[a, b, c].astype(F32)
    source = iota((256, 1280), 0)
    tap, i = source >> 3, source & 7
    a = (tap * 7282) >> 16
    rest = tap - 9 * a
    b = (rest * 21846) >> 16
    target = jnp.where(tap < 27, a * K3 + (rest - 3 * b) * (8 * Y2) + 8 * b + i, -1)
    base = jnp.dot(
        stack3[...].T[0:16].astype(BF),
        (iota((256, 1280), 1) == target).astype(F32).astype(BF),
        preferred_element_type=F32,
    )
    rows = [pltpu.roll(base, 16 * y, 1) if y else base for y in range(SPAN // 2)]
    by_row = jnp.concatenate(rows, axis=0).astype(BF)
    r = iota((128, 128), 0)
    swap = iota((128, 128), 1) == (r & 7) * 16 + (r >> 3)
    w3[...] = jnp.dot(
        swap.astype(F32).astype(BF), by_row, preferred_element_type=F32
    ).astype(BF)


def third_matmul(x3, first, w3, bias3, out):
    data = jnp.concatenate(
        [x3[h * K3 : (h + 3) * K3, :] for h in (first, first + 2)], axis=1
    )
    sums = jnp.dot(w3[:, 0 : 3 * K3], data, preferred_element_type=F32)
    for n in range(2):
        values = leaky(sums[:, 128 * n : 128 * (n + 1)] + bias3[...])
        out[:, n, :, :] = values[:, 0:64].reshape(16, 8, 64).astype(BF)
        swapped = pltpu.roll(values, 64, 1)
        out[:, n + 2, :, :] = swapped[:, 0:64].reshape(16, 8, 64).astype(BF)


def all_layers(place, cube, arrive, b1, b2, bias3, x1, x2, l2, x3_upper, x3, w1, w2, w3, upper):
    groups, strips, g, t = place
    first_g, last_g = one_if(g > 0), one_if(g < groups - 1)
    first_t, last_t = one_if(t > 0), one_if(t < strips - 1)

    def operand(f):
        pieces = beside(cube[f].reshape(ROWS, 128).astype(F32))
        block = jnp.concatenate([*pieces, jnp.zeros((K1 - 3 * ROWS, 128), F32)], axis=0)
        x1[f * K1 : (f + 1) * K1, :] = block.astype(BF)

    bias1 = column_of(b1, 8 * Y1, 8)
    row = iota((8 * Y1, 128), 0)
    keep1 = jnp.where(row < 16, first_t, jnp.where(row >= 8 * (Y1 - 1), last_t, 1.0))

    def layer_one(*fs):
        data = jnp.concatenate([x1[h * K1 : (h + 3) * K1, :] for h in fs], axis=1)
        sums = jnp.dot(w1[0 : 8 * Y1, 0 : 3 * K1], data, preferred_element_type=F32)
        for n, h in enumerate(fs):
            values = leaky(sums[:, 128 * n : 128 * (n + 1)] + bias1) * keep1
            if h < 2:
                values = values * first_g
            if h == F1 - 1:
                values = values * last_g
            block = jnp.concatenate(
                [*beside(values), jnp.zeros((K2 - 24 * Y1, 128), F32)], axis=0
            )
            x2[h * K2 : (h + 1) * K2, :] = block.astype(BF)

    bias2 = column_of(b2, 8 * Y2, 8)
    keep2 = jnp.where(iota((8 * Y2, 128), 0) < 8, first_t, 1.0)

    def layer_two(*fs):
        data = jnp.concatenate([x2[h * K2 : (h + 3) * K2, :] for h in fs], axis=1)
        sums = jnp.dot(w2[0 : 8 * Y2, 0 : 3 * K2], data, preferred_element_type=F32)
        for n, h in enumerate(fs):
            values = leaky(sums[:, 128 * n : 128 * (n + 1)] + bias2) * keep2
            if h == 0:
                values = values * first_g
            l2[h] = values

    lane = iota((8 * Y2, 128), 1)

    def joined(to, at, f):
        lower, upper = l2[f], l2[f + 4]
        before = jnp.where(lane < 64, pltpu.roll(lower, 65, 1), pltpu.roll(upper, 1, 1))
        block = jnp.concatenate(
            [
                jnp.where((lane & 63) == 0, 0.0, before),
                jnp.where(lane < 64, lower, pltpu.roll(upper, 64, 1)),
                jnp.where(lane < 64, pltpu.roll(lower, 64, 1), upper),
                jnp.zeros((K3 - 24 * Y2, 128), F32),
            ],
            axis=0,
        )
        to[at * K3 : (at + 1) * K3, :] = block.astype(BF)

    arrive("inner")
    for f in range(5, SPAN):
        operand(f)
    for f in (5, 7, 9, 11):
        layer_one(f, f + 1)
    for f in (5, 7, 9):
        layer_two(f, f + 1)
    arrive("upper")
    for f in range(SPAN, PLANES):
        operand(f)
    for f in (13, 15, 17):
        layer_one(f, f + 1)
    for f in (11, 13, 15):
        layer_two(f, f + 1)
    for n in range(5):
        joined(x3_upper, n, 8 + n)
    third_matmul(x3_upper, 0, w3, bias3, upper)
    arrive("lower")
    for f in range(5):
        operand(f)
    layer_one(0, 1)
    layer_one(2, 3)
    layer_one(4)
    layer_two(0, 1)
    layer_two(2, 3)
    layer_two(4)
    for n in range(5):
        joined(x3, n, n)


def spread_kernel(
    sky, k1_in, k2_in, k3_in, b1_in, b2_in, b3_in,
    x3, w3, bias3, upper,
    raw, moved, slab, cube, k1, k2, k3, b1, b2, b3, stack1, base2, stack3, w1, w2, x1, x2, l2, x3_upper,
    in_sem, send_sem, recv_sem,
):
    groups, strips = lax.axis_size("freq"), lax.axis_size("tile")
    g, t = lax.axis_index("freq"), lax.axis_index("tile")
    height = raw.shape[0]

    barrier = pltpu.get_barrier_semaphore()

    def greet(group, strip):
        pl.semaphore_signal(barrier, inc=1, device_id=(group, strip), device_id_type=MESH)

    @pl.when(g < groups - 1)
    def _():
        for strip in (0, 1):
            greet(g + 1, strip)

    @pl.when(g > 0)
    def _():
        for strip in (strips - 3, strips - 2, strips - 1):
            greet(g - 1, strip)

    @pl.loop(1, strips)
    def _(k):
        greet(g, lax.rem(t + k, strips))

    pairs = [(sky.at[0], raw), (k1_in, k1), (k2_in, k2), (k3_in, k3), (b1_in, b1), (b2_in, b2), (b3_in, b3)]
    loads = [pltpu.make_async_copy(a, b, in_sem.at[n]) for n, (a, b) in enumerate(pairs)]
    for load in loads:
        load.start()

    lane = iota((128, 128), 1)
    column = jnp.where(lane < 64, 2 * lane, 2 * lane - 127)
    order = (iota((128, 128), 0) == column).astype(F32).astype(BF)
    moved[0:8, :] = jnp.zeros((8, 128), F32)
    moved[height : height + 16, :] = jnp.zeros((16, 128), F32)
    loads[0].wait()
    values = jnp.dot(raw[...].astype(BF), order, preferred_element_type=F32)
    moved[4 : height + 4, :] = values
    slab[...] = moved[...].reshape(slab.shape).astype(BF)

    high = t >= strips - 3
    low = t < 2
    beyond = jnp.logical_or(jnp.logical_and(low, g > 0), jnp.logical_and(high, g < groups - 1))
    other = jnp.where(low, jnp.maximum(g - 1, 0), jnp.minimum(g + 1, groups - 1))
    plane = 3 + t
    far_plane = jnp.where(low, SPAN + 3 + t, jnp.maximum(t - (strips - 3), 0))

    def near(k):
        strip = lax.rem(t + k, strips)
        return pltpu.make_async_remote_copy(
            src_ref=slab.at[pl.ds(2 * strip, 3)],
            dst_ref=cube.at[plane],
            send_sem=send_sem.at[k],
            recv_sem=recv_sem.at[plane],
            device_id=(g, strip),
            device_id_type=MESH,
        )

    def far(k):
        pair = k // 2
        far_z = jnp.logical_or(pair == 1, pair >= 5)
        y = pair - jnp.where(pair >= 5, 4, jnp.where(pair >= 1, 1, 0))
        strip = jnp.where(far_z, strips // 2, 0) + 2 * y + lax.rem(k, 2)
        return pltpu.make_async_remote_copy(
            src_ref=slab.at[pl.ds(2 * strip, 3)],
            dst_ref=cube.at[far_plane],
            send_sem=send_sem.at[strips + k],
            recv_sem=recv_sem.at[far_plane],
            device_id=(other, strip),
            device_id_type=MESH,
        )

    late = jnp.logical_and(jnp.logical_and(low, g > 0), lax.rem(g, 4) == 0)
    expand_at = jnp.where(late, 0, 1)

    @pl.loop(0, 2)
    def _(turn):
        @pl.when(turn == expand_at)
        def _():
            for load in loads[1:]:
                load.wait()
            banded_weights(k1, k2, k3, stack1, base2, stack3, w1, w2, w3)
            for o in range(16):
                bias3[8 * o : 8 * o + 8, :] = jnp.full((8, 128), b3[o], F32)

        @pl.when(jnp.logical_and(turn == 0, beyond))
        def _():
            pl.semaphore_wait(barrier, 2 * strips - 1)

            @pl.when(jnp.logical_not(late))
            def _():
                @pl.loop(0, strips)
                def _(k):
                    far(k).start()

        @pl.when(jnp.logical_and(turn == 0, jnp.logical_not(beyond)))
        def _():
            pl.semaphore_wait(barrier, strips - 1)

        @pl.when(turn == 0)
        def _():
            @pl.loop(1, strips)
            def _(k):
                near(k).start()

            own = slab.at[pl.ds(2 * t, 3)]
            pltpu.make_async_copy(own, cube.at[plane], recv_sem.at[plane]).start()

            @pl.when(late)
            def _():
                @pl.loop(0, strips)
                def _(k):
                    far(k).start()

    def arrived(p):
        pltpu.make_async_copy(cube.at[p], cube.at[p], recv_sem.at[p]).wait()

    def arrive(side):
        if side == "inner":
            @pl.loop(5, SPAN)
            def _(p):
                arrived(p)
        elif side == "upper":
            for p in (SPAN, SPAN + 1, SPAN + 2):
                arrived(p)

            @pl.when(g < groups - 1)
            def _():
                for p in (SPAN + 3, SPAN + 4):
                    arrived(p)

            @pl.when(g == groups - 1)
            def _():
                cube[SPAN + 3 : SPAN + 5] = jnp.zeros((2, 3, 8, 128), BF)
        else:
            for p in (3, 4):
                arrived(p)

            @pl.when(g > 0)
            def _():
                for p in range(3):
                    arrived(p)

            @pl.when(g == 0)
            def _():
                cube[0:3] = jnp.zeros((3, 3, 8, 128), BF)

    all_layers(
        (groups, strips, g, t), cube, arrive, b1, b2, bias3, x1, x2, l2, x3_upper, x3, w1, w2, w3, upper
    )

    @pl.loop(1, strips)
    def _(k):
        near(k).wait_send()

    @pl.when(beyond)
    def _():
        @pl.loop(0, strips)
        def _(k):
            far(k).wait_send()


X3_SHAPE = (5 * K3, 128)
HALF_SHAPE = (16, SPAN // 4, SPAN // 2, 64)
WEIGHT_SCRATCH = [
    pltpu.VMEM((128, 128), F32),
    pltpu.VMEM((8, 1408), F32),
    pltpu.VMEM((256, 128), F32),
    pltpu.VMEM((160, 256), BF),
    pltpu.VMEM((144, 1408), BF),
]
LAYER_SCRATCH = [
    pltpu.VMEM((PLANES * K1, 128), BF),
    pltpu.VMEM((F1 * K2, 128), BF),
    pltpu.VMEM((F2, 8 * Y2, 128), F32),
    pltpu.VMEM(X3_SHAPE, BF),
]


def first_layers(sky_cube, k1, k2, k3, b1, b2, b3):
    height = sky_cube.shape[1]
    strips = height // SPAN
    operands = [
        pltpu.with_memory_space_constraint(x, pltpu.HBM)
        for x in (sky_cube, k1, k2, k3, b1, b2, b3)
    ]
    vmem = pl.BlockSpec(memory_space=pltpu.VMEM)
    return pl.pallas_call(
        spread_kernel,
        out_shape=[
            jax.ShapeDtypeStruct(X3_SHAPE, BF),
            jax.ShapeDtypeStruct((128, 1280), BF),
            jax.ShapeDtypeStruct((128, 128), F32),
            jax.ShapeDtypeStruct(HALF_SHAPE, BF),
        ],
        in_specs=[pl.BlockSpec(memory_space=pltpu.HBM)] * len(operands),
        out_specs=[vmem] * 4,
        scratch_shapes=[
            pltpu.VMEM((height, 128), F32),
            pltpu.VMEM((height + 16, 128), F32),
            pltpu.VMEM(((height + 16) // 8, 8, 128), BF),
            pltpu.VMEM((PLANES, 3, 8, 128), BF),
            pltpu.VMEM(k1.shape, BF),
            pltpu.VMEM(k2.shape, BF),
            pltpu.VMEM(k3.shape, BF),
            pltpu.SMEM(b1.shape, F32),
            pltpu.SMEM(b2.shape, F32),
            pltpu.SMEM(b3.shape, F32),
            *WEIGHT_SCRATCH,
            *LAYER_SCRATCH,
            pltpu.SemaphoreType.DMA((len(operands),)),
            pltpu.SemaphoreType.DMA((2 * strips,)),
            pltpu.SemaphoreType.DMA((PLANES,)),
        ],
        compiler_params=pltpu.CompilerParams(
            collective_id=0, has_side_effects=True, vmem_limit_bytes=24 << 20
        ),
        name="first_layers",
    )(*operands)


def third_kernel(x3, w3, bias3, upper, out, lower, sem):
    quarter = SPAN // 4
    done = pltpu.make_async_copy(upper, out.at[:, quarter : 2 * quarter], sem.at[0])
    done.start()
    third_matmul(x3, 0, w3, bias3, lower)
    rest = pltpu.make_async_copy(lower, out.at[:, 0:quarter], sem.at[1])
    rest.start()
    done.wait()
    rest.wait()


def third_layer(x3, w3, bias3, upper):
    vmem = pl.BlockSpec(memory_space=pltpu.VMEM)
    half = SPAN // 2
    return pl.pallas_call(
        third_kernel,
        out_shape=jax.ShapeDtypeStruct((16, half, half, 64), BF),
        in_specs=[vmem] * 4,
        out_specs=pl.BlockSpec(memory_space=pl.ANY),
        scratch_shapes=[pltpu.VMEM(HALF_SHAPE, BF), pltpu.SemaphoreType.DMA((2,))],
        compiler_params=pltpu.CompilerParams(vmem_limit_bytes=8 << 20),
        name="third_layer",
    )(x3, w3, bias3, upper)


def body(sky_cube, kernel_one, bias_one, kernel_two, bias_two, kernel_three, bias_three):
    return third_layer(
        *first_layers(
            sky_cube,
            kernel_one.transpose(1, 2, 3, 4, 0),
            kernel_two.transpose(2, 3, 4, 0, 1),
            kernel_three.transpose(2, 3, 4, 1, 0),
            bias_one,
            bias_two,
            bias_three,
        )
    )


def solution(mesh):
    return jax.shard_map(
        body,
        mesh=mesh,
        in_specs=(P(("freq", "tile"), None, None), P(), P(), P(), P(), P(), P()),
        out_specs=P(None, "freq", "tile", None),
        check_vma=False,
    )
```
